32 devices in a mesh: row: 8 (over y, x, core), col: 4 (over z).
Axes of the slice: x: 2, y: 2, z: 4, core: 2. Of those that a mesh axis runs over, the one named last changes fastest.
Arguments:
- potential: float32 [3, 128, 64, 256], P(None, 'row', 'col'), may hold values from -6 to 6
- source: float32 [3, 128, 64, 256], P(None, 'row', 'col'), may hold values from -3.2 to 3.2
- labels: int32 [128, 64, 256], P('row', 'col'), may hold values from 0 to 7
- coil_mask: int32 [128, 64, 256], P('row', 'col'), may hold values 0 or 1
- floor_table: float32 [8], replicated, may hold values from 0.3 to 3
- rise_table: float32 [8], replicated, may hold values from 0.5 to 5
Outputs:
- field: float32 [3, 128, 64, 256], P(None, 'row', 'col')
- reluct: float32 [128, 64, 256], P('row', 'col')
- coarse_target: float32 [3, 16, 8, 32], P(None, None, 'col')
The draws below stay inside these ranges and needn't reach their ends.
Inputs may be any that keep to these rules, and one draw needn't show every extreme that they name: `labels`: each cell's material.
All inputs are finite; a program needn't handle non-finite values. No bound on the sum of `coil_mask` on one device may be relied on, other than what follows from the above.
Results may differ from the reference program's by a relative error of at most 0.00019.
Values sent between devices are 32-bit elements; how exact they have to be, the bound alone decides.
No kernel may reach another device: no remote copies, remote signals or barrier semaphores. Data moves between devices by JAX's collectives and lax.ppermute only.
A program may use at most 128 MiB of HBM per device.

```python
import math
import jax
import jax.numpy as jnp
from jax import lax

CY = 16
ITERS = 3
SWEEPS = 2
COARSE_SWEEPS = 16
COARSEN = 8
LABELS = 8
NX = 128
NY = 64
NZ = 256
N_COL = 4


def draw_source(key, part):
    sign_key = jax.random.fold_in(key, 11)
    scale_key = jax.random.fold_in(key, 23)
    run_x = 64
    run_y = 8
    run_z = 16
    count_x = NX // run_x + 1
    count_y = NY // run_y + 1
    count_z = NZ // run_z + 1
    signs = (2 * jax.random.randint(sign_key, (3, count_x, count_y, count_z), 0, 2) - 1).astype(jnp.float32)
    index_x = jnp.arange(NX, dtype=jnp.int32) // run_x
    index_y = jnp.arange(NY, dtype=jnp.int32) // run_y
    index_z = jnp.arange(NZ, dtype=jnp.int32) // run_z
    expanded = jnp.take(signs, index_x, axis=1)
    expanded = jnp.take(expanded, index_y, axis=2)
    expanded = jnp.take(expanded, index_z, axis=3)
    shape = (3, NX, NY, NZ)
    amplitude = jnp.exp(jax.random.uniform(scale_key, shape, jnp.float32, math.log(0.4), math.log(1.6)))
    return (2.0 * expanded * amplitude).astype(jnp.float32)


def set_ends(array, key, least, top_value):
    extent = array.shape
    spot = [jax.random.randint(jax.random.fold_in(key, axis), (), 0, extent[axis]) for axis in range(len(extent))]
    array = array.at[tuple(spot)].set(least)
    longest = extent.index(max(extent))
    spot[longest] = (spot[longest] + 1) % extent[longest]
    return array.at[tuple(spot)].set(top_value)


def block_levels(rng, extent, shards, smallest, top_value):
    factor_of, own = 1.0, jax.random.fold_in(rng, 6)
    for dim, shards_of in shards:
        steps = jnp.exp(jax.random.uniform(jax.random.fold_in(own, dim), (shards_of,), jnp.float32, smallest / len(shards), top_value / len(shards)))
        factor_of = factor_of * jnp.repeat(steps, extent[dim] // shards_of).reshape([-1 if axis == dim else 1 for axis in range(len(extent))])
    return factor_of


def gaussian(key, dims, width, bound, split=(), kind=jnp.bfloat16):
    drawn = width * jax.random.normal(key, dims, jnp.float32)
    if split:
        drawn = drawn * block_levels(key, dims, split, -0.22, 0.18)
    return jnp.clip(drawn, -bound, bound).astype(kind)


def setup_inputs(seed: int = 0) -> dict:
    splits = jax.random.split(jax.random.key(seed), 7)
    return {
        "potential": gaussian(splits[0], (3, NX, NY, NZ), 1.0, 6.0, ((1, 8), (2, 4)), jnp.float32),
        "source": draw_source(jax.random.fold_in(splits[6], 71), 0),
        "labels": set_ends(jax.random.randint(splits[2], (NX, NY, NZ), 0, LABELS), jax.random.fold_in(splits[2], 1), 0, LABELS - 1).astype(jnp.int32),
        "coil_mask": set_ends((jax.random.randint(splits[3], (NX, NY, NZ), 0, 2) < 1).astype(jnp.int32), jax.random.fold_in(splits[3], 1), 0, 1),
        "floor_table": jnp.clip(jnp.exp(jax.random.uniform(splits[4], (LABELS,), jnp.float32, math.log(0.3), math.log(3.0))), 0.3, 3.0),
        "rise_table": jnp.clip(jnp.exp(jax.random.uniform(splits[5], (LABELS,), jnp.float32, math.log(0.5), math.log(5.0))), 0.5, 5.0),
    }


relax = 0.8


def pad_depth(values):
    widths = [(0, 0)] * (values.ndim - 1) + [(1, 1)]
    return jnp.pad(values, widths)


def pad_plane(values, reach):
    widths = [(0, 0)] * (values.ndim - 3) + [(reach, reach), (reach, reach), (0, 0)]
    return jnp.pad(values, widths)


def field_square(field):
    def along_x(comp):
        return 0.5 * (field[comp, 2:, 1:-1] - field[comp, :-2, 1:-1])

    def along_y(comp):
        return 0.5 * (field[comp, 1:-1, 2:] - field[comp, 1:-1, :-2])

    def along_z(comp):
        padded = pad_depth(field[comp, 1:-1, 1:-1])
        return 0.5 * (padded[..., 2:] - padded[..., :-2])

    first = along_y(2) - along_z(1)
    second = along_z(0) - along_x(2)
    third = along_x(1) - along_y(0)
    return first * first + second * second + third * third


def reluctivity(square, labels, floor_table, rise_table):
    floor_cell = jnp.zeros(labels.shape, jnp.float32)
    rise_cell = jnp.zeros(labels.shape, jnp.float32)
    for label in range(floor_table.shape[0]):
        chosen = labels == label
        floor_cell = jnp.where(chosen, floor_table[label], floor_cell)
        rise_cell = jnp.where(chosen, rise_table[label], rise_cell)
    return floor_cell + rise_cell * (square / (1.0 + square))


def operator(field, reluct):
    centre = reluct[1:-1, 1:-1]
    depth_reluct = pad_depth(centre)
    coeffs = [0.5 * (centre + reluct[2:, 1:-1]), 0.5 * (centre + reluct[:-2, 1:-1]),
              0.5 * (centre + reluct[1:-1, 2:]), 0.5 * (centre + reluct[1:-1, :-2]),
              0.5 * (centre + depth_reluct[..., 2:]), 0.5 * (centre + depth_reluct[..., :-2])]
    centre_cells = field[:, 1:-1, 1:-1]
    depth_field = pad_depth(centre_cells)
    neighbours = [field[:, 2:, 1:-1], field[:, :-2, 1:-1], field[:, 1:-1, 2:], field[:, 1:-1, :-2],
                  depth_field[..., 2:], depth_field[..., :-2]]
    diagonal = coeffs[0]
    offdiag = coeffs[0] * neighbours[0]
    for number in range(1, 6):
        diagonal = diagonal + coeffs[number]
        offdiag = offdiag + coeffs[number] * neighbours[number]
    applied = diagonal * centre_cells - offdiag
    return diagonal, applied, centre_cells


def relax_step(field, reluct, driving):
    diagonal, applied, centre = operator(field, reluct)
    return centre + relax * (driving - applied) / diagonal


def restrict(resid, reluct):
    block = COARSEN
    comps, size_x, size_y, size_z = resid.shape
    coarse_resid = resid.reshape(comps, size_x // block, block, size_y // block, block, size_z // block, block).sum(axis=(2, 4, 6))
    coarse_reluct = reluct.reshape(size_x // block, block, size_y // block, block, size_z // block, block).mean(axis=(1, 3, 5))
    return coarse_resid, coarse_reluct


def coarse_solve(coarse_resid, coarse_reluct):
    face_area = float(COARSEN * COARSEN)
    padded_reluct = pad_plane(coarse_reluct, 1)
    target = coarse_resid / face_area

    def sweep_once(count, correction):
        diagonal, applied, centre = operator(pad_plane(correction, 1), padded_reluct)
        return centre + relax * (target - applied) / diagonal

    correction = lax.fori_loop(0, COARSE_SWEEPS, sweep_once, jnp.zeros_like(coarse_resid))
    diagonal, applied, centre = operator(pad_plane(correction, 1), padded_reluct)
    leftover = jnp.sum(target - applied, axis=(1, 2, 3))
    total_diag = jnp.sum(diagonal)
    return correction + (leftover / total_diag)[:, None, None, None]


def spread(correction):
    block = COARSEN
    comps, size_x, size_y, size_z = correction.shape
    wide = jnp.broadcast_to(correction[:, :, None, :, None, :, None], (comps, size_x, block, size_y, block, size_z, block))
    return wide.reshape(comps, size_x * block, size_y * block, size_z * block)


def reference(potential, source, labels, coil_mask, floor_table, rise_table):
    driving = source * coil_mask.astype(jnp.float32)
    field = potential
    reluct = jnp.zeros(labels.shape, jnp.float32)
    coarse_target = jnp.zeros((3, NX // COARSEN, NY // COARSEN, NZ // COARSEN), jnp.float32)
    for iteration in range(ITERS):
        reluct = reluctivity(field_square(pad_plane(field, 1)), labels, floor_table, rise_table)
        reluct_pad = pad_plane(reluct, 1)
        for sweep in range(SWEEPS):
            field = relax_step(pad_plane(field, 1), reluct_pad, driving)
        diagonal, applied, centre = operator(pad_plane(field, 1), reluct_pad)
        resid = driving - applied
        coarse_resid, coarse_reluct = restrict(resid, reluct)
        coarse_target = coarse_resid / float(COARSEN * COARSEN)
        comps, coarse_x, coarse_y, coarse_z = coarse_resid.shape
        stripe_y = CY // COARSEN
        split_resid = coarse_resid.reshape(comps, coarse_x, N_COL, stripe_y, coarse_z).transpose(2, 0, 1, 3, 4)
        split_reluct = coarse_reluct.reshape(coarse_x, N_COL, stripe_y, coarse_z).transpose(1, 0, 2, 3)
        corrections = jax.vmap(coarse_solve)(split_resid, split_reluct)
        correction = corrections.transpose(1, 2, 0, 3, 4).reshape(comps, coarse_x, coarse_y, coarse_z)
        field = field + spread(correction)
    return field, reluct, coarse_target
```

```python
import functools
import jax
import jax.numpy as jnp
from jax import lax
from jax.experimental import pallas as pl
from jax.experimental.pallas import tpu as pltpu
from jax.sharding import PartitionSpec as P

ITERS = 3
SWEEPS = 2
COARSE_SWEEPS = 16
COARSEN = 8
RELAX = 0.8

HALO = 4
BLOCK = 16
EXT = BLOCK + 2 * HALO
LANES = 128
TOP = 8
CORE = TOP + HALO
ROWS = 40
HIGH = lax.Precision.HIGHEST
X_PAGES = 21
Y_PAGES = 124

VMEM = pl.BlockSpec(memory_space=pltpu.VMEM)
SMEM = pl.BlockSpec(memory_space=pltpu.SMEM)
PARAMS = pltpu.CompilerParams(vmem_limit_bytes=44 * 1024 * 1024)


def f32(*shape):
    return jax.ShapeDtypeStruct(shape, jnp.float32)


def place():
    return (
        lax.axis_index("row"), lax.axis_size("row"), lax.axis_index("col"), lax.axis_size("col"),
    )


def pack_x_kernel(pot_lo, pot_hi, src_lo, src_hi, mask_lo, mask_hi, lab_lo, lab_hi, out_lo, out_hi):
    for pot, src, mask, lab, out, drive, first in (
        (pot_lo, src_lo, mask_lo, lab_lo, out_lo, 0, 0), (pot_hi, src_hi, mask_hi, lab_hi, out_hi, 2, 1),
    ):
        for comp in range(3):
            out[comp * 4 : comp * 4 + 4] = pot[comp]
            for cell in range(2):
                out[12 + comp * 2 + cell] = (
                    2.0 * src[comp, drive + cell] * mask[drive + cell].astype(jnp.float32)
                )
        out[18:21] = lab[first : first + 3].astype(jnp.float32)


def pack_x(potential, source, labels, coil_mask):
    last = BLOCK // HALO - 1
    depth = potential.shape[-1]
    wide = [
        pl.BlockSpec((3, HALO, BLOCK, depth), functools.partial(lambda side, step: (0, side, 0, 0), side))
        for side in (0, last)
    ]
    thin = [
        pl.BlockSpec((HALO, BLOCK, depth), functools.partial(lambda side, step: (side, 0, 0), side))
        for side in (0, last)
    ]
    out = pl.BlockSpec((X_PAGES, BLOCK, depth), lambda step: (0, 0, 0))
    return pl.pallas_call(
        pack_x_kernel,
        grid=(1,),
        in_specs=wide + wide + thin + thin,
        out_specs=[out, out],
        out_shape=[f32(X_PAGES, BLOCK, depth)] * 2,
        compiler_params=PARAMS,
        name="pack_x",
    )(potential, potential, source, source, coil_mask, coil_mask, labels, labels)


def pack_y_kernel(
    pot_lo, pot_hi, src_lo, src_hi, mask_lo, mask_hi, lab_lo, lab_hi, low, high, out_lo, out_hi
):
    for pot, src, mask, lab, out, row, cell in (
        (pot_lo, src_lo, mask_lo, lab_lo, out_lo, 0, 0),
        (pot_hi, src_hi, mask_hi, lab_hi, out_hi, 4, BLOCK - HALO),
    ):
        wide = slice(cell, cell + 4)
        drive = 0 if cell == 0 else 2
        for comp in range(3):
            base = comp * EXT
            out[base : base + 4] = low[comp * 4 : comp * 4 + 4, wide]
            out[base + 4 : base + 20] = pot[comp, :, row : row + 4]
            out[base + 20 : base + 24] = high[comp * 4 : comp * 4 + 4, wide]
            base = 72 + comp * 10
            for x in range(20):
                if x < 2:
                    part = low[12 + comp * 2 + x, cell + drive : cell + drive + 2]
                elif x < 18:
                    rows = slice(row + drive, row + drive + 2)
                    part = 2.0 * src[comp, x - 2, rows] * mask[x - 2, rows].astype(jnp.float32)
                else:
                    part = high[12 + comp * 2 + x - 18, cell + drive : cell + drive + 2]
                out[base + x // 2, (x % 2) * 2 : (x % 2) * 2 + 2] = part
        out[102:105] = low[18:21, wide]
        out[105:121] = lab[:, row : row + 4].astype(jnp.float32)
        out[121:124] = high[18:21, wide]


def pack_y(potential, source, labels, coil_mask, low, high):
    depth = potential.shape[-1]
    wide = [
        pl.BlockSpec((3, BLOCK, 8, depth), functools.partial(lambda side, step: (0, 0, side, 0), side))
        for side in (0, BLOCK // 8 - 1)
    ]
    thin = [
        pl.BlockSpec((BLOCK, 8, depth), functools.partial(lambda side, step: (0, side, 0), side))
        for side in (0, BLOCK // 8 - 1)
    ]
    msg = pl.BlockSpec((X_PAGES, BLOCK, depth), lambda step: (0, 0, 0))
    out = pl.BlockSpec((Y_PAGES, HALO, depth), lambda step: (0, 0, 0))
    return pl.pallas_call(
        pack_y_kernel,
        grid=(1,),
        in_specs=wide + wide + thin + thin + [msg, msg],
        out_specs=[out, out],
        out_shape=[f32(Y_PAGES, HALO, depth)] * 2,
        compiler_params=PARAMS,
        name="pack_y",
    )(
        potential, potential, source, source, coil_mask, coil_mask, labels, labels, low, high
    )


def pack_edge_kernel(field, low, high, out_lo, out_hi):
    for out, cell in ((out_lo, 0), (out_hi, BLOCK - HALO)):
        wide = slice(cell, cell + 4)
        for comp in range(3):
            base = comp * EXT
            out[base : base + 4] = low[comp * 4 : comp * 4 + 4, wide]
            out[base + 4 : base + 20] = field[comp, :, wide]
            out[base + 20 : base + 24] = high[comp * 4 : comp * 4 + 4, wide]


def pack_edge(field, low, high):
    depth = field.shape[-1]
    return pl.pallas_call(
        pack_edge_kernel,
        in_specs=[VMEM] * 3,
        out_specs=[VMEM] * 2,
        out_shape=[f32(3 * EXT, HALO, depth)] * 2,
        compiler_params=PARAMS,
        name="pack_edge",
    )(field, low, high)


def coarse_solve(targets, relucts):
    shape = relucts[0].shape
    count = shape[0]
    lane = lax.broadcasted_iota(jnp.int32, shape, 1)
    row = lax.broadcasted_iota(jnp.int32, shape, 0)
    z = lane % 32
    first_y = (lane // 32) % 2 == 0
    first_x = lane // 64 == 0
    up_ok, down_ok = z < 31, z > 0
    far_ok = jnp.logical_not(
        jnp.logical_or(
            jnp.logical_and(first_x, row == 0),
            jnp.logical_and(jnp.logical_not(first_x), row == count - 1),
        )
    )

    def up(v):
        return pltpu.roll(v, LANES - 1, 1)

    def down(v):
        return pltpu.roll(v, 1, 1)

    def side(v):
        return jnp.where(first_y, pltpu.roll(v, LANES - 32, 1), pltpu.roll(v, 32, 1))

    def near(v):
        return pltpu.roll(v, 64, 1)

    def far(swapped):
        return jnp.where(first_x, pltpu.roll(swapped, 1, 0), pltpu.roll(swapped, count - 1, 0))

    sets = []
    for r in relucts:
        swapped = near(r)
        c_up = r + jnp.where(up_ok, up(r), 0.0)
        c_down = r + jnp.where(down_ok, down(r), 0.0)
        c_side = r + side(r)
        c_near = r + swapped
        c_far = r + jnp.where(far_ok, far(swapped), 0.0)
        diag = ((c_up + c_down) + (c_side + r)) + (c_near + c_far)
        c_up = jnp.where(up_ok, c_up, 0.0)
        c_down = jnp.where(down_ok, c_down, 0.0)
        c_far = jnp.where(far_ok, c_far, 0.0)
        sets.append((c_up, c_down, c_side, c_near, c_far, diag, RELAX / diag))

    def neighbours(coeffs, v):
        c_up, c_down, c_side, c_near, c_far = coeffs[:5]
        swapped = near(v)
        return (
            (c_up * up(v) + c_down * down(v)) + (c_side * side(v) + c_near * swapped)
        ) + c_far * far(swapped)

    doubled = [[2.0 * t for t in stripe] for stripe in targets]
    start = [
        [coeffs[6] * t for t in stripe] for coeffs, stripe in zip(sets, doubled)
    ]

    def sweep(step, values):
        return [
            [
                (1.0 - RELAX) * v + coeffs[6] * (t + neighbours(coeffs, v))
                for v, t in zip(stripe, stripe_t)
            ]
            for coeffs, stripe, stripe_t in zip(sets, values, doubled)
        ]

    values = lax.fori_loop(0, COARSE_SWEEPS - 1, sweep, start)
    out = []
    for coeffs, stripe, stripe_t in zip(sets, values, doubled):
        total = jnp.sum(jnp.sum(coeffs[5], axis=1, keepdims=True), axis=0, keepdims=True)
        done = []
        for v, t in zip(stripe, stripe_t):
            left = t - (coeffs[5] * v - neighbours(coeffs, v))
            left = jnp.sum(jnp.sum(left, axis=1, keepdims=True), axis=0, keepdims=True)
            done.append(v + left / total)
        out.append(done)
    return out


def pick_row(values, index):
    row = lax.broadcasted_iota(jnp.int32, values.shape, 0)
    return jnp.sum(jnp.where(row == index, values, 0.0), axis=0, keepdims=True)


def spread_matrix(group):
    lane = lax.broadcasted_iota(jnp.int32, (LANES, 2 * LANES), 0)
    cell = lax.broadcasted_iota(jnp.int32, (LANES, 2 * LANES), 1)
    return jnp.where(lane == group * 32 + cell // COARSEN, 1.0, 0.0)


def gather_matrix(group):
    cell = lax.broadcasted_iota(jnp.int32, (2 * LANES, LANES), 0)
    lane = lax.broadcasted_iota(jnp.int32, (2 * LANES, LANES), 1)
    return jnp.where(lane == group * 32 + cell // COARSEN, 1.0, 0.0)


def load_stripe(table, gathered, count, pick):
    for row in range(count):
        for comp in range(4):
            table[comp, row : row + 1, :] = pick(row)[comp : comp + 1, :]
    scale = 1.0 / float(COARSEN * COARSEN)
    return [table[comp] * scale for comp in range(3)], table[3]


def put_field(field, core, low, high, back, front, row, rows, col, cols):
    has_low, has_high = row > 0, row < rows - 1
    has_back, has_front = col > 0, col < cols - 1
    both = jnp.logical_and
    for comp in range(3):
        for half in range(2):
            z = slice(half * LANES, half * LANES + LANES)
            own = slice(CORE, CORE + BLOCK)
            field[comp, half, 4:20, own, :] = core[comp, :, :, z]
            pages = slice(comp * 4, comp * 4 + 4)
            field[comp, half, 0:4, own, :] = jnp.where(has_low, low[pages, :, z], 0.0)
            field[comp, half, 20:24, own, :] = jnp.where(has_high, high[pages, :, z], 0.0)
            base = comp * EXT
            for message, there, top in ((back, has_back, TOP), (front, has_front, CORE + BLOCK)):
                for first, last, inside in (
                    (0, 4, both(there, has_low)), (4, 20, there), (20, 24, both(there, has_high)),
                ):
                    field[comp, half, first:last, top : top + HALO, :] = jnp.where(
                        inside, message[base + first : base + last, :, z], 0.0
                    )


def put_material(
    drive, floor, rise, source, coil_mask, labels, low, high, back, front, floor_table, rise_table,
    row, rows, col, cols,
):
    has_low, has_high = row > 0, row < rows - 1
    has_back, has_front = col > 0, col < cols - 1
    both = jnp.logical_and
    for half in range(2):
        z = slice(half * LANES, half * LANES + LANES)
        own = slice(HALO, HALO + BLOCK)
        coil = 2.0 * coil_mask[:, :, z].astype(jnp.float32)
        for comp in range(3):
            drive[comp, half, 4:20, own, :] = source[comp, :, :, z] * coil
            pages = slice(12 + comp * 2, 14 + comp * 2)
            drive[comp, half, 2:4, own, :] = low[pages, :, z]
            drive[comp, half, 20:22, own, :] = high[pages, :, z]
            for x in range(20):
                page, part = 72 + comp * 10 + x // 2, (x % 2) * 2
                drive[comp, half, 2 + x, 2:4, :] = back[page, part : part + 2, z]
                drive[comp, half, 2 + x, 20:22, :] = front[page, part : part + 2, z]
        floor[half, 4:20, own, :] = labels[:, :, z].astype(jnp.float32)
        floor[half, 1:4, own, :] = jnp.where(has_low, low[18:21, :, z], -1.0)
        floor[half, 20:23, own, :] = jnp.where(has_high, high[18:21, :, z], -1.0)
        for message, there, top in ((back, has_back, 0), (front, has_front, HALO + BLOCK)):
            for first, last, inside in (
                (1, 4, both(there, has_low)), (4, 20, there), (20, 23, both(there, has_high)),
            ):
                floor[half, first:last, top : top + HALO, :] = jnp.where(
                    inside, message[101 + first : 101 + last, :, z], -1.0
                )

    def look_up(x, carry):
        for half in range(2):
            label = floor[half, x]
            floor_cell = jnp.zeros_like(label)
            rise_cell = jnp.zeros_like(label)
            for number in range(floor_table.shape[0]):
                chosen = label == float(number)
                floor_cell = jnp.where(chosen, floor_table[number], floor_cell)
                rise_cell = jnp.where(chosen, rise_table[number], rise_cell)
            floor[half, x] = floor_cell
            rise[half, x] = rise_cell
        return carry

    lax.fori_loop(1, EXT - 1, look_up, 0)


def right_of(low, high, last):
    a, b = pltpu.roll(low, LANES - 1, 1), pltpu.roll(high, LANES - 1, 1)
    return jnp.where(last, b, a), b


def left_of(low, high, first):
    a, b = pltpu.roll(low, 1, 1), pltpu.roll(high, 1, 1)
    return a, jnp.where(first, a, b)


def fine_iteration(
    field, other, reluct, c_x, c_y, c_up, c_down, weight, diag, sums, drive, floor, rise,
):
    mid = slice(TOP, TOP + EXT)
    plus = slice(TOP + 1, TOP + EXT + 1)
    minus = slice(TOP - 1, TOP + EXT - 1)
    lane = lax.broadcasted_iota(jnp.int32, (EXT, LANES), 1)
    first, last = lane == 0, lane == LANES - 1

    def reluct_plane(x, carry):
        along_z = []
        for comp in range(2):
            low, high = field[comp, 0, x, mid], field[comp, 1, x, mid]
            r0, r1 = right_of(low, high, last)
            l0, l1 = left_of(low, high, first)
            along_z.append((r0 - jnp.where(first, 0.0, l0), jnp.where(last, 0.0, r1) - l1))
        for half in range(2):
            def along_y(comp):
                return field[comp, half, x, plus] - field[comp, half, x, minus]

            def along_x(comp):
                return field[comp, half, x + 1, mid] - field[comp, half, x - 1, mid]

            b0 = along_y(2) - along_z[1][half]
            b1 = along_z[0][half] - along_x(2)
            b2 = along_x(1) - along_y(0)
            square = 0.25 * (b0 * b0 + b1 * b1 + b2 * b2)
            reluct[half, x, mid] = floor[half, x] + rise[half, x] * (square / (1.0 + square))
        return carry

    lax.fori_loop(1, EXT - 1, reluct_plane, 0)

    for half in range(2):
        c_x[half, 1, mid] = reluct[half, 1, mid] + reluct[half, 2, mid]

    def coeff_plane(x, carry):
        low, high = reluct[0, x, mid], reluct[1, x, mid]
        r0, r1 = right_of(low, high, last)
        l0, l1 = left_of(low, high, first)
        ups = (low + r0, high + jnp.where(last, 0.0, r1))
        downs = (low + jnp.where(first, 0.0, l0), high + l1)
        for half in range(2):
            here = (low, high)[half]
            x_plus = here + reluct[half, x + 1, mid]
            x_minus = here + reluct[half, x - 1, mid]
            y_plus = here + reluct[half, x, plus]
            y_minus = here + reluct[half, x, minus]
            total = ((x_plus + x_minus) + (y_plus + y_minus)) + (ups[half] + downs[half])
            c_x[half, x, mid] = x_plus
            c_y[half, x, mid] = y_plus
            c_up[half, x, mid] = ups[half] if half == 0 else jnp.where(last, 0.0, ups[half])
            c_down[half, x, mid] = jnp.where(first, 0.0, downs[half]) if half == 0 else downs[half]
            diag[half, x, mid] = total
            weight[half, x, mid] = jnp.where(floor[half, x] > 0.0, RELAX / total, 0.0)
        return carry

    lax.fori_loop(2, EXT - 2, coeff_plane, 0)

    def off_diagonal(src, comp, x, rows, first_lane, last_lane):
        rows_plus = slice(rows.start + 1, rows.stop + 1)
        rows_minus = slice(rows.start - 1, rows.stop - 1)
        low, high = src[comp, 0, x, rows], src[comp, 1, x, rows]
        rights = right_of(low, high, last_lane)
        lefts = left_of(low, high, first_lane)
        out = []
        for half in range(2):
            out.append(
                (
                    c_x[half, x, rows] * src[comp, half, x + 1, rows]
                    + c_x[half, x - 1, rows] * src[comp, half, x - 1, rows]
                )
                + (
                    c_y[half, x, rows] * src[comp, half, x, rows_plus]
                    + c_y[half, x, rows_minus] * src[comp, half, x, rows_minus]
                )
                + (c_up[half, x, rows] * rights[half] + c_down[half, x, rows] * lefts[half])
            )
        return (low, high), out

    def sweep(src, dst, begin, end):
        def plane(x, carry):
            for comp in range(3):
                here, off = off_diagonal(src, comp, x, mid, first, last)
                for half in range(2):
                    dst[comp, half, x, mid] = (1.0 - RELAX) * here[half] + weight[half, x, mid] * (
                        drive[comp, half, x] + off[half]
                    )
            return carry

        lax.fori_loop(begin, end, plane, 0)

    sweep(field, other, 2, EXT - 2)
    sweep(other, field, 3, EXT - 3)

    own = slice(CORE, CORE + BLOCK)
    lane = lax.broadcasted_iota(jnp.int32, (BLOCK, LANES), 1)
    first_own, last_own = lane == 0, lane == LANES - 1
    zero = jnp.zeros((BLOCK, LANES), jnp.float32)
    result = jnp.zeros((8, LANES), jnp.float32)
    sums[...] = jnp.zeros(sums.shape, jnp.float32)
    for coarse in range(BLOCK // COARSEN):
        def plane(step, totals):
            x = HALO + coarse * COARSEN + step
            out = []
            for comp in range(3):
                here, off = off_diagonal(field, comp, x, own, first_own, last_own)
                for half in range(2):
                    out.append(
                        totals[comp * 2 + half]
                        + (
                            drive[comp, half, x, HALO : HALO + BLOCK]
                            - (diag[half, x, own] * here[half] - off[half])
                        )
                    )
            for half in range(2):
                out.append(totals[6 + half] + reluct[half, x, own])
            return tuple(out)

        totals = lax.fori_loop(0, COARSEN, plane, (zero,) * 8)
        for part in range(BLOCK // COARSEN):
            group = coarse * 2 + part
            for comp in range(4):
                scale = 0.5 if comp < 3 else 1.0 / float(COARSEN ** 3)
                for half in range(2):
                    block = totals[comp * 2 + half][part * COARSEN : (part + 1) * COARSEN]
                    sums[group, comp : comp + 1, half * LANES : (half + 1) * LANES] = scale * jnp.sum(
                        block, axis=0, keepdims=True
                    )
            result = result + jnp.dot(
                sums[group], gather_matrix(group), precision=HIGH, preferred_element_type=jnp.float32
            )
    return result[0:4]


SCRATCH = (
    [pltpu.VMEM((3, 2, EXT, ROWS, LANES), jnp.float32)] * 2
    + [pltpu.VMEM((2, EXT, ROWS, LANES), jnp.float32)] * 7
    + [pltpu.VMEM((4, 8, 2 * LANES), jnp.float32)]
)


def emit(field, coarse, field_out, low_out, high_out, coarse_out):
    own = slice(CORE, CORE + BLOCK)
    for comp in range(3):
        for half in range(2):
            z = slice(half * LANES, half * LANES + LANES)
            field_out[comp, :, :, z] = field[comp, half, 4:20, own, :]
            if low_out is not None:
                low_out[comp * 4 : comp * 4 + 4, :, z] = field[comp, half, 4:8, own, :]
                high_out[comp * 4 : comp * 4 + 4, :, z] = field[comp, half, 16:20, own, :]
    coarse_out[...] = jnp.broadcast_to(coarse[None], coarse_out.shape)


def first_kernel(
    potential, source, coil_mask, labels, low, high, back, front, floor_table, rise_table,
    field_out, low_out, high_out, coarse_out, drive, floor, rise, *scratch,
):
    row, rows, col, cols = place()
    field = scratch[0]
    put_field(field, potential, low, high, back, front, row, rows, col, cols)
    put_material(
        drive, floor, rise, source, coil_mask, labels, low, high, back, front, floor_table,
        rise_table, row, rows, col, cols,
    )
    coarse = fine_iteration(*scratch, drive, floor, rise)
    emit(field, coarse, field_out, low_out, high_out, coarse_out)


def first_iteration(potential, source, coil_mask, labels, low, high, back, front, tables, devices):
    depth = potential.shape[-1]
    return pl.pallas_call(
        first_kernel,
        in_specs=[VMEM] * 8 + [SMEM] * 2,
        out_specs=[VMEM] * 7,
        out_shape=[
            f32(*potential.shape),
            f32(3 * HALO, BLOCK, depth),
            f32(3 * HALO, BLOCK, depth),
            f32(devices, 4, LANES),
            f32(3, 2, EXT, EXT, LANES),
            f32(2, EXT, EXT, LANES),
            f32(2, EXT, EXT, LANES),
        ],
        scratch_shapes=SCRATCH,
        compiler_params=PARAMS,
        name="first_iteration",
    )(potential, source, coil_mask, labels, low, high, back, front, *tables)


def next_kernel(
    final, gathered, core, low, high, back, front, drive, floor, rise, *refs
):
    if final:
        field_out, coarse_out, reluct_out, *scratch = refs
        low_out = high_out = None
    else:
        field_out, low_out, high_out, coarse_out, *scratch = refs
    table, picked = scratch[-2:]
    scratch = scratch[:-2]
    row, rows, col, cols = place()
    field = scratch[0]
    targets, relucts = [], []
    for stripe in range(3):
        index = jnp.clip(col + stripe - 1, 0, cols - 1)
        target, reluct = load_stripe(
            table.at[stripe], gathered, gathered.shape[0] , lambda r: gathered[r, index]
        )
        targets.append(target)
        relucts.append(reluct)
    corrections = coarse_solve(targets, relucts)
    put_field(field, core, low, high, back, front, row, rows, col, cols)
    picked[...] = jnp.zeros(picked.shape, jnp.float32)
    for stripe in range(3):
        there = (col > 0, True, col < cols - 1)[stripe]
        for comp in range(3):
            for shift in range(3):
                line = pick_row(corrections[stripe][comp], row + shift - 1)
                spot = (stripe * 3 + comp) * 3 + shift
                picked[spot : spot + 1, :] = jnp.where(there, line, 0.0)
    wide = [
        jnp.dot(picked[...], spread_matrix(group), precision=HIGH, preferred_element_type=jnp.float32)
        for group in range(4)
    ]
    mid = slice(TOP, TOP + EXT)
    cell = lax.broadcasted_iota(jnp.int32, (EXT, LANES), 0)
    for begin, end, shift, x in ((0, 4, 0, 1), (4, 12, 1, 0), (12, 20, 1, 1), (20, 24, 2, 0)):
        for comp in range(3):
            for half in range(2):
                def line(stripe, y):
                    spot = (stripe * 3 + comp) * 3 + shift
                    return wide[x * 2 + y][spot : spot + 1, half * LANES : (half + 1) * LANES]

                tile = jnp.where(
                    cell < 12,
                    jnp.where(cell < 4, line(0, 1), line(1, 0)),
                    jnp.where(cell < 20, line(1, 1), line(2, 0)),
                )
                for plane in range(begin, end):
                    field[comp, half, plane, mid] = field[comp, half, plane, mid] + tile
    coarse = fine_iteration(*scratch, drive, floor, rise)
    emit(field, coarse, field_out, low_out, high_out, coarse_out)
    if final:
        reluct = scratch[2]
        for half in range(2):
            reluct_out[:, :, half * LANES : (half + 1) * LANES] = reluct[
                half, 4:20, CORE : CORE + BLOCK, :
            ]


def next_iteration(final, gathered, core, low, high, back, front, material, devices):
    depth = core.shape[-1]
    edge = f32(3 * HALO, BLOCK, depth)
    coarse = f32(devices, 4, LANES)
    if final:
        outs = [f32(*core.shape), coarse, f32(*core.shape[1:])]
    else:
        outs = [f32(*core.shape), edge, edge, coarse]
    return pl.pallas_call(
        functools.partial(next_kernel, final),
        in_specs=[VMEM] * 9,
        out_specs=[VMEM] * len(outs),
        out_shape=outs,
        scratch_shapes=SCRATCH
        + [
            pltpu.VMEM((3, 4, gathered.shape[0], LANES), jnp.float32),
            pltpu.VMEM((32, LANES), jnp.float32),
        ],
        compiler_params=PARAMS,
        name="last_iteration" if final else "next_iteration",
    )(gathered, core, low, high, back, front, *material)


def correct_kernel(gathered, core, field_out, target_out, table, picked):
    row, rows, col, cols = place()
    target, reluct = load_stripe(table, gathered, gathered.shape[0], lambda r: gathered[r])
    correction, = coarse_solve([target], [reluct])
    picked[...] = jnp.zeros(picked.shape, jnp.float32)
    for comp in range(3):
        picked[comp : comp + 1, :] = pick_row(correction[comp], row)
    wide = [
        jnp.dot(picked[...], spread_matrix(group), precision=HIGH, preferred_element_type=jnp.float32)
        for group in range(4)
    ]
    cell = lax.broadcasted_iota(jnp.int32, (BLOCK, 2 * LANES), 0)
    for x in range(2):
        for comp in range(3):
            tile = jnp.where(
                cell < COARSEN, wide[x * 2][comp : comp + 1, :], wide[x * 2 + 1][comp : comp + 1, :]
            )
            for plane in range(x * COARSEN, (x + 1) * COARSEN):
                field_out[comp, plane] = core[comp, plane] + tile
    for comp in range(3):
        for x in range(2):
            for y in range(2):
                group = x * 2 + y
                moved = target[comp] if group == 0 else pltpu.roll(target[comp], LANES - 32 * group, 1)
                for r in range(gathered.shape[0]):
                    target_out[comp, 2 * r + x, y : y + 1, :] = moved[r : r + 1, 0:32]


def correct(gathered, core):
    rows = gathered.shape[0]
    return pl.pallas_call(
        correct_kernel,
        in_specs=[VMEM] * 2,
        out_specs=[VMEM] * 2,
        out_shape=[f32(*core.shape), f32(3, 2 * rows, 2, 32)],
        scratch_shapes=[
            pltpu.VMEM((4, rows, LANES), jnp.float32),
            pltpu.VMEM((8, LANES), jnp.float32),
        ],
        compiler_params=PARAMS,
        name="correct",
    )(gathered, core)


def swap(axis, to_low, to_high):
    count = lax.axis_size(axis)
    forward = [(i, (i + 1) % count) for i in range(count)]
    backward = [(target, source) for source, target in forward]
    return lax.ppermute(to_high, axis, forward), lax.ppermute(to_low, axis, backward)


def shards(potential, source, labels, coil_mask, floor_table, rise_table):
    rows, cols = lax.axis_size("row"), lax.axis_size("col")
    low, high = swap("row", *pack_x(potential, source, labels, coil_mask))
    back, front = swap("col", *pack_y(potential, source, labels, coil_mask, low, high))
    field, to_low, to_high, coarse, *material = first_iteration(
        potential, source, coil_mask, labels, low, high, back, front, (floor_table, rise_table),
        rows * cols,
    )
    for iteration in range(1, ITERS):
        final = iteration == ITERS - 1
        gathered = lax.all_to_all(coarse, ("row", "col"), 0, 0)
        gathered = gathered.reshape(rows, cols, 4, LANES)
        low, high = swap("row", to_low, to_high)
        back, front = swap("col", *pack_edge(field, low, high))
        outs = next_iteration(
            final, gathered, field, low, high, back, front, material, rows if final else rows * cols
        )
        if final:
            field, coarse, reluct = outs
        else:
            field, to_low, to_high, coarse = outs
    gathered = lax.all_to_all(coarse, "row", 0, 0)
    field, coarse_target = correct(gathered, field)
    return (field, reluct, coarse_target)


def solution(mesh):
    in_specs = (
        P(None, "row", "col", None),
        P(None, "row", "col", None),
        P("row", "col", None),
        P("row", "col", None),
        P(),
        P(),
    )
    out_specs = (P(None, "row", "col", None), P("row", "col", None), P(None, None, "col", None))
    return jax.shard_map(shards, mesh=mesh, in_specs=in_specs, out_specs=out_specs, check_vma=False)
```

```python
import functools
import jax
import jax.numpy as jnp
from jax import lax
from jax.experimental import pallas as pl
from jax.experimental.pallas import tpu as pltpu
from jax.sharding import PartitionSpec as P

ITERS = 3
SWEEPS = 2
COARSE_SWEEPS = 16
COARSEN = 8
RELAX = 0.8

HALO = 4
BLOCK = 16
EXT = BLOCK + 2 * HALO
LANES = 128
TOP = 8
CORE = TOP + HALO
ROWS = 40
HIGH = lax.Precision.HIGHEST
X_PAGES = 21
Y_PAGES = 88

VMEM = pl.BlockSpec(memory_space=pltpu.VMEM)
SMEM = pl.BlockSpec(memory_space=pltpu.SMEM)
PARAMS = pltpu.CompilerParams(vmem_limit_bytes=44 * 1024 * 1024)


def f32(*shape):
    return jax.ShapeDtypeStruct(shape, jnp.float32)


def turns(even, low_edge, high_edge):
    return jnp.where(even, high_edge, low_edge), jnp.where(even, low_edge, high_edge)


def corner_parts(reach):
    first = 0
    parts = []
    for distance in range(1, reach):
        parts.append((distance, first, reach - distance))
        first += reach - distance
    return parts, first


CORNER_FIELD, FIELD_ROWS = corner_parts(4)
CORNER_LABEL, LABEL_ROWS = corner_parts(3)
CORNER_DRIVE = 6 * FIELD_ROWS
CORNER_TABLE = CORNER_DRIVE + 6
CORNER_ALL = CORNER_TABLE + 2 * LABEL_ROWS
CORNER_LATER = 40


def pack_first_kernel(
    potential, source, coil_mask, labels, x_lo, x_hi, y_a, y_b,
    pot_x, src_x, mask_x, lab_x, pot_y, src_y, mask_y, lab_y, sems,
):
    even = lax.axis_index("col") % 2 == 0
    copies = []

    def fetch(ref, scratch):
        copy = pltpu.make_async_copy(ref, scratch, sems.at[len(copies)])
        copy.start()
        copies.append(copy)

    for side, (cells, pair, rows) in enumerate((
        (slice(0, 4), slice(0, 2), slice(0, 8)),
        (slice(BLOCK - 4, BLOCK), slice(BLOCK - 2, BLOCK), slice(BLOCK - 8, BLOCK)),
    )):
        fetch(potential.at[:, cells], pot_x.at[side])
        fetch(source.at[:, pair], src_x.at[side])
        fetch(coil_mask.at[pair], mask_x.at[side])
        fetch(labels.at[cells], lab_x.at[side])
        fetch(potential.at[:, :, rows], pot_y.at[side])
        fetch(source.at[:, :, rows], src_y.at[side])
        fetch(coil_mask.at[:, rows], mask_y.at[side])
        fetch(labels.at[:, rows], lab_y.at[side])
    for copy in copies:
        copy.wait()
    for side, out in enumerate((x_lo, x_hi)):
        for comp in range(3):
            out[comp * 4 : comp * 4 + 4] = pot_x[side, comp]
            out[12 + comp * 2 : 14 + comp * 2] = (
                2.0 * src_x[side, comp] * mask_x[side].astype(jnp.float32)
            )
        out[18:21] = lab_x[side, side : side + 3].astype(jnp.float32)

    def send(page, low_edge, high_edge, rows=slice(0, 4)):
        first, second = turns(even, low_edge, high_edge)
        y_a[page, rows] = first
        y_b[page, rows] = second

    for x in range(BLOCK):
        mask_lo = 2.0 * mask_y[0, x, 0:2].astype(jnp.float32)
        mask_hi = 2.0 * mask_y[1, x, 6:8].astype(jnp.float32)
        for comp in range(3):
            send(comp * 16 + x, pot_y[0, comp, x, 0:4], pot_y[1, comp, x, 4:8])
            send(
                48 + comp * 8 + x // 2, src_y[0, comp, x, 0:2] * mask_lo,
                src_y[1, comp, x, 6:8] * mask_hi, slice((x % 2) * 2, (x % 2) * 2 + 2),
            )
        send(72 + x, lab_y[0, x, 0:4].astype(jnp.float32), lab_y[1, x, 4:8].astype(jnp.float32))


def pack_first(potential, source, labels, coil_mask):
    depth = potential.shape[-1]
    scratch = [
        pltpu.VMEM((2, 3, 4, BLOCK, depth), jnp.float32),
        pltpu.VMEM((2, 3, 2, BLOCK, depth), jnp.float32),
        pltpu.VMEM((2, 2, BLOCK, depth), jnp.int32),
        pltpu.VMEM((2, 4, BLOCK, depth), jnp.int32),
        pltpu.VMEM((2, 3, BLOCK, 8, depth), jnp.float32),
        pltpu.VMEM((2, 3, BLOCK, 8, depth), jnp.float32),
        pltpu.VMEM((2, BLOCK, 8, depth), jnp.int32),
        pltpu.VMEM((2, BLOCK, 8, depth), jnp.int32),
        pltpu.SemaphoreType.DMA((16,)),
    ]
    return pl.pallas_call(
        pack_first_kernel,
        in_specs=[pl.BlockSpec(memory_space=pl.ANY)] * 4,
        out_specs=[VMEM] * 4,
        out_shape=[f32(X_PAGES, BLOCK, depth)] * 2 + [f32(Y_PAGES, HALO, depth)] * 2,
        scratch_shapes=scratch,
        compiler_params=PARAMS,
        name="pack_first",
    )(potential, source, coil_mask, labels)


def pack_corner_kernel(whole, low, high, out_a, out_b):
    even = lax.axis_index("col") % 2 == 0

    def send(row, count, ref, page):
        rows = slice(row, row + count)
        first, second = turns(even, ref[page, 0:count], ref[page, BLOCK - count : BLOCK])
        out_a[rows, :] = first
        out_b[rows, :] = second

    for comp in range(3):
        for distance, first, count in CORNER_FIELD:
            row = comp * 2 * FIELD_ROWS + first
            send(row, count, low, comp * 4 + 4 - distance)
            send(row + FIELD_ROWS, count, high, comp * 4 + distance - 1)
        if whole:
            send(CORNER_DRIVE + comp * 2, 1, low, 12 + comp * 2 + 1)
            send(CORNER_DRIVE + comp * 2 + 1, 1, high, 12 + comp * 2)
    if whole:
        for distance, first, count in CORNER_LABEL:
            row = CORNER_TABLE + first
            send(row, count, low, 18 + 3 - distance)
            send(row + LABEL_ROWS, count, high, 18 + distance - 1)


def pack_corner(whole, low, high):
    depth = low.shape[-1]
    return pl.pallas_call(
        functools.partial(pack_corner_kernel, whole),
        in_specs=[VMEM] * 2,
        out_specs=[VMEM] * 2,
        out_shape=[f32(CORNER_ALL if whole else CORNER_LATER, depth)] * 2,
        compiler_params=PARAMS,
        name="pack_corner",
    )(low, high)


def coarse_solve(targets, relucts):
    shape = relucts[0].shape
    count = shape[0]
    lane = lax.broadcasted_iota(jnp.int32, shape, 1)
    row = lax.broadcasted_iota(jnp.int32, shape, 0)
    z = lane % 32
    first_y = (lane // 32) % 2 == 0
    first_x = lane // 64 == 0
    up_ok, down_ok = z < 31, z > 0
    far_ok = jnp.logical_not(
        jnp.logical_or(
            jnp.logical_and(first_x, row == 0),
            jnp.logical_and(jnp.logical_not(first_x), row == count - 1),
        )
    )

    def up(v):
        return pltpu.roll(v, LANES - 1, 1)

    def down(v):
        return pltpu.roll(v, 1, 1)

    def side(v):
        return jnp.where(first_y, pltpu.roll(v, LANES - 32, 1), pltpu.roll(v, 32, 1))

    def near(v):
        return pltpu.roll(v, 64, 1)

    def far(swapped):
        return jnp.where(first_x, pltpu.roll(swapped, 1, 0), pltpu.roll(swapped, count - 1, 0))

    sets = []
    for r in relucts:
        swapped = near(r)
        c_up = r + jnp.where(up_ok, up(r), 0.0)
        c_down = r + jnp.where(down_ok, down(r), 0.0)
        c_side = r + side(r)
        c_near = r + swapped
        c_far = r + jnp.where(far_ok, far(swapped), 0.0)
        diag = ((c_up + c_down) + (c_side + r)) + (c_near + c_far)
        c_up = jnp.where(up_ok, c_up, 0.0)
        c_down = jnp.where(down_ok, c_down, 0.0)
        c_far = jnp.where(far_ok, c_far, 0.0)
        sets.append((c_up, c_down, c_side, c_near, c_far, diag, RELAX / diag))

    def neighbours(coeffs, v):
        c_up, c_down, c_side, c_near, c_far = coeffs[:5]
        swapped = near(v)
        return (
            (c_up * up(v) + c_down * down(v)) + (c_side * side(v) + c_near * swapped)
        ) + c_far * far(swapped)

    doubled = [[2.0 * t for t in stripe] for stripe in targets]
    start = [
        [coeffs[6] * t for t in stripe] for coeffs, stripe in zip(sets, doubled)
    ]

    def sweep(step, values):
        return [
            [
                (1.0 - RELAX) * v + coeffs[6] * (t + neighbours(coeffs, v))
                for v, t in zip(stripe, stripe_t)
            ]
            for coeffs, stripe, stripe_t in zip(sets, values, doubled)
        ]

    values = lax.fori_loop(0, COARSE_SWEEPS - 1, sweep, start)
    out = []
    for coeffs, stripe, stripe_t in zip(sets, values, doubled):
        total = jnp.sum(jnp.sum(coeffs[5], axis=1, keepdims=True), axis=0, keepdims=True)
        done = []
        for v, t in zip(stripe, stripe_t):
            left = t - (coeffs[5] * v - neighbours(coeffs, v))
            left = jnp.sum(jnp.sum(left, axis=1, keepdims=True), axis=0, keepdims=True)
            done.append(v + left / total)
        out.append(done)
    return out


def pick_row(values, index):
    row = lax.broadcasted_iota(jnp.int32, values.shape, 0)
    return jnp.sum(jnp.where(row == index, values, 0.0), axis=0, keepdims=True)


def spread_matrix(group):
    lane = lax.broadcasted_iota(jnp.int32, (LANES, 2 * LANES), 0)
    cell = lax.broadcasted_iota(jnp.int32, (LANES, 2 * LANES), 1)
    return jnp.where(lane == group * 32 + cell // COARSEN, 1.0, 0.0)


def gather_matrix(group):
    cell = lax.broadcasted_iota(jnp.int32, (2 * LANES, LANES), 0)
    lane = lax.broadcasted_iota(jnp.int32, (2 * LANES, LANES), 1)
    return jnp.where(lane == group * 32 + cell // COARSEN, 1.0, 0.0)


def load_stripe(table, gathered, count, pick):
    for row in range(count):
        for comp in range(4):
            table[comp, row : row + 1, :] = pick(row)[comp : comp + 1, :]
    scale = 1.0 / float(COARSEN * COARSEN)
    return [table[comp] * scale for comp in range(3)], table[3]


class Place:
    def __init__(self):
        self.row, self.rows = lax.axis_index("row"), lax.axis_size("row")
        self.col, self.cols = lax.axis_index("col"), lax.axis_size("col")
        self.low, self.high = self.row > 0, self.row < self.rows - 1
        self.back, self.front = self.col > 0, self.col < self.cols - 1
        self.even = self.col % 2 == 0

    def sides(self, turn_a, turn_b):
        return jnp.where(self.even, turn_b, turn_a), jnp.where(self.even, turn_a, turn_b)


def put_corner(put, message, place, row, distance, count):
    for side, there in ((0, place.low), (1, place.high)):
        back, front = place.sides(message[0](row[side], count), message[1](row[side], count))
        plane = HALO - distance if side == 0 else HALO + BLOCK - 1 + distance
        put(plane, HALO - count, count, jnp.logical_and(there, place.back), back)
        put(plane, HALO + BLOCK, count, jnp.logical_and(there, place.front), front)


def put_field(field, core, low, high, y_a, y_b, c_a, c_b, place):
    for comp in range(3):
        for half in range(2):
            z = slice(half * LANES, half * LANES + LANES)
            own = slice(CORE, CORE + BLOCK)
            field[comp, half, 4:20, own, :] = core[comp, :, :, z]
            pages = slice(comp * 4, comp * 4 + 4)
            field[comp, half, 0:4, own, :] = jnp.where(place.low, low[pages, :, z], 0.0)
            field[comp, half, 20:24, own, :] = jnp.where(place.high, high[pages, :, z], 0.0)
            pages = slice(comp * 16, comp * 16 + 16)
            back, front = place.sides(y_a[pages, :, z], y_b[pages, :, z])
            field[comp, half, 4:20, TOP : TOP + HALO, :] = jnp.where(place.back, back, 0.0)
            field[comp, half, 4:20, CORE + BLOCK : CORE + BLOCK + HALO, :] = jnp.where(
                place.front, front, 0.0
            )

            def put(plane, row, count, there, value):
                field[comp, half, plane, TOP + row : TOP + row + count, :] = jnp.where(
                    there, value, 0.0
                )

            message = [
                lambda row, count, ref=ref: ref[row : row + count, z] for ref in (c_a, c_b)
            ]
            for distance, first, count in CORNER_FIELD:
                row = comp * 2 * FIELD_ROWS + first
                put_corner(put, message, place, (row, row + FIELD_ROWS), distance, count)


def put_material(
    drive, floor, rise, source, coil_mask, labels, low, high, y_a, y_b, c_a, c_b, floor_table,
    rise_table, place,
):
    for half in range(2):
        z = slice(half * LANES, half * LANES + LANES)
        own = slice(HALO, HALO + BLOCK)
        coil = 2.0 * coil_mask[:, :, z].astype(jnp.float32)
        message = [lambda row, count, ref=ref: ref[row : row + count, z] for ref in (c_a, c_b)]
        for comp in range(3):
            drive[comp, half, 4:20, own, :] = source[comp, :, :, z] * coil
            pages = slice(12 + comp * 2, 14 + comp * 2)
            drive[comp, half, 2:4, own, :] = low[pages, :, z]
            drive[comp, half, 20:22, own, :] = high[pages, :, z]
            for x in range(BLOCK):
                page, part = 48 + comp * 8 + x // 2, slice((x % 2) * 2, (x % 2) * 2 + 2)
                back, front = place.sides(y_a[page, part, z], y_b[page, part, z])
                drive[comp, half, 4 + x, 2:4, :] = back
                drive[comp, half, 4 + x, 20:22, :] = front

            def put_drive(plane, row, count, there, value):
                drive[comp, half, plane, row : row + count, :] = value

            row = CORNER_DRIVE + comp * 2
            put_corner(put_drive, message, place, (row, row + 1), 1, 1)
        floor[half, 4:20, own, :] = labels[:, :, z].astype(jnp.float32)
        floor[half, 1:4, own, :] = jnp.where(place.low, low[18:21, :, z], -1.0)
        floor[half, 20:23, own, :] = jnp.where(place.high, high[18:21, :, z], -1.0)
        back, front = place.sides(y_a[72:88, :, z], y_b[72:88, :, z])
        floor[half, 4:20, 0:HALO, :] = jnp.where(place.back, back, -1.0)
        floor[half, 4:20, HALO + BLOCK : EXT, :] = jnp.where(place.front, front, -1.0)

        def put_label(plane, row, count, there, value):
            floor[half, plane, row : row + count, :] = jnp.where(there, value, -1.0)

        for distance, first, count in CORNER_LABEL:
            row = CORNER_TABLE + first
            put_corner(put_label, message, place, (row, row + LABEL_ROWS), distance, count)

    def look_up(x, carry):
        for half in range(2):
            label = floor[half, x]
            floor_cell = jnp.zeros_like(label)
            rise_cell = jnp.zeros_like(label)
            for number in range(floor_table.shape[0]):
                chosen = label == float(number)
                floor_cell = jnp.where(chosen, floor_table[number], floor_cell)
                rise_cell = jnp.where(chosen, rise_table[number], rise_cell)
            floor[half, x] = floor_cell
            rise[half, x] = rise_cell
        return carry

    lax.fori_loop(1, EXT - 1, look_up, 0)


def right_of(low, high, last):
    a, b = pltpu.roll(low, LANES - 1, 1), pltpu.roll(high, LANES - 1, 1)
    return jnp.where(last, b, a), b


def left_of(low, high, first):
    a, b = pltpu.roll(low, 1, 1), pltpu.roll(high, 1, 1)
    return a, jnp.where(first, a, b)


def in_pairs(begin, end, plane):
    def step(number, carry):
        x = begin + 2 * number
        for ref, value in plane(x) + plane(x + 1):
            ref[...] = value
        return carry

    lax.fori_loop(0, (end - begin) // 2, step, 0)


def fine_iteration(
    field, other, reluct, c_x, c_y, c_up, c_down, weight, diag, sums, drive, floor, rise,
):
    mid = slice(TOP, TOP + EXT)
    plus = slice(TOP + 1, TOP + EXT + 1)
    minus = slice(TOP - 1, TOP + EXT - 1)
    lane = lax.broadcasted_iota(jnp.int32, (EXT, LANES), 1)
    first, last = lane == 0, lane == LANES - 1

    def reluct_plane(x):
        stores = []
        along_z = []
        for comp in range(2):
            low, high = field[comp, 0, x, mid], field[comp, 1, x, mid]
            r0, r1 = right_of(low, high, last)
            l0, l1 = left_of(low, high, first)
            along_z.append((r0 - jnp.where(first, 0.0, l0), jnp.where(last, 0.0, r1) - l1))
        for half in range(2):
            def along_y(comp):
                return field[comp, half, x, plus] - field[comp, half, x, minus]

            def along_x(comp):
                return field[comp, half, x + 1, mid] - field[comp, half, x - 1, mid]

            b0 = along_y(2) - along_z[1][half]
            b1 = along_z[0][half] - along_x(2)
            b2 = along_x(1) - along_y(0)
            square = 0.25 * (b0 * b0 + b1 * b1 + b2 * b2)
            stores.append((
                reluct.at[half, x, mid], floor[half, x] + rise[half, x] * (square / (1.0 + square))
            ))
        return stores

    in_pairs(1, EXT - 1, reluct_plane)

    def apply(src, x, rows, coeffs, first_lane, last_lane):
        rows_plus = slice(rows.start + 1, rows.stop + 1)
        rows_minus = slice(rows.start - 1, rows.stop - 1)
        out = []
        for comp in range(3):
            low, high = src[comp, 0, x, rows], src[comp, 1, x, rows]
            rights = right_of(low, high, last_lane)
            lefts = left_of(low, high, first_lane)
            for half in range(2):
                x_plus, x_minus, y_plus, y_minus, up, down = coeffs[half]
                total = (
                    (x_plus * src[comp, half, x + 1, rows] + x_minus * src[comp, half, x - 1, rows])
                    + (y_plus * src[comp, half, x, rows_plus] + y_minus * src[comp, half, x, rows_minus])
                    + (up * rights[half] + down * lefts[half])
                )
                out.append((comp, half, (low, high)[half], total))
        return out

    def load_coeffs(x, rows):
        rows_minus = slice(rows.start - 1, rows.stop - 1)
        return [
            (
                c_x[half, x, rows], c_x[half, x - 1, rows], c_y[half, x, rows],
                c_y[half, x, rows_minus], c_up[half, x, rows], c_down[half, x, rows],
            )
            for half in range(2)
        ]

    def first_plane(x):
        low, high = reluct[0, x, mid], reluct[1, x, mid]
        r0, r1 = right_of(low, high, last)
        l0, l1 = left_of(low, high, first)
        ups = (low + r0, high + jnp.where(last, 0.0, r1))
        downs = (low + jnp.where(first, 0.0, l0), high + l1)
        stores, coeffs, weights = [], [], []
        for half in range(2):
            here = (low, high)[half]
            x_plus = here + reluct[half, x + 1, mid]
            x_minus = here + reluct[half, x - 1, mid]
            y_plus = here + reluct[half, x, plus]
            y_minus = here + reluct[half, x, minus]
            total = ((x_plus + x_minus) + (y_plus + y_minus)) + (ups[half] + downs[half])
            up = ups[half] if half == 0 else jnp.where(last, 0.0, ups[half])
            down = jnp.where(first, 0.0, downs[half]) if half == 0 else downs[half]
            scale = jnp.where(floor[half, x] > 0.0, RELAX / total, 0.0)
            coeffs.append((x_plus, x_minus, y_plus, y_minus, up, down))
            weights.append(scale)
            for ref, value in (
                (c_x, x_plus), (c_y, y_plus), (c_up, up), (c_down, down), (diag, total), (weight, scale),
            ):
                stores.append((ref.at[half, x, mid], value))
        for comp, half, here, total in apply(field, x, mid, coeffs, first, last):
            stores.append((
                other.at[comp, half, x, mid],
                (1.0 - RELAX) * here + weights[half] * (drive[comp, half, x] + total),
            ))
        return stores

    in_pairs(2, EXT - 2, first_plane)

    def second_plane(x):
        stores = []
        weights = [weight[half, x, mid] for half in range(2)]
        for comp, half, here, total in apply(other, x, mid, load_coeffs(x, mid), first, last):
            stores.append((
                field.at[comp, half, x, mid],
                (1.0 - RELAX) * here + weights[half] * (drive[comp, half, x] + total),
            ))
        return stores

    in_pairs(3, EXT - 3, second_plane)

    own = slice(CORE, CORE + BLOCK)
    lane = lax.broadcasted_iota(jnp.int32, (BLOCK, LANES), 1)
    first_own, last_own = lane == 0, lane == LANES - 1
    zero = jnp.zeros((BLOCK, LANES), jnp.float32)
    result = jnp.zeros((8, LANES), jnp.float32)
    sums[...] = jnp.zeros(sums.shape, jnp.float32)
    for coarse in range(BLOCK // COARSEN):
        def plane(step, totals):
            x = HALO + coarse * COARSEN + step
            out = []
            diags = [diag[half, x, own] for half in range(2)]
            for comp, half, here, off in apply(
                field, x, own, load_coeffs(x, own), first_own, last_own
            ):
                out.append(
                    totals[comp * 2 + half]
                    + (drive[comp, half, x, HALO : HALO + BLOCK] - (diags[half] * here - off))
                )
            for half in range(2):
                out.append(totals[6 + half] + reluct[half, x, own])
            return tuple(out)

        totals = lax.fori_loop(0, COARSEN, plane, (zero,) * 8)
        for part in range(BLOCK // COARSEN):
            group = coarse * 2 + part
            for comp in range(4):
                scale = 0.5 if comp < 3 else 1.0 / float(COARSEN ** 3)
                for half in range(2):
                    block = totals[comp * 2 + half][part * COARSEN : (part + 1) * COARSEN]
                    sums[group, comp : comp + 1, half * LANES : (half + 1) * LANES] = scale * jnp.sum(
                        block, axis=0, keepdims=True
                    )
            result = result + jnp.dot(
                sums[group], gather_matrix(group), precision=HIGH, preferred_element_type=jnp.float32
            )
    return result[0:4]


SCRATCH = (
    [pltpu.VMEM((3, 2, EXT, ROWS, LANES), jnp.float32)] * 2
    + [pltpu.VMEM((2, EXT, ROWS, LANES), jnp.float32)] * 7
    + [pltpu.VMEM((4, 8, 2 * LANES), jnp.float32)]
)


def emit(field, coarse, field_out, edges, coarse_out, place):
    own = slice(CORE, CORE + BLOCK)
    for comp in range(3):
        for half in range(2):
            z = slice(half * LANES, half * LANES + LANES)
            field_out[comp, :, :, z] = field[comp, half, 4:20, own, :]
            if edges:
                x_lo, x_hi, y_a, y_b = edges
                x_lo[comp * 4 : comp * 4 + 4, :, z] = field[comp, half, 4:8, own, :]
                x_hi[comp * 4 : comp * 4 + 4, :, z] = field[comp, half, 16:20, own, :]
                first, second = turns(
                    place.even, field[comp, half, 4:20, CORE : CORE + 4, :],
                    field[comp, half, 4:20, CORE + BLOCK - 4 : CORE + BLOCK, :],
                )
                y_a[comp * 16 : comp * 16 + 16, :, z] = first
                y_b[comp * 16 : comp * 16 + 16, :, z] = second
    coarse_out[...] = jnp.broadcast_to(coarse[None], coarse_out.shape)


def edge_shapes(depth):
    return [f32(3 * HALO, BLOCK, depth)] * 2 + [f32(3 * BLOCK, HALO, depth)] * 2


def first_kernel(
    potential, source, coil_mask, labels, low, high, y_a, y_b, c_a, c_b, floor_table, rise_table,
    field_out, coarse_out, x_lo, x_hi, yo_a, yo_b, drive, floor, rise, *scratch,
):
    place = Place()
    field = scratch[0]
    put_field(field, potential, low, high, y_a, y_b, c_a, c_b, place)
    put_material(
        drive, floor, rise, source, coil_mask, labels, low, high, y_a, y_b, c_a, c_b, floor_table,
        rise_table, place,
    )
    coarse = fine_iteration(*scratch, drive, floor, rise)
    emit(field, coarse, field_out, (x_lo, x_hi, yo_a, yo_b), coarse_out, place)


def first_iteration(potential, source, coil_mask, labels, messages, tables, devices):
    depth = potential.shape[-1]
    return pl.pallas_call(
        first_kernel,
        in_specs=[VMEM] * 10 + [SMEM] * 2,
        out_specs=[VMEM] * 9,
        out_shape=[f32(*potential.shape), f32(devices, 4, LANES)]
        + edge_shapes(depth)
        + [f32(3, 2, EXT, EXT, LANES), f32(2, EXT, EXT, LANES), f32(2, EXT, EXT, LANES)],
        scratch_shapes=SCRATCH,
        compiler_params=PARAMS,
        name="first_iteration",
    )(potential, source, coil_mask, labels, *messages, *tables)


def solve_kernel(gathered, wide_out, table, picked):
    place = Place()
    targets, relucts = [], []
    for stripe in range(3):
        index = jnp.clip(place.col + stripe - 1, 0, place.cols - 1)
        target, reluct = load_stripe(
            table.at[stripe], gathered, gathered.shape[0], lambda r: gathered[r, index]
        )
        targets.append(target)
        relucts.append(reluct)
    corrections = coarse_solve(targets, relucts)
    picked[...] = jnp.zeros(picked.shape, jnp.float32)
    for stripe in range(3):
        there = (place.back, True, place.front)[stripe]
        for comp in range(3):
            for shift in range(3):
                line = pick_row(corrections[stripe][comp], place.row + shift - 1)
                spot = (stripe * 3 + comp) * 3 + shift
                picked[spot : spot + 1, :] = jnp.where(there, line, 0.0)
    for group in range(4):
        wide_out[group] = jnp.dot(
            picked[...], spread_matrix(group), precision=HIGH, preferred_element_type=jnp.float32
        )


def solve(gathered):
    return pl.pallas_call(
        solve_kernel,
        in_specs=[VMEM],
        out_specs=VMEM,
        out_shape=f32(4, 32, 2 * LANES),
        scratch_shapes=[
            pltpu.VMEM((3, 4, gathered.shape[0], LANES), jnp.float32),
            pltpu.VMEM((32, LANES), jnp.float32),
        ],
        compiler_params=PARAMS,
        name="solve",
    )(gathered)


def next_kernel(
    final, wide, core, low, high, y_a, y_b, c_a, c_b, drive, floor, rise, *refs
):
    if final:
        field_out, coarse_out, reluct_out, *scratch = refs
        edges = None
    else:
        field_out, coarse_out, x_lo, x_hi, yo_a, yo_b, *scratch = refs
        edges = (x_lo, x_hi, yo_a, yo_b)
    place = Place()
    field = scratch[0]
    put_field(field, core, low, high, y_a, y_b, c_a, c_b, place)
    mid = slice(TOP, TOP + EXT)
    cell = lax.broadcasted_iota(jnp.int32, (EXT, LANES), 0)
    for begin, end, shift, x in ((0, 4, 0, 1), (4, 12, 1, 0), (12, 20, 1, 1), (20, 24, 2, 0)):
        for comp in range(3):
            for half in range(2):
                def line(stripe, y):
                    spot = (stripe * 3 + comp) * 3 + shift
                    return wide[
                        x * 2 + y, spot : spot + 1, half * LANES : (half + 1) * LANES
                    ]

                tile = jnp.where(
                    cell < 12,
                    jnp.where(cell < 4, line(0, 1), line(1, 0)),
                    jnp.where(cell < 20, line(1, 1), line(2, 0)),
                )
                for plane in range(begin, end):
                    field[comp, half, plane, mid] = field[comp, half, plane, mid] + tile
    coarse = fine_iteration(*scratch, drive, floor, rise)
    emit(field, coarse, field_out, edges, coarse_out, place)
    if final:
        reluct = scratch[2]
        for half in range(2):
            reluct_out[:, :, half * LANES : (half + 1) * LANES] = reluct[
                half, 4:20, CORE : CORE + BLOCK, :
            ]


def next_iteration(final, wide, core, messages, material, devices):
    outs = [f32(*core.shape), f32(devices, 4, LANES)]
    outs += [f32(*core.shape[1:])] if final else edge_shapes(core.shape[-1])
    return pl.pallas_call(
        functools.partial(next_kernel, final),
        in_specs=[VMEM] * 11,
        out_specs=[VMEM] * len(outs),
        out_shape=outs,
        scratch_shapes=SCRATCH,
        compiler_params=PARAMS,
        name="last_iteration" if final else "next_iteration",
    )(wide, core, *messages, *material)


def correct_kernel(gathered, core, field_out, target_out, table, picked):
    row = lax.axis_index("row")
    target, reluct = load_stripe(table, gathered, gathered.shape[0], lambda r: gathered[r])
    correction, = coarse_solve([target], [reluct])
    picked[...] = jnp.zeros(picked.shape, jnp.float32)
    for comp in range(3):
        picked[comp : comp + 1, :] = pick_row(correction[comp], row)
    wide = [
        jnp.dot(picked[...], spread_matrix(group), precision=HIGH, preferred_element_type=jnp.float32)
        for group in range(4)
    ]
    cell = lax.broadcasted_iota(jnp.int32, (BLOCK, 2 * LANES), 0)
    for x in range(2):
        for comp in range(3):
            tile = jnp.where(
                cell < COARSEN, wide[x * 2][comp : comp + 1, :], wide[x * 2 + 1][comp : comp + 1, :]
            )
            for plane in range(x * COARSEN, (x + 1) * COARSEN):
                field_out[comp, plane] = core[comp, plane] + tile
    for comp in range(3):
        for x in range(2):
            for y in range(2):
                group = x * 2 + y
                moved = target[comp] if group == 0 else pltpu.roll(target[comp], LANES - 32 * group, 1)
                for r in range(gathered.shape[0]):
                    target_out[comp, 2 * r + x, y : y + 1, :] = moved[r : r + 1, 0:32]


def correct(gathered, core):
    rows = gathered.shape[0]
    return pl.pallas_call(
        correct_kernel,
        in_specs=[VMEM] * 2,
        out_specs=[VMEM] * 2,
        out_shape=[f32(*core.shape), f32(3, 2 * rows, 2, 32)],
        scratch_shapes=[
            pltpu.VMEM((4, rows, LANES), jnp.float32),
            pltpu.VMEM((8, LANES), jnp.float32),
        ],
        compiler_params=PARAMS,
        name="correct",
    )(gathered, core)


def rings(to_low, to_high):
    count = lax.axis_size("row")
    forward = [(i, (i + 1) % count) for i in range(count)]
    backward = [(target, source) for source, target in forward]
    return lax.ppermute(to_high, "row", forward), lax.ppermute(to_low, "row", backward)


def swaps(turn_a, turn_b):
    count = lax.axis_size("col")
    pairs = []
    for begin in (0, 1):
        partner = list(range(count))
        for i in range(begin, count - 1, 2):
            partner[i], partner[i + 1] = i + 1, i
        pairs.append(list(enumerate(partner)))
    return lax.ppermute(turn_a, "col", pairs[0]), lax.ppermute(turn_b, "col", pairs[1])


def shards(potential, source, labels, coil_mask, floor_table, rise_table):
    rows, cols = lax.axis_size("row"), lax.axis_size("col")
    x_lo, x_hi, y_a, y_b = pack_first(potential, source, labels, coil_mask)
    low, high = rings(x_lo, x_hi)
    y_a, y_b = swaps(y_a, y_b)
    c_a, c_b = swaps(*pack_corner(True, low, high))
    field, coarse, x_lo, x_hi, y_a, y_b, *material = first_iteration(
        potential, source, coil_mask, labels, (low, high, y_a, y_b, c_a, c_b),
        (floor_table, rise_table), rows * cols,
    )
    for iteration in range(1, ITERS):
        final = iteration == ITERS - 1
        low, high = rings(x_lo, x_hi)
        y_a, y_b = swaps(y_a, y_b)
        gathered = lax.all_to_all(coarse, ("row", "col"), 0, 0)
        gathered, low, high = lax.optimization_barrier((gathered, low, high))
        c_a, c_b = swaps(*pack_corner(False, low, high))
        wide = solve(gathered.reshape(rows, cols, 4, LANES))
        outs = next_iteration(
            final, wide, field, (low, high, y_a, y_b, c_a, c_b), material,
            rows if final else rows * cols,
        )
        if final:
            field, coarse, reluct = outs
        else:
            field, coarse, x_lo, x_hi, y_a, y_b = outs
    gathered = lax.all_to_all(coarse, "row", 0, 0)
    field, coarse_target = correct(gathered, field)
    return (field, reluct, coarse_target)


def solution(mesh):
    in_specs = (
        P(None, "row", "col", None),
        P(None, "row", "col", None),
        P("row", "col", None),
        P("row", "col", None),
        P(),
        P(),
    )
    out_specs = (P(None, "row", "col", None), P("row", "col", None), P(None, None, "col", None))
    return jax.shard_map(shards, mesh=mesh, in_specs=in_specs, out_specs=out_specs, check_vma=False)
```

```python
import functools
import jax
import jax.numpy as jnp
from jax import lax
from jax.experimental import pallas as pl
from jax.experimental.pallas import tpu as pltpu
from jax.sharding import PartitionSpec as P

ITERS = 3
SWEEPS = 2
COARSE_SWEEPS = 16
COARSEN = 8
RELAX = 0.8

HALO = 4
BLOCK = 16
EXT = BLOCK + 2 * HALO
LANES = 128
TOP = 8
CORE = TOP + HALO
ROWS = 40
HIGH = lax.Precision.HIGHEST
X_PAGES = 21
Y_PAGES = 88

VMEM = pl.BlockSpec(memory_space=pltpu.VMEM)
SMEM = pl.BlockSpec(memory_space=pltpu.SMEM)
PARAMS = pltpu.CompilerParams(vmem_limit_bytes=44 * 1024 * 1024)


def f32(*shape):
    return jax.ShapeDtypeStruct(shape, jnp.float32)


def turns(even, low_edge, high_edge):
    return jnp.where(even, high_edge, low_edge), jnp.where(even, low_edge, high_edge)


def corner_parts(reach):
    first = 0
    parts = []
    for distance in range(1, reach):
        parts.append((distance, first, reach - distance))
        first += reach - distance
    return parts, first


CORNER_FIELD, FIELD_ROWS = corner_parts(4)
CORNER_LABEL, LABEL_ROWS = corner_parts(3)
CORNER_DRIVE = 6 * FIELD_ROWS
CORNER_TABLE = CORNER_DRIVE + 6
CORNER_ALL = CORNER_TABLE + 2 * LABEL_ROWS
CORNER_LATER = 48
SLABS = ((0, 4, 0, 1), (4, 12, 1, 0), (12, 20, 1, 1), (20, 24, 2, 0))


def pack_first_kernel(
    potential, source, coil_mask, labels, x_lo, x_hi, y_a, y_b,
    pot_x, src_x, mask_x, lab_x, pot_y, src_y, mask_y, lab_y, sems,
):
    even = lax.axis_index("col") % 2 == 0
    copies = []

    def fetch(ref, scratch):
        copy = pltpu.make_async_copy(ref, scratch, sems.at[len(copies)])
        copy.start()
        copies.append(copy)

    for side, (cells, pair, rows) in enumerate((
        (slice(0, 4), slice(0, 2), slice(0, 8)),
        (slice(BLOCK - 4, BLOCK), slice(BLOCK - 2, BLOCK), slice(BLOCK - 8, BLOCK)),
    )):
        fetch(potential.at[:, cells], pot_x.at[side])
        fetch(source.at[:, pair], src_x.at[side])
        fetch(coil_mask.at[pair], mask_x.at[side])
        fetch(labels.at[cells], lab_x.at[side])
        fetch(potential.at[:, :, rows], pot_y.at[side])
        fetch(source.at[:, :, rows], src_y.at[side])
        fetch(coil_mask.at[:, rows], mask_y.at[side])
        fetch(labels.at[:, rows], lab_y.at[side])
    for copy in copies:
        copy.wait()
    for side, out in enumerate((x_lo, x_hi)):
        for comp in range(3):
            out[comp * 4 : comp * 4 + 4] = pot_x[side, comp]
            out[12 + comp * 2 : 14 + comp * 2] = (
                2.0 * src_x[side, comp] * mask_x[side].astype(jnp.float32)
            )
        out[18:21] = lab_x[side, side : side + 3].astype(jnp.float32)

    def send(page, low_edge, high_edge, rows=slice(0, 4)):
        first, second = turns(even, low_edge, high_edge)
        y_a[page, rows] = first
        y_b[page, rows] = second

    for x in range(BLOCK):
        mask_lo = 2.0 * mask_y[0, x, 0:2].astype(jnp.float32)
        mask_hi = 2.0 * mask_y[1, x, 6:8].astype(jnp.float32)
        for comp in range(3):
            send(comp * 16 + x, pot_y[0, comp, x, 0:4], pot_y[1, comp, x, 4:8])
            send(
                48 + comp * 8 + x // 2, src_y[0, comp, x, 0:2] * mask_lo,
                src_y[1, comp, x, 6:8] * mask_hi, slice((x % 2) * 2, (x % 2) * 2 + 2),
            )
        send(72 + x, lab_y[0, x, 0:4].astype(jnp.float32), lab_y[1, x, 4:8].astype(jnp.float32))


def pack_first(potential, source, labels, coil_mask):
    depth = potential.shape[-1]
    scratch = [
        pltpu.VMEM((2, 3, 4, BLOCK, depth), jnp.float32),
        pltpu.VMEM((2, 3, 2, BLOCK, depth), jnp.float32),
        pltpu.VMEM((2, 2, BLOCK, depth), jnp.int32),
        pltpu.VMEM((2, 4, BLOCK, depth), jnp.int32),
        pltpu.VMEM((2, 3, BLOCK, 8, depth), jnp.float32),
        pltpu.VMEM((2, 3, BLOCK, 8, depth), jnp.float32),
        pltpu.VMEM((2, BLOCK, 8, depth), jnp.int32),
        pltpu.VMEM((2, BLOCK, 8, depth), jnp.int32),
        pltpu.SemaphoreType.DMA((16,)),
    ]
    return pl.pallas_call(
        pack_first_kernel,
        in_specs=[pl.BlockSpec(memory_space=pltpu.HBM)] * 4,
        out_specs=[VMEM] * 4,
        out_shape=[f32(X_PAGES, BLOCK, depth)] * 2 + [f32(Y_PAGES, HALO, depth)] * 2,
        scratch_shapes=scratch,
        compiler_params=PARAMS,
        name="pack_first",
    )(potential, source, coil_mask, labels)


def corner_sender(low, high, out_a, out_b, even):
    def send(row, count, ref, page):
        rows = slice(row, row + count)
        first, second = turns(even, ref[page, 0:count], ref[page, BLOCK - count : BLOCK])
        out_a[rows, :] = first
        out_b[rows, :] = second

    for comp in range(3):
        for distance, first, count in CORNER_FIELD:
            row = comp * 2 * FIELD_ROWS + first
            send(row, count, low, comp * 4 + 4 - distance)
            send(row + FIELD_ROWS, count, high, comp * 4 + distance - 1)
    return send


def pack_corner_kernel(low, high, out_a, out_b):
    even = lax.axis_index("col") % 2 == 0
    send = corner_sender(low, high, out_a, out_b, even)
    for comp in range(3):
        send(CORNER_DRIVE + comp * 2, 1, low, 12 + comp * 2 + 1)
        send(CORNER_DRIVE + comp * 2 + 1, 1, high, 12 + comp * 2)
    for distance, first, count in CORNER_LABEL:
        row = CORNER_TABLE + first
        send(row, count, low, 18 + 3 - distance)
        send(row + LABEL_ROWS, count, high, 18 + distance - 1)


def pack_corner(low, high):
    depth = low.shape[-1]
    return pl.pallas_call(
        pack_corner_kernel,
        in_specs=[VMEM] * 2,
        out_specs=[VMEM] * 2,
        out_shape=[f32(CORNER_ALL, depth)] * 2,
        compiler_params=PARAMS,
        name="pack_corner",
    )(low, high)


def coarse_solve(targets, relucts):
    shape = relucts[0].shape
    count = shape[0]
    lane = lax.broadcasted_iota(jnp.int32, shape, 1)
    row = lax.broadcasted_iota(jnp.int32, shape, 0)
    z = lane % 32
    first_y = (lane // 32) % 2 == 0
    first_x = lane // 64 == 0
    up_ok, down_ok = z < 31, z > 0
    far_ok = jnp.logical_not(
        jnp.logical_or(
            jnp.logical_and(first_x, row == 0),
            jnp.logical_and(jnp.logical_not(first_x), row == count - 1),
        )
    )

    def up(v):
        return pltpu.roll(v, LANES - 1, 1)

    def down(v):
        return pltpu.roll(v, 1, 1)

    def side(v):
        return jnp.where(first_y, pltpu.roll(v, LANES - 32, 1), pltpu.roll(v, 32, 1))

    def near(v):
        return pltpu.roll(v, 64, 1)

    def far(swapped):
        return jnp.where(first_x, pltpu.roll(swapped, 1, 0), pltpu.roll(swapped, count - 1, 0))

    sets = []
    for r in relucts:
        swapped = near(r)
        c_up = r + jnp.where(up_ok, up(r), 0.0)
        c_down = r + jnp.where(down_ok, down(r), 0.0)
        c_side = r + side(r)
        c_near = r + swapped
        c_far = r + jnp.where(far_ok, far(swapped), 0.0)
        diag = ((c_up + c_down) + (c_side + r)) + (c_near + c_far)
        c_up = jnp.where(up_ok, c_up, 0.0)
        c_down = jnp.where(down_ok, c_down, 0.0)
        c_far = jnp.where(far_ok, c_far, 0.0)
        sets.append((c_up, c_down, c_side, c_near, c_far, diag, RELAX / diag))

    def neighbours(coeffs, v):
        c_up, c_down, c_side, c_near, c_far = coeffs[:5]
        swapped = near(v)
        return (
            (c_up * up(v) + c_down * down(v)) + (c_side * side(v) + c_near * swapped)
        ) + c_far * far(swapped)

    doubled = [[2.0 * t for t in stripe] for stripe in targets]
    start = [
        [coeffs[6] * t for t in stripe] for coeffs, stripe in zip(sets, doubled)
    ]

    def sweep(step, values):
        return [
            [
                (1.0 - RELAX) * v + coeffs[6] * (t + neighbours(coeffs, v))
                for v, t in zip(stripe, stripe_t)
            ]
            for coeffs, stripe, stripe_t in zip(sets, values, doubled)
        ]

    values = lax.fori_loop(0, COARSE_SWEEPS - 1, sweep, start)
    out = []
    for coeffs, stripe, stripe_t in zip(sets, values, doubled):
        total = jnp.sum(jnp.sum(coeffs[5], axis=1, keepdims=True), axis=0, keepdims=True)
        done = []
        for v, t in zip(stripe, stripe_t):
            left = t - (coeffs[5] * v - neighbours(coeffs, v))
            left = jnp.sum(jnp.sum(left, axis=1, keepdims=True), axis=0, keepdims=True)
            done.append(v + left / total)
        out.append(done)
    return out


def pick_row(values, index):
    row = lax.broadcasted_iota(jnp.int32, values.shape, 0)
    return jnp.sum(jnp.where(row == index, values, 0.0), axis=0, keepdims=True)


def block_matrix(lanes_first):
    shape = (LANES, 2 * LANES) if lanes_first else (2 * LANES, LANES)
    lane = lax.broadcasted_iota(jnp.int32, shape, 0 if lanes_first else 1)
    cell = lax.broadcasted_iota(jnp.int32, shape, 1 if lanes_first else 0)
    return jnp.where(lane == cell // COARSEN, 1.0, 0.0)


def side_matrix():
    lane = lax.broadcasted_iota(jnp.int32, (2 * LANES, LANES), 1)
    cell = lax.broadcasted_iota(jnp.int32, (2 * LANES, LANES), 0)
    end = jnp.logical_and(cell % COARSEN == COARSEN - 1, lane < 32)
    block = cell // COARSEN
    return jnp.where(
        end, jnp.where(lane == block, 1.0, jnp.where(lane == block + 1, -1.0, 0.0)), 0.0
    )


def stripe_rows(gathered):
    rows = gathered.shape[0]
    spot = lax.broadcasted_iota(jnp.int32, (rows, LANES), 0)
    out = []
    for comp in range(4):
        total = jnp.zeros((rows, LANES), jnp.float32)
        for row in range(rows):
            total = jnp.where(spot == row, gathered[row, comp : comp + 1, :], total)
        out.append(total)
    scale = 1.0 / float(COARSEN * COARSEN)
    return [out[comp] * scale for comp in range(3)], out[3]


def widen(correction, row, picked):
    picked[...] = jnp.zeros(picked.shape, jnp.float32)
    for comp in range(3):
        for shift in range(3):
            spot = comp * 3 + shift
            picked[spot : spot + 1, :] = pick_row(correction[comp], row + shift - 1)
    for group in range(1, 4):
        picked[group * 16 : group * 16 + 16, :] = pltpu.roll(
            picked[0:16, :], LANES - 32 * group, 1
        )
    return jnp.dot(
        picked[...], block_matrix(True), precision=HIGH, preferred_element_type=jnp.float32
    )


class Place:
    def __init__(self):
        self.row, self.rows = lax.axis_index("row"), lax.axis_size("row")
        self.col, self.cols = lax.axis_index("col"), lax.axis_size("col")
        self.low, self.high = self.row > 0, self.row < self.rows - 1
        self.back, self.front = self.col > 0, self.col < self.cols - 1
        self.even = self.col % 2 == 0

    def sides(self, turn_a, turn_b):
        return jnp.where(self.even, turn_b, turn_a), jnp.where(self.even, turn_a, turn_b)


def put_corner(put, message, place, row, distance, count):
    for side, there in ((0, place.low), (1, place.high)):
        back, front = place.sides(message[0](row[side], count), message[1](row[side], count))
        plane = HALO - distance if side == 0 else HALO + BLOCK - 1 + distance
        put(plane, HALO - count, count, jnp.logical_and(there, place.back), back)
        put(plane, HALO + BLOCK, count, jnp.logical_and(there, place.front), front)


def put_field(field, core, low, high, y_a, y_b, c_a, c_b, place):
    for comp in range(3):
        for half in range(2):
            z = slice(half * LANES, half * LANES + LANES)
            own = slice(CORE, CORE + BLOCK)
            field[comp, half, 4:20, own, :] = core[comp, :, :, z]
            pages = slice(comp * 4, comp * 4 + 4)
            field[comp, half, 0:4, own, :] = jnp.where(place.low, low[pages, :, z], 0.0)
            field[comp, half, 20:24, own, :] = jnp.where(place.high, high[pages, :, z], 0.0)
            pages = slice(comp * 16, comp * 16 + 16)
            back, front = place.sides(y_a[pages, :, z], y_b[pages, :, z])
            field[comp, half, 4:20, TOP : TOP + HALO, :] = jnp.where(place.back, back, 0.0)
            field[comp, half, 4:20, CORE + BLOCK : CORE + BLOCK + HALO, :] = jnp.where(
                place.front, front, 0.0
            )

            def put(plane, row, count, there, value):
                field[comp, half, plane, TOP + row : TOP + row + count, :] = jnp.where(
                    there, value, 0.0
                )

            message = [
                lambda row, count, ref=ref: ref[row : row + count, z] for ref in (c_a, c_b)
            ]
            for distance, first, count in CORNER_FIELD:
                row = comp * 2 * FIELD_ROWS + first
                put_corner(put, message, place, (row, row + FIELD_ROWS), distance, count)


def put_material(
    drive, floor, rise, source, coil_mask, labels, low, high, y_a, y_b, c_a, c_b, floor_table,
    rise_table, place,
):
    for half in range(2):
        z = slice(half * LANES, half * LANES + LANES)
        own = slice(HALO, HALO + BLOCK)
        coil = 2.0 * coil_mask[:, :, z].astype(jnp.float32)
        message = [lambda row, count, ref=ref: ref[row : row + count, z] for ref in (c_a, c_b)]
        for comp in range(3):
            drive[comp, half, 4:20, own, :] = source[comp, :, :, z] * coil
            pages = slice(12 + comp * 2, 14 + comp * 2)
            drive[comp, half, 2:4, own, :] = low[pages, :, z]
            drive[comp, half, 20:22, own, :] = high[pages, :, z]
            for x in range(BLOCK):
                page, part = 48 + comp * 8 + x // 2, slice((x % 2) * 2, (x % 2) * 2 + 2)
                back, front = place.sides(y_a[page, part, z], y_b[page, part, z])
                drive[comp, half, 4 + x, 2:4, :] = back
                drive[comp, half, 4 + x, 20:22, :] = front

            def put_drive(plane, row, count, there, value):
                drive[comp, half, plane, row : row + count, :] = value

            row = CORNER_DRIVE + comp * 2
            put_corner(put_drive, message, place, (row, row + 1), 1, 1)
        floor[half, 4:20, own, :] = labels[:, :, z].astype(jnp.float32)
        floor[half, 1:4, own, :] = jnp.where(place.low, low[18:21, :, z], -1.0)
        floor[half, 20:23, own, :] = jnp.where(place.high, high[18:21, :, z], -1.0)
        back, front = place.sides(y_a[72:88, :, z], y_b[72:88, :, z])
        floor[half, 4:20, 0:HALO, :] = jnp.where(place.back, back, -1.0)
        floor[half, 4:20, HALO + BLOCK : EXT, :] = jnp.where(place.front, front, -1.0)

        def put_label(plane, row, count, there, value):
            floor[half, plane, row : row + count, :] = jnp.where(there, value, -1.0)

        for distance, first, count in CORNER_LABEL:
            row = CORNER_TABLE + first
            put_corner(put_label, message, place, (row, row + LABEL_ROWS), distance, count)

    def look_up(x, carry):
        for half in range(2):
            label = floor[half, x]
            floor_cell = jnp.zeros_like(label)
            rise_cell = jnp.zeros_like(label)
            for number in range(floor_table.shape[0]):
                chosen = label == float(number)
                floor_cell = jnp.where(chosen, floor_table[number], floor_cell)
                rise_cell = jnp.where(chosen, rise_table[number], rise_cell)
            floor[half, x] = floor_cell
            rise[half, x] = rise_cell
        return carry

    lax.fori_loop(1, EXT - 1, look_up, 0)


def right_of(low, high, last):
    a, b = pltpu.roll(low, LANES - 1, 1), pltpu.roll(high, LANES - 1, 1)
    return jnp.where(last, b, a), b


def left_of(low, high, first):
    a, b = pltpu.roll(low, 1, 1), pltpu.roll(high, 1, 1)
    return a, jnp.where(first, a, b)


def in_pairs(begin, end, plane):
    def step(number, carry):
        x = begin + 2 * number
        for ref, value in plane(x) + plane(x + 1):
            ref[...] = value
        return carry

    lax.fori_loop(0, (end - begin) // 2, step, 0)


def fine_iteration(
    field, other, reluct, c_x, c_y, c_up, c_down, weight, sums, drive_sums, drive, floor, rise,
):
    mid = slice(TOP, TOP + EXT)
    plus = slice(TOP + 1, TOP + EXT + 1)
    minus = slice(TOP - 1, TOP + EXT - 1)
    lane = lax.broadcasted_iota(jnp.int32, (EXT, LANES), 1)
    first, last = lane == 0, lane == LANES - 1

    def reluct_plane(x):
        stores = []
        along_z = []
        for comp in range(2):
            low, high = field[comp, 0, x, mid], field[comp, 1, x, mid]
            r0, r1 = right_of(low, high, last)
            l0, l1 = left_of(low, high, first)
            along_z.append((r0 - jnp.where(first, 0.0, l0), jnp.where(last, 0.0, r1) - l1))
        for half in range(2):
            def along_y(comp):
                return field[comp, half, x, plus] - field[comp, half, x, minus]

            def along_x(comp):
                return field[comp, half, x + 1, mid] - field[comp, half, x - 1, mid]

            b0 = along_y(2) - along_z[1][half]
            b1 = along_z[0][half] - along_x(2)
            b2 = along_x(1) - along_y(0)
            square = 0.25 * (b0 * b0 + b1 * b1 + b2 * b2)
            stores.append((
                reluct.at[half, x, mid], floor[half, x] + rise[half, x] * (square / (1.0 + square))
            ))
        return stores

    in_pairs(1, EXT - 1, reluct_plane)

    def apply(src, x, rows, coeffs, first_lane, last_lane):
        rows_plus = slice(rows.start + 1, rows.stop + 1)
        rows_minus = slice(rows.start - 1, rows.stop - 1)
        out = []
        for comp in range(3):
            low, high = src[comp, 0, x, rows], src[comp, 1, x, rows]
            rights = right_of(low, high, last_lane)
            lefts = left_of(low, high, first_lane)
            for half in range(2):
                x_plus, x_minus, y_plus, y_minus, up, down = coeffs[half]
                total = (
                    (x_plus * src[comp, half, x + 1, rows] + x_minus * src[comp, half, x - 1, rows])
                    + (y_plus * src[comp, half, x, rows_plus] + y_minus * src[comp, half, x, rows_minus])
                    + (up * rights[half] + down * lefts[half])
                )
                out.append((comp, half, (low, high)[half], total))
        return out

    def load_coeffs(x, rows):
        rows_minus = slice(rows.start - 1, rows.stop - 1)
        return [
            (
                c_x[half, x, rows], c_x[half, x - 1, rows], c_y[half, x, rows],
                c_y[half, x, rows_minus], c_up[half, x, rows], c_down[half, x, rows],
            )
            for half in range(2)
        ]

    def first_plane(x):
        low, high = reluct[0, x, mid], reluct[1, x, mid]
        r0, r1 = right_of(low, high, last)
        l0, l1 = left_of(low, high, first)
        ups = (low + r0, high + jnp.where(last, 0.0, r1))
        downs = (low + jnp.where(first, 0.0, l0), high + l1)
        stores, coeffs, weights = [], [], []
        for half in range(2):
            here = (low, high)[half]
            x_plus = here + reluct[half, x + 1, mid]
            x_minus = here + reluct[half, x - 1, mid]
            y_plus = here + reluct[half, x, plus]
            y_minus = here + reluct[half, x, minus]
            total = ((x_plus + x_minus) + (y_plus + y_minus)) + (ups[half] + downs[half])
            up = ups[half] if half == 0 else jnp.where(last, 0.0, ups[half])
            down = jnp.where(first, 0.0, downs[half]) if half == 0 else downs[half]
            scale = jnp.where(floor[half, x] > 0.0, RELAX / total, 0.0)
            coeffs.append((x_plus, x_minus, y_plus, y_minus, up, down))
            weights.append(scale)
            for ref, value in (
                (c_x, x_plus), (c_y, y_plus), (c_up, up), (c_down, down), (weight, scale),
            ):
                stores.append((ref.at[half, x, mid], value))
        for comp, half, here, total in apply(field, x, mid, coeffs, first, last):
            stores.append((
                other.at[comp, half, x, mid],
                (1.0 - RELAX) * here + weights[half] * (drive[comp, half, x] + total),
            ))
        return stores

    in_pairs(2, EXT - 2, first_plane)

    def second_plane(x):
        stores = []
        weights = [weight[half, x, mid] for half in range(2)]
        for comp, half, here, total in apply(other, x, mid, load_coeffs(x, mid), first, last):
            stores.append((
                field.at[comp, half, x, mid],
                (1.0 - RELAX) * here + weights[half] * (drive[comp, half, x] + total),
            ))
        return stores

    in_pairs(3, EXT - 3, second_plane)

    own = slice(CORE, CORE + BLOCK)
    ends = pl.ds(CORE - 1, 3, stride=COARSEN)
    beyond = pl.ds(CORE, 3, stride=COARSEN)
    lane = lax.broadcasted_iota(jnp.int32, (BLOCK, LANES), 1)
    last_own = lane == LANES - 1
    lane = lax.broadcasted_iota(jnp.int32, (1, LANES), 1)
    rims = (lane == 0, lane == LANES - 1)
    zero = jnp.zeros((BLOCK, LANES), jnp.float32)
    thin = jnp.zeros((3, LANES), jnp.float32)

    def blocks(values):
        return [
            jnp.sum(values[part * COARSEN : (part + 1) * COARSEN], axis=0, keepdims=True)
            for part in range(2)
        ]

    def side(plane, comp, half):
        return blocks(
            c_x[half, plane, own]
            * (field[comp, half, plane + 1, own] - field[comp, half, plane, own])
        )

    sums[...] = jnp.zeros(sums.shape, jnp.float32)
    sides = [
        [[side(HALO - 1 + COARSEN * k, comp, half) for half in range(2)] for comp in range(3)]
        for k in range(3)
    ]
    for coarse in range(2):
        def plane(step, totals):
            x = HALO + coarse * COARSEN + step
            across, rim, along, material = totals
            relucts = [reluct[half, x, own] for half in range(2)]
            ups = [c_up[half, x, own] for half in range(2)]
            ys = [c_y[half, x, ends, :] for half in range(2)]
            across_new, rim_new, along_new = [], [], []
            for comp in range(3):
                here = [field[comp, half, x, own] for half in range(2)]
                rights = right_of(here[0], here[1], last_own)
                for half in range(2):
                    number = comp * 2 + half
                    across_new.append(across[number] + ups[half] * (rights[half] - here[half]))
                    rim_new.append(rim[number] + relucts[half] * here[half])
                    along_new.append(
                        along[number]
                        + ys[half] * (field[comp, half, x, beyond, :] - field[comp, half, x, ends, :])
                    )
            return (
                tuple(across_new), tuple(rim_new), tuple(along_new),
                tuple(material[half] + relucts[half] for half in range(2)),
            )

        across, rim, along, material = lax.fori_loop(
            0, COARSEN, plane, ((zero,) * 6, (zero,) * 6, (thin,) * 6, (zero,) * 2)
        )
        for half in range(2):
            z = slice(half * LANES, (half + 1) * LANES)
            means = blocks(material[half])
            for comp in range(3):
                number = comp * 2 + half
                rims_sum, across_sum = blocks(rim[number]), blocks(across[number])
                for part in range(2):
                    row = (coarse * 2 + part) * 8
                    y_side = along[number][part + 1 : part + 2] - along[number][part : part + 1]
                    x_side = sides[coarse + 1][comp][half][part] - sides[coarse][comp][half][part]
                    spot = row + comp
                    sums[0, spot : spot + 1, z] = 0.5 * (
                        (drive_sums[spot : spot + 1, z] + (x_side + y_side))
                        - jnp.where(rims[half], rims_sum[part], 0.0)
                    )
                    sums[1, spot : spot + 1, z] = 0.5 * across_sum[part]
            for part in range(2):
                spot = (coarse * 2 + part) * 8 + 3
                sums[0, spot : spot + 1, z] = means[part] * (1.0 / float(COARSEN ** 3))
    totals = jnp.dot(
        sums[0], block_matrix(False), precision=HIGH, preferred_element_type=jnp.float32
    ) + jnp.dot(sums[1], side_matrix(), precision=HIGH, preferred_element_type=jnp.float32)
    result = totals[0:8]
    for group in range(1, 4):
        result = result + pltpu.roll(totals[group * 8 : group * 8 + 8], 32 * group, 1)
    return result[0:4]


def sum_drive(drive, drive_sums):
    own = slice(HALO, HALO + BLOCK)
    drive_sums[...] = jnp.zeros(drive_sums.shape, jnp.float32)
    for comp in range(3):
        for half in range(2):
            for coarse in range(2):
                total = drive[comp, half, HALO + coarse * COARSEN, own]
                for x in range(HALO + coarse * COARSEN + 1, HALO + (coarse + 1) * COARSEN):
                    total = total + drive[comp, half, x, own]
                for part in range(2):
                    spot = (coarse * 2 + part) * 8 + comp
                    drive_sums[spot : spot + 1, half * LANES : (half + 1) * LANES] = jnp.sum(
                        total[part * COARSEN : (part + 1) * COARSEN], axis=0, keepdims=True
                    )


SCRATCH = (
    [pltpu.VMEM((3, 2, EXT, ROWS, LANES), jnp.float32)] * 2
    + [pltpu.VMEM((2, EXT, ROWS, LANES), jnp.float32)] * 6
    + [pltpu.VMEM((2, 32, 2 * LANES), jnp.float32)]
)


def emit(field, coarse, field_out, edges, coarse_out, place):
    own = slice(CORE, CORE + BLOCK)
    for comp in range(3):
        for half in range(2):
            z = slice(half * LANES, half * LANES + LANES)
            field_out[comp, :, :, z] = field[comp, half, 4:20, own, :]
            if edges:
                x_lo, x_hi, y_a, y_b = edges
                x_lo[comp * 4 : comp * 4 + 4, :, z] = field[comp, half, 4:8, own, :]
                x_hi[comp * 4 : comp * 4 + 4, :, z] = field[comp, half, 16:20, own, :]
                first, second = turns(
                    place.even, field[comp, half, 4:20, CORE : CORE + 4, :],
                    field[comp, half, 4:20, CORE + BLOCK - 4 : CORE + BLOCK, :],
                )
                y_a[comp * 16 : comp * 16 + 16, :, z] = first
                y_b[comp * 16 : comp * 16 + 16, :, z] = second
    coarse_out[...] = jnp.broadcast_to(coarse[None], coarse_out.shape)


def edge_shapes(depth):
    return [f32(3 * HALO, BLOCK, depth)] * 2 + [f32(3 * BLOCK, HALO, depth)] * 2


def first_kernel(
    potential, source, coil_mask, labels, low, high, y_a, y_b, c_a, c_b, floor_table, rise_table,
    field_out, coarse_out, x_lo, x_hi, yo_a, yo_b, drive_sums, drive, floor, rise, *scratch,
):
    place = Place()
    field = scratch[0]
    put_field(field, potential, low, high, y_a, y_b, c_a, c_b, place)
    put_material(
        drive, floor, rise, source, coil_mask, labels, low, high, y_a, y_b, c_a, c_b, floor_table,
        rise_table, place,
    )
    sum_drive(drive, drive_sums)
    coarse = fine_iteration(*scratch, drive_sums, drive, floor, rise)
    emit(field, coarse, field_out, (x_lo, x_hi, yo_a, yo_b), coarse_out, place)


def first_iteration(potential, source, coil_mask, labels, messages, tables, rows):
    depth = potential.shape[-1]
    return pl.pallas_call(
        first_kernel,
        in_specs=[VMEM] * 10 + [SMEM] * 2,
        out_specs=[VMEM] * 10,
        out_shape=[f32(*potential.shape), f32(rows, 4, LANES)]
        + edge_shapes(depth)
        + [f32(32, 2 * LANES), f32(3, 2, EXT, EXT, LANES), f32(2, EXT, EXT, LANES), f32(2, EXT, EXT, LANES)],
        scratch_shapes=SCRATCH,
        compiler_params=PARAMS,
        name="first_iteration",
    )(potential, source, coil_mask, labels, *messages, *tables)


def solve_kernel(gathered, low, high, wide_out, c_a, c_b, picked):
    place = Place()
    target, reluct = stripe_rows(gathered)
    correction, = coarse_solve([target], [reluct])
    wide = widen(correction, place.row, picked)
    wide_out[...] = wide
    corner_sender(low, high, c_a, c_b, place.even)
    for slab, (begin, end, shift, x) in enumerate(SLABS):
        for comp in range(3):
            low_edge, high_edge = (
                wide[spot : spot + 1] for spot in (x * 32 + 16 * y + comp * 3 + shift for y in range(2))
            )
            row = CORNER_DRIVE + slab * 3 + comp
            first, second = turns(place.even, low_edge, high_edge)
            c_a[row : row + 1, :] = first
            c_b[row : row + 1, :] = second


def solve(gathered, low, high):
    depth = low.shape[-1]
    return pl.pallas_call(
        solve_kernel,
        in_specs=[VMEM] * 3,
        out_specs=[VMEM] * 3,
        out_shape=[f32(64, depth)] + [f32(CORNER_LATER, depth)] * 2,
        scratch_shapes=[pltpu.VMEM((64, LANES), jnp.float32)],
        compiler_params=PARAMS,
        name="solve",
    )(gathered, low, high)


def next_kernel(
    final, wide, core, low, high, y_a, y_b, c_a, c_b, drive_sums, drive, floor, rise, *refs
):
    if final:
        field_out, coarse_out, reluct_out, *scratch = refs
        edges = None
    else:
        field_out, coarse_out, x_lo, x_hi, yo_a, yo_b, *scratch = refs
        edges = (x_lo, x_hi, yo_a, yo_b)
    place = Place()
    field = scratch[0]
    put_field(field, core, low, high, y_a, y_b, c_a, c_b, place)
    mid = slice(TOP, TOP + EXT)
    cell = lax.broadcasted_iota(jnp.int32, (EXT, LANES), 0)
    for slab, (begin, end, shift, x) in enumerate(SLABS):
        for comp in range(3):
            for half in range(2):
                z = slice(half * LANES, (half + 1) * LANES)
                spot = CORNER_DRIVE + slab * 3 + comp
                back, front = place.sides(c_a[spot : spot + 1, z], c_b[spot : spot + 1, z])
                back = jnp.where(place.back, back, 0.0)
                front = jnp.where(place.front, front, 0.0)
                spot = x * 32 + comp * 3 + shift
                own = [wide[spot + 16 * y : spot + 16 * y + 1, z] for y in range(2)]
                tile = jnp.where(
                    cell < 12,
                    jnp.where(cell < 4, back, own[0]),
                    jnp.where(cell < 20, own[1], front),
                )
                for plane in range(begin, end):
                    field[comp, half, plane, mid] = field[comp, half, plane, mid] + tile
    coarse = fine_iteration(*scratch, drive_sums, drive, floor, rise)
    emit(field, coarse, field_out, edges, coarse_out, place)
    if final:
        reluct = scratch[2]
        for half in range(2):
            reluct_out[:, :, half * LANES : (half + 1) * LANES] = reluct[
                half, 4:20, CORE : CORE + BLOCK, :
            ]


def next_iteration(final, wide, core, messages, material, rows):
    outs = [f32(*core.shape), f32(rows, 4, LANES)]
    outs += [f32(*core.shape[1:])] if final else edge_shapes(core.shape[-1])
    return pl.pallas_call(
        functools.partial(next_kernel, final),
        in_specs=[VMEM] * 12,
        out_specs=[VMEM] * len(outs),
        out_shape=outs,
        scratch_shapes=SCRATCH,
        compiler_params=PARAMS,
        name="last_iteration" if final else "next_iteration",
    )(wide, core, *messages, *material)


def correct_kernel(gathered, core, field_out, target_out, picked):
    row = lax.axis_index("row")
    rows = gathered.shape[0]
    target, reluct = stripe_rows(gathered)
    correction, = coarse_solve([target], [reluct])
    wide = widen(correction, row, picked)
    cell = lax.broadcasted_iota(jnp.int32, (BLOCK, 2 * LANES), 0)
    for x in range(2):
        for comp in range(3):
            spot = x * 32 + comp * 3 + 1
            tile = jnp.where(
                cell < COARSEN, wide[spot : spot + 1], wide[spot + 16 : spot + 17]
            )
            for plane in range(x * COARSEN, (x + 1) * COARSEN):
                field_out[comp, plane] = core[comp, plane] + tile
    for comp in range(3):
        for x in range(2):
            for y in range(2):
                group = x * 2 + y
                moved = target[comp] if group == 0 else pltpu.roll(target[comp], LANES - 32 * group, 1)
                for r in range(rows):
                    target_out[comp, 2 * r + x, y : y + 1, :] = moved[r : r + 1, 0:32]


def correct(gathered, core):
    rows = gathered.shape[0]
    return pl.pallas_call(
        correct_kernel,
        in_specs=[VMEM] * 2,
        out_specs=[VMEM] * 2,
        out_shape=[f32(*core.shape), f32(3, 2 * rows, 2, 32)],
        scratch_shapes=[pltpu.VMEM((64, LANES), jnp.float32)],
        compiler_params=PARAMS,
        name="correct",
    )(gathered, core)


def rings(to_low, to_high):
    count = lax.axis_size("row")
    forward = [(i, (i + 1) % count) for i in range(count)]
    backward = [(target, source) for source, target in forward]
    return lax.ppermute(to_high, "row", forward), lax.ppermute(to_low, "row", backward)


def swaps(turn_a, turn_b):
    count = lax.axis_size("col")
    pairs = []
    for begin in (0, 1):
        partner = list(range(count))
        for i in range(begin, count - 1, 2):
            partner[i], partner[i + 1] = i + 1, i
        pairs.append(list(enumerate(partner)))
    return lax.ppermute(turn_a, "col", pairs[0]), lax.ppermute(turn_b, "col", pairs[1])


def shards(potential, source, labels, coil_mask, floor_table, rise_table):
    rows = lax.axis_size("row")
    x_lo, x_hi, y_a, y_b = pack_first(
        *(pltpu.with_memory_space_constraint(v, pltpu.HBM) for v in (potential, source, labels, coil_mask))
    )
    low, high = rings(x_lo, x_hi)
    y_a, y_b = swaps(y_a, y_b)
    c_a, c_b = swaps(*pack_corner(low, high))
    field, coarse, x_lo, x_hi, y_a, y_b, *material = first_iteration(
        potential, source, coil_mask, labels, (low, high, y_a, y_b, c_a, c_b),
        (floor_table, rise_table), rows,
    )
    for iteration in range(1, ITERS):
        final = iteration == ITERS - 1
        low, high = rings(x_lo, x_hi)
        y_a, y_b = swaps(y_a, y_b)
        gathered = lax.all_to_all(coarse, "row", 0, 0)
        wide, c_a, c_b = solve(gathered, low, high)
        c_a, c_b = swaps(c_a, c_b)
        outs = next_iteration(final, wide, field, (low, high, y_a, y_b, c_a, c_b), material, rows)
        if final:
            field, coarse, reluct = outs
        else:
            field, coarse, x_lo, x_hi, y_a, y_b = outs
    gathered = lax.all_to_all(coarse, "row", 0, 0)
    field, coarse_target = correct(gathered, field)
    return (field, reluct, coarse_target)


def solution(mesh):
    in_specs = (
        P(None, "row", "col", None),
        P(None, "row", "col", None),
        P("row", "col", None),
        P("row", "col", None),
        P(),
        P(),
    )
    out_specs = (P(None, "row", "col", None), P("row", "col", None), P(None, None, "col", None))
    return jax.shard_map(shards, mesh=mesh, in_specs=in_specs, out_specs=out_specs, check_vma=False)
```

```python
import functools
import jax
import jax.numpy as jnp
from jax import lax
from jax.experimental import pallas as pl
from jax.experimental.pallas import tpu as pltpu
from jax.sharding import PartitionSpec as P

ITERS = 3
SWEEPS = 2
COARSE_SWEEPS = 16
COARSEN = 8
RELAX = 0.8

HALO = 4
BLOCK = 16
EXT = BLOCK + 2 * HALO
LANES = 128
TOP = 8
CORE = TOP + HALO
ROWS = 40
HIGH = lax.Precision.HIGHEST
X_PAGES = 21
Y_PAGES = 88

VMEM = pl.BlockSpec(memory_space=pltpu.VMEM)
SMEM = pl.BlockSpec(memory_space=pltpu.SMEM)
PARAMS = pltpu.CompilerParams(vmem_limit_bytes=44 * 1024 * 1024)


def f32(*shape):
    return jax.ShapeDtypeStruct(shape, jnp.float32)


def turns(even, low_edge, high_edge):
    return jnp.where(even, high_edge, low_edge), jnp.where(even, low_edge, high_edge)


def corner_parts(reach):
    first = 0
    parts = []
    for distance in range(1, reach):
        parts.append((distance, first, reach - distance))
        first += reach - distance
    return parts, first


CORNER_FIELD, FIELD_ROWS = corner_parts(4)
CORNER_LABEL, LABEL_ROWS = corner_parts(3)
CORNER_DRIVE = 6 * FIELD_ROWS
CORNER_TABLE = CORNER_DRIVE + 6
CORNER_ALL = CORNER_TABLE + 2 * LABEL_ROWS
CORNER_LATER = 48
SLABS = ((0, 4, 0, 1), (4, 12, 1, 0), (12, 20, 1, 1), (20, 24, 2, 0))


def pack_first_kernel(
    potential, source, coil_mask, labels, x_lo, x_hi, y_a, y_b,
    pot_x, src_x, mask_x, lab_x, pot_y, src_y, mask_y, lab_y, sems,
):
    even = lax.axis_index("col") % 2 == 0
    copies = []

    def fetch(ref, scratch):
        copy = pltpu.make_async_copy(ref, scratch, sems.at[len(copies)])
        copy.start()
        copies.append(copy)

    for side, (cells, pair, rows) in enumerate((
        (slice(0, 4), slice(0, 2), slice(0, 8)),
        (slice(BLOCK - 4, BLOCK), slice(BLOCK - 2, BLOCK), slice(BLOCK - 8, BLOCK)),
    )):
        fetch(potential.at[:, cells], pot_x.at[side])
        fetch(source.at[:, pair], src_x.at[side])
        fetch(coil_mask.at[pair], mask_x.at[side])
        fetch(labels.at[cells], lab_x.at[side])
        fetch(potential.at[:, :, rows], pot_y.at[side])
        fetch(source.at[:, :, rows], src_y.at[side])
        fetch(coil_mask.at[:, rows], mask_y.at[side])
        fetch(labels.at[:, rows], lab_y.at[side])
    for copy in copies:
        copy.wait()
    for side, out in enumerate((x_lo, x_hi)):
        for comp in range(3):
            out[comp * 4 : comp * 4 + 4] = pot_x[side, comp]
            out[12 + comp * 2 : 14 + comp * 2] = (
                2.0 * src_x[side, comp] * mask_x[side].astype(jnp.float32)
            )
        out[18:21] = lab_x[side, side : side + 3].astype(jnp.float32)

    def send(page, low_edge, high_edge, rows=slice(0, 4)):
        first, second = turns(even, low_edge, high_edge)
        y_a[page, rows] = first
        y_b[page, rows] = second

    for x in range(BLOCK):
        mask_lo = 2.0 * mask_y[0, x, 0:2].astype(jnp.float32)
        mask_hi = 2.0 * mask_y[1, x, 6:8].astype(jnp.float32)
        for comp in range(3):
            send(comp * 16 + x, pot_y[0, comp, x, 0:4], pot_y[1, comp, x, 4:8])
            send(
                48 + comp * 8 + x // 2, src_y[0, comp, x, 0:2] * mask_lo,
                src_y[1, comp, x, 6:8] * mask_hi, slice((x % 2) * 2, (x % 2) * 2 + 2),
            )
        send(72 + x, lab_y[0, x, 0:4].astype(jnp.float32), lab_y[1, x, 4:8].astype(jnp.float32))


def pack_first(potential, source, labels, coil_mask):
    depth = potential.shape[-1]
    scratch = [
        pltpu.VMEM((2, 3, 4, BLOCK, depth), jnp.float32),
        pltpu.VMEM((2, 3, 2, BLOCK, depth), jnp.float32),
        pltpu.VMEM((2, 2, BLOCK, depth), jnp.int32),
        pltpu.VMEM((2, 4, BLOCK, depth), jnp.int32),
        pltpu.VMEM((2, 3, BLOCK, 8, depth), jnp.float32),
        pltpu.VMEM((2, 3, BLOCK, 8, depth), jnp.float32),
        pltpu.VMEM((2, BLOCK, 8, depth), jnp.int32),
        pltpu.VMEM((2, BLOCK, 8, depth), jnp.int32),
        pltpu.SemaphoreType.DMA((16,)),
    ]
    return pl.pallas_call(
        pack_first_kernel,
        in_specs=[pl.BlockSpec(memory_space=pltpu.HBM)] * 4,
        out_specs=[VMEM] * 4,
        out_shape=[f32(X_PAGES, BLOCK, depth)] * 2 + [f32(Y_PAGES, HALO, depth)] * 2,
        scratch_shapes=scratch,
        compiler_params=PARAMS,
        name="pack_first",
    )(potential, source, coil_mask, labels)


def corner_sender(low, high, out_a, out_b, even):
    def send(row, count, ref, page):
        rows = slice(row, row + count)
        first, second = turns(even, ref[page, 0:count], ref[page, BLOCK - count : BLOCK])
        out_a[rows, :] = first
        out_b[rows, :] = second

    for comp in range(3):
        for distance, first, count in CORNER_FIELD:
            row = comp * 2 * FIELD_ROWS + first
            send(row, count, low, comp * 4 + 4 - distance)
            send(row + FIELD_ROWS, count, high, comp * 4 + distance - 1)
    return send


def pack_corner_kernel(low, high, out_a, out_b):
    even = lax.axis_index("col") % 2 == 0
    send = corner_sender(low, high, out_a, out_b, even)
    for comp in range(3):
        send(CORNER_DRIVE + comp * 2, 1, low, 12 + comp * 2 + 1)
        send(CORNER_DRIVE + comp * 2 + 1, 1, high, 12 + comp * 2)
    for distance, first, count in CORNER_LABEL:
        row = CORNER_TABLE + first
        send(row, count, low, 18 + 3 - distance)
        send(row + LABEL_ROWS, count, high, 18 + distance - 1)


def pack_corner(low, high):
    depth = low.shape[-1]
    return pl.pallas_call(
        pack_corner_kernel,
        in_specs=[VMEM] * 2,
        out_specs=[VMEM] * 2,
        out_shape=[f32(CORNER_ALL, depth)] * 2,
        compiler_params=PARAMS,
        name="pack_corner",
    )(low, high)


def coarse_solve(targets, relucts):
    shape = relucts[0].shape
    count = shape[0]
    lane = lax.broadcasted_iota(jnp.int32, shape, 1)
    row = lax.broadcasted_iota(jnp.int32, shape, 0)
    z = lane % 32
    first_y = (lane // 32) % 2 == 0
    first_x = lane // 64 == 0
    up_ok, down_ok = z < 31, z > 0
    far_ok = jnp.logical_not(
        jnp.logical_or(
            jnp.logical_and(first_x, row == 0),
            jnp.logical_and(jnp.logical_not(first_x), row == count - 1),
        )
    )

    def up(v):
        return pltpu.roll(v, LANES - 1, 1)

    def down(v):
        return pltpu.roll(v, 1, 1)

    def side(v):
        return jnp.where(first_y, pltpu.roll(v, LANES - 32, 1), pltpu.roll(v, 32, 1))

    def near(v):
        return pltpu.roll(v, 64, 1)

    def far(swapped, turned=False):
        below, above = pltpu.roll(swapped, 1, 0), pltpu.roll(swapped, count - 1, 0)
        return jnp.where(first_x, above, below) if turned else jnp.where(first_x, below, above)

    sets = []
    for r in relucts:
        swapped = near(r)
        c_up = r + jnp.where(up_ok, up(r), 0.0)
        c_down = r + jnp.where(down_ok, down(r), 0.0)
        c_side = r + side(r)
        c_near = r + swapped
        c_far = r + jnp.where(far_ok, far(swapped), 0.0)
        diag = ((c_up + c_down) + (c_side + r)) + (c_near + c_far)
        c_up = jnp.where(up_ok, c_up, 0.0)
        c_down = jnp.where(down_ok, c_down, 0.0)
        c_far = jnp.where(far_ok, c_far, 0.0)
        sets.append((c_up, c_down, c_side, c_near, c_far, diag, RELAX / diag))

    def neighbours(coeffs, v, swapped, turned=False):
        c_up, c_down, c_side, c_near, c_far = coeffs[:5]
        return (
            (c_up * up(v) + c_down * down(v)) + (c_side * side(v) + c_near * swapped)
        ) + c_far * far(swapped, turned)

    out = []
    for coeffs, stripe in zip(sets, targets):
        turned = [near(c) for c in coeffs]
        doubled = [2.0 * t for t in stripe]
        swapped_t = [near(t) for t in doubled]
        start = (
            tuple(coeffs[6] * t for t in doubled), tuple(turned[6] * t for t in swapped_t),
        )

        def sweep(values):
            plain, swapped = values
            return (
                tuple(
                    (1.0 - RELAX) * v + coeffs[6] * (t + neighbours(coeffs, v, s))
                    for v, s, t in zip(plain, swapped, doubled)
                ),
                tuple(
                    (1.0 - RELAX) * s + turned[6] * (t + neighbours(turned, s, v, True))
                    for v, s, t in zip(plain, swapped, swapped_t)
                ),
            )

        values = start
        for step in range(COARSE_SWEEPS - 1):
            values = sweep(values)
        plain, swapped = values
        total = jnp.sum(jnp.sum(coeffs[5], axis=1, keepdims=True), axis=0, keepdims=True)
        done = []
        for v, s, t in zip(plain, swapped, doubled):
            left = t - (coeffs[5] * v - neighbours(coeffs, v, s))
            left = jnp.sum(jnp.sum(left, axis=1, keepdims=True), axis=0, keepdims=True)
            done.append(v + left / total)
        out.append(done)
    return out


def pick_row(values, index):
    row = lax.broadcasted_iota(jnp.int32, values.shape, 0)
    return jnp.sum(jnp.where(row == index, values, 0.0), axis=0, keepdims=True)


def block_matrix(lanes_first):
    shape = (LANES, 2 * LANES) if lanes_first else (2 * LANES, LANES)
    lane = lax.broadcasted_iota(jnp.int32, shape, 0 if lanes_first else 1)
    cell = lax.broadcasted_iota(jnp.int32, shape, 1 if lanes_first else 0)
    return jnp.where(lane == cell // COARSEN, 1.0, 0.0)


def side_matrix():
    lane = lax.broadcasted_iota(jnp.int32, (2 * LANES, LANES), 1)
    cell = lax.broadcasted_iota(jnp.int32, (2 * LANES, LANES), 0)
    end = jnp.logical_and(cell % COARSEN == COARSEN - 1, lane < 32)
    block = cell // COARSEN
    return jnp.where(
        end, jnp.where(lane == block, 1.0, jnp.where(lane == block + 1, -1.0, 0.0)), 0.0
    )


def stripe_rows(gathered):
    rows = gathered.shape[0]
    spot = lax.broadcasted_iota(jnp.int32, (rows, LANES), 0)
    out = []
    for comp in range(4):
        total = jnp.zeros((rows, LANES), jnp.float32)
        for row in range(rows):
            total = jnp.where(spot == row, gathered[row, comp : comp + 1, :], total)
        out.append(total)
    scale = 1.0 / float(COARSEN * COARSEN)
    return [out[comp] * scale for comp in range(3)], out[3]


def widen(correction, row, picked):
    picked[...] = jnp.zeros(picked.shape, jnp.float32)
    for comp in range(3):
        for shift in range(3):
            spot = comp * 3 + shift
            picked[spot : spot + 1, :] = pick_row(correction[comp], row + shift - 1)
    for group in range(1, 4):
        picked[group * 16 : group * 16 + 16, :] = pltpu.roll(
            picked[0:16, :], LANES - 32 * group, 1
        )
    return jnp.dot(
        picked[...], block_matrix(True), precision=HIGH, preferred_element_type=jnp.float32
    )


class Place:
    def __init__(self):
        self.row, self.rows = lax.axis_index("row"), lax.axis_size("row")
        self.col, self.cols = lax.axis_index("col"), lax.axis_size("col")
        self.low, self.high = self.row > 0, self.row < self.rows - 1
        self.back, self.front = self.col > 0, self.col < self.cols - 1
        self.even = self.col % 2 == 0

    def sides(self, turn_a, turn_b):
        return jnp.where(self.even, turn_b, turn_a), jnp.where(self.even, turn_a, turn_b)


def put_corner(put, message, place, row, distance, count):
    for side, there in ((0, place.low), (1, place.high)):
        back, front = place.sides(message[0](row[side], count), message[1](row[side], count))
        plane = HALO - distance if side == 0 else HALO + BLOCK - 1 + distance
        put(plane, HALO - count, count, jnp.logical_and(there, place.back), back)
        put(plane, HALO + BLOCK, count, jnp.logical_and(there, place.front), front)


def put_field(field, core, low, high, y_a, y_b, c_a, c_b, place):
    for comp in range(3):
        for half in range(2):
            z = slice(half * LANES, half * LANES + LANES)
            own = slice(CORE, CORE + BLOCK)
            field[comp, half, 4:20, own, :] = core[comp, :, :, z]
            pages = slice(comp * 4, comp * 4 + 4)
            field[comp, half, 0:4, own, :] = jnp.where(place.low, low[pages, :, z], 0.0)
            field[comp, half, 20:24, own, :] = jnp.where(place.high, high[pages, :, z], 0.0)
            pages = slice(comp * 16, comp * 16 + 16)
            back, front = place.sides(y_a[pages, :, z], y_b[pages, :, z])
            field[comp, half, 4:20, TOP : TOP + HALO, :] = jnp.where(place.back, back, 0.0)
            field[comp, half, 4:20, CORE + BLOCK : CORE + BLOCK + HALO, :] = jnp.where(
                place.front, front, 0.0
            )

            def put(plane, row, count, there, value):
                field[comp, half, plane, TOP + row : TOP + row + count, :] = jnp.where(
                    there, value, 0.0
                )

            message = [
                lambda row, count, ref=ref: ref[row : row + count, z] for ref in (c_a, c_b)
            ]
            for distance, first, count in CORNER_FIELD:
                row = comp * 2 * FIELD_ROWS + first
                put_corner(put, message, place, (row, row + FIELD_ROWS), distance, count)


def put_material(
    drive, floor, rise, source, coil_mask, labels, low, high, y_a, y_b, c_a, c_b, floor_table,
    rise_table, place,
):
    for half in range(2):
        z = slice(half * LANES, half * LANES + LANES)
        own = slice(HALO, HALO + BLOCK)
        coil = 2.0 * coil_mask[:, :, z].astype(jnp.float32)
        message = [lambda row, count, ref=ref: ref[row : row + count, z] for ref in (c_a, c_b)]
        for comp in range(3):
            drive[comp, half, 4:20, own, :] = source[comp, :, :, z] * coil
            pages = slice(12 + comp * 2, 14 + comp * 2)
            drive[comp, half, 2:4, own, :] = low[pages, :, z]
            drive[comp, half, 20:22, own, :] = high[pages, :, z]
            for x in range(BLOCK):
                page, part = 48 + comp * 8 + x // 2, slice((x % 2) * 2, (x % 2) * 2 + 2)
                back, front = place.sides(y_a[page, part, z], y_b[page, part, z])
                drive[comp, half, 4 + x, 2:4, :] = back
                drive[comp, half, 4 + x, 20:22, :] = front

            def put_drive(plane, row, count, there, value):
                drive[comp, half, plane, row : row + count, :] = value

            row = CORNER_DRIVE + comp * 2
            put_corner(put_drive, message, place, (row, row + 1), 1, 1)
        floor[half, 4:20, own, :] = labels[:, :, z].astype(jnp.float32)
        floor[half, 1:4, own, :] = jnp.where(place.low, low[18:21, :, z], -1.0)
        floor[half, 20:23, own, :] = jnp.where(place.high, high[18:21, :, z], -1.0)
        back, front = place.sides(y_a[72:88, :, z], y_b[72:88, :, z])
        floor[half, 4:20, 0:HALO, :] = jnp.where(place.back, back, -1.0)
        floor[half, 4:20, HALO + BLOCK : EXT, :] = jnp.where(place.front, front, -1.0)

        def put_label(plane, row, count, there, value):
            floor[half, plane, row : row + count, :] = jnp.where(there, value, -1.0)

        for distance, first, count in CORNER_LABEL:
            row = CORNER_TABLE + first
            put_corner(put_label, message, place, (row, row + LABEL_ROWS), distance, count)

    for x in range(1, EXT - 1):
        for half in range(2):
            label = floor[half, x]
            floor_cell = jnp.zeros_like(label)
            rise_cell = jnp.zeros_like(label)
            for number in range(floor_table.shape[0]):
                chosen = label == float(number)
                floor_cell = jnp.where(chosen, floor_table[number], floor_cell)
                rise_cell = jnp.where(chosen, rise_table[number], rise_cell)
            floor[half, x] = floor_cell
            rise[half, x] = rise_cell


def right_of(low, high, last):
    a, b = pltpu.roll(low, LANES - 1, 1), pltpu.roll(high, LANES - 1, 1)
    return jnp.where(last, b, a), b


def left_of(low, high, first):
    a, b = pltpu.roll(low, 1, 1), pltpu.roll(high, 1, 1)
    return a, jnp.where(first, a, b)


def each(begin, end, plane):
    for x in range(begin, end):
        for ref, value in plane(x):
            ref[...] = value


def fine_iteration(
    field, other, reluct, c_x, c_y, c_up, c_down, weight, sums, drive_sums, drive, floor, rise,
):
    mid = slice(TOP, TOP + EXT)
    plus = slice(TOP + 1, TOP + EXT + 1)
    minus = slice(TOP - 1, TOP + EXT - 1)
    lane = lax.broadcasted_iota(jnp.int32, (EXT, LANES), 1)
    first, last = lane == 0, lane == LANES - 1

    def reluct_plane(x):
        stores = []
        along_z = []
        for comp in range(2):
            low, high = field[comp, 0, x, mid], field[comp, 1, x, mid]
            r0, r1 = right_of(low, high, last)
            l0, l1 = left_of(low, high, first)
            along_z.append((r0 - jnp.where(first, 0.0, l0), jnp.where(last, 0.0, r1) - l1))
        for half in range(2):
            def along_y(comp):
                return field[comp, half, x, plus] - field[comp, half, x, minus]

            def along_x(comp):
                return field[comp, half, x + 1, mid] - field[comp, half, x - 1, mid]

            b0 = along_y(2) - along_z[1][half]
            b1 = along_z[0][half] - along_x(2)
            b2 = along_x(1) - along_y(0)
            square = 0.25 * (b0 * b0 + b1 * b1 + b2 * b2)
            stores.append((
                reluct.at[half, x, mid], floor[half, x] + rise[half, x] * (square / (1.0 + square))
            ))
        return stores

    each(1, EXT - 1, reluct_plane)

    def apply(src, x, rows, coeffs, first_lane, last_lane):
        rows_plus = slice(rows.start + 1, rows.stop + 1)
        rows_minus = slice(rows.start - 1, rows.stop - 1)
        out = []
        for comp in range(3):
            low, high = src[comp, 0, x, rows], src[comp, 1, x, rows]
            rights = right_of(low, high, last_lane)
            lefts = left_of(low, high, first_lane)
            for half in range(2):
                x_plus, x_minus, y_plus, y_minus, up, down = coeffs[half]
                total = (
                    (x_plus * src[comp, half, x + 1, rows] + x_minus * src[comp, half, x - 1, rows])
                    + (y_plus * src[comp, half, x, rows_plus] + y_minus * src[comp, half, x, rows_minus])
                    + (up * rights[half] + down * lefts[half])
                )
                out.append((comp, half, (low, high)[half], total))
        return out

    def load_coeffs(x, rows):
        rows_minus = slice(rows.start - 1, rows.stop - 1)
        return [
            (
                c_x[half, x, rows], c_x[half, x - 1, rows], c_y[half, x, rows],
                c_y[half, x, rows_minus], c_up[half, x, rows], c_down[half, x, rows],
            )
            for half in range(2)
        ]

    def first_plane(x):
        low, high = reluct[0, x, mid], reluct[1, x, mid]
        r0, r1 = right_of(low, high, last)
        l0, l1 = left_of(low, high, first)
        ups = (low + r0, high + jnp.where(last, 0.0, r1))
        downs = (low + jnp.where(first, 0.0, l0), high + l1)
        stores, coeffs, weights = [], [], []
        for half in range(2):
            here = (low, high)[half]
            x_plus = here + reluct[half, x + 1, mid]
            x_minus = here + reluct[half, x - 1, mid]
            y_plus = here + reluct[half, x, plus]
            y_minus = here + reluct[half, x, minus]
            total = ((x_plus + x_minus) + (y_plus + y_minus)) + (ups[half] + downs[half])
            up = ups[half] if half == 0 else jnp.where(last, 0.0, ups[half])
            down = jnp.where(first, 0.0, downs[half]) if half == 0 else downs[half]
            scale = jnp.where(floor[half, x] > 0.0, RELAX / total, 0.0)
            coeffs.append((x_plus, x_minus, y_plus, y_minus, up, down))
            weights.append(scale)
            for ref, value in (
                (c_x, x_plus), (c_y, y_plus), (c_up, up), (c_down, down), (weight, scale),
            ):
                stores.append((ref.at[half, x, mid], value))
        for comp, half, here, total in apply(field, x, mid, coeffs, first, last):
            stores.append((
                other.at[comp, half, x, mid],
                (1.0 - RELAX) * here + weights[half] * (drive[comp, half, x] + total),
            ))
        return stores

    each(2, EXT - 2, first_plane)

    def second_plane(x):
        stores = []
        weights = [weight[half, x, mid] for half in range(2)]
        for comp, half, here, total in apply(other, x, mid, load_coeffs(x, mid), first, last):
            stores.append((
                field.at[comp, half, x, mid],
                (1.0 - RELAX) * here + weights[half] * (drive[comp, half, x] + total),
            ))
        return stores

    each(3, EXT - 3, second_plane)

    own = slice(CORE, CORE + BLOCK)
    ends = pl.ds(CORE - 1, 3, stride=COARSEN)
    beyond = pl.ds(CORE, 3, stride=COARSEN)
    lane = lax.broadcasted_iota(jnp.int32, (BLOCK, LANES), 1)
    last_own = lane == LANES - 1
    lane = lax.broadcasted_iota(jnp.int32, (1, LANES), 1)
    rims = (lane == 0, lane == LANES - 1)
    zero = jnp.zeros((BLOCK, LANES), jnp.float32)
    thin = jnp.zeros((3, LANES), jnp.float32)

    def blocks(values):
        return [
            jnp.sum(values[part * COARSEN : (part + 1) * COARSEN], axis=0, keepdims=True)
            for part in range(2)
        ]

    def side(plane, comp, half):
        return blocks(
            c_x[half, plane, own]
            * (field[comp, half, plane + 1, own] - field[comp, half, plane, own])
        )

    sums[...] = jnp.zeros(sums.shape, jnp.float32)
    sides = [
        [[side(HALO - 1 + COARSEN * k, comp, half) for half in range(2)] for comp in range(3)]
        for k in range(3)
    ]
    for coarse in range(2):
        def plane(x, totals):
            across, rim, along, material = totals
            relucts = [reluct[half, x, own] for half in range(2)]
            ups = [c_up[half, x, own] for half in range(2)]
            ys = [c_y[half, x, ends, :] for half in range(2)]
            across_new, rim_new, along_new = [], [], []
            for comp in range(3):
                here = [field[comp, half, x, own] for half in range(2)]
                rights = right_of(here[0], here[1], last_own)
                for half in range(2):
                    number = comp * 2 + half
                    across_new.append(across[number] + ups[half] * (rights[half] - here[half]))
                    rim_new.append(rim[number] + relucts[half] * here[half])
                    along_new.append(
                        along[number]
                        + ys[half] * (field[comp, half, x, beyond, :] - field[comp, half, x, ends, :])
                    )
            return (
                tuple(across_new), tuple(rim_new), tuple(along_new),
                tuple(material[half] + relucts[half] for half in range(2)),
            )

        totals = ((zero,) * 6, (zero,) * 6, (thin,) * 6, (zero,) * 2)
        for step in range(COARSEN):
            totals = plane(HALO + coarse * COARSEN + step, totals)
        across, rim, along, material = totals
        for half in range(2):
            z = slice(half * LANES, (half + 1) * LANES)
            means = blocks(material[half])
            for comp in range(3):
                number = comp * 2 + half
                rims_sum, across_sum = blocks(rim[number]), blocks(across[number])
                for part in range(2):
                    row = (coarse * 2 + part) * 8
                    y_side = along[number][part + 1 : part + 2] - along[number][part : part + 1]
                    x_side = sides[coarse + 1][comp][half][part] - sides[coarse][comp][half][part]
                    spot = row + comp
                    sums[0, spot : spot + 1, z] = 0.5 * (
                        (drive_sums[spot : spot + 1, z] + (x_side + y_side))
                        - jnp.where(rims[half], rims_sum[part], 0.0)
                    )
                    sums[1, spot : spot + 1, z] = 0.5 * across_sum[part]
            for part in range(2):
                spot = (coarse * 2 + part) * 8 + 3
                sums[0, spot : spot + 1, z] = means[part] * (1.0 / float(COARSEN ** 3))
    totals = jnp.dot(
        sums[0], block_matrix(False), precision=HIGH, preferred_element_type=jnp.float32
    ) + jnp.dot(sums[1], side_matrix(), precision=HIGH, preferred_element_type=jnp.float32)
    result = totals[0:8]
    for group in range(1, 4):
        result = result + pltpu.roll(totals[group * 8 : group * 8 + 8], 32 * group, 1)
    return result[0:4]


def sum_drive(drive, drive_sums):
    own = slice(HALO, HALO + BLOCK)
    drive_sums[...] = jnp.zeros(drive_sums.shape, jnp.float32)
    for comp in range(3):
        for half in range(2):
            for coarse in range(2):
                total = drive[comp, half, HALO + coarse * COARSEN, own]
                for x in range(HALO + coarse * COARSEN + 1, HALO + (coarse + 1) * COARSEN):
                    total = total + drive[comp, half, x, own]
                for part in range(2):
                    spot = (coarse * 2 + part) * 8 + comp
                    drive_sums[spot : spot + 1, half * LANES : (half + 1) * LANES] = jnp.sum(
                        total[part * COARSEN : (part + 1) * COARSEN], axis=0, keepdims=True
                    )


SCRATCH = (
    [pltpu.VMEM((3, 2, EXT, ROWS, LANES), jnp.float32)] * 2
    + [pltpu.VMEM((2, EXT, ROWS, LANES), jnp.float32)] * 6
    + [pltpu.VMEM((2, 32, 2 * LANES), jnp.float32)]
)


def emit(field, coarse, field_out, edges, coarse_out, place):
    own = slice(CORE, CORE + BLOCK)
    for comp in range(3):
        for half in range(2):
            z = slice(half * LANES, half * LANES + LANES)
            field_out[comp, :, :, z] = field[comp, half, 4:20, own, :]
            if edges:
                x_lo, x_hi, y_a, y_b = edges
                x_lo[comp * 4 : comp * 4 + 4, :, z] = field[comp, half, 4:8, own, :]
                x_hi[comp * 4 : comp * 4 + 4, :, z] = field[comp, half, 16:20, own, :]
                first, second = turns(
                    place.even, field[comp, half, 4:20, CORE : CORE + 4, :],
                    field[comp, half, 4:20, CORE + BLOCK - 4 : CORE + BLOCK, :],
                )
                y_a[comp * 16 : comp * 16 + 16, :, z] = first
                y_b[comp * 16 : comp * 16 + 16, :, z] = second
    coarse_out[...] = jnp.broadcast_to(coarse[None], coarse_out.shape)


def edge_shapes(depth):
    return [f32(3 * HALO, BLOCK, depth)] * 2 + [f32(3 * BLOCK, HALO, depth)] * 2


def first_kernel(
    potential, source, coil_mask, labels, low, high, y_a, y_b, c_a, c_b, floor_table, rise_table,
    field_out, coarse_out, x_lo, x_hi, yo_a, yo_b, drive_sums, drive, floor, rise, *scratch,
):
    place = Place()
    field = scratch[0]
    put_field(field, potential, low, high, y_a, y_b, c_a, c_b, place)
    put_material(
        drive, floor, rise, source, coil_mask, labels, low, high, y_a, y_b, c_a, c_b, floor_table,
        rise_table, place,
    )
    sum_drive(drive, drive_sums)
    coarse = fine_iteration(*scratch, drive_sums, drive, floor, rise)
    emit(field, coarse, field_out, (x_lo, x_hi, yo_a, yo_b), coarse_out, place)


def first_iteration(potential, source, coil_mask, labels, messages, tables, rows):
    depth = potential.shape[-1]
    return pl.pallas_call(
        first_kernel,
        in_specs=[VMEM] * 10 + [SMEM] * 2,
        out_specs=[VMEM] * 10,
        out_shape=[f32(*potential.shape), f32(rows, 4, LANES)]
        + edge_shapes(depth)
        + [f32(32, 2 * LANES), f32(3, 2, EXT, EXT, LANES), f32(2, EXT, EXT, LANES), f32(2, EXT, EXT, LANES)],
        scratch_shapes=SCRATCH,
        compiler_params=PARAMS,
        name="first_iteration",
    )(potential, source, coil_mask, labels, *messages, *tables)


def solve_kernel(gathered, low, high, wide_out, c_a, c_b, picked):
    place = Place()
    target, reluct = stripe_rows(gathered)
    correction, = coarse_solve([target], [reluct])
    wide = widen(correction, place.row, picked)
    wide_out[...] = wide
    corner_sender(low, high, c_a, c_b, place.even)
    for slab, (begin, end, shift, x) in enumerate(SLABS):
        for comp in range(3):
            low_edge, high_edge = (
                wide[spot : spot + 1] for spot in (x * 32 + 16 * y + comp * 3 + shift for y in range(2))
            )
            row = CORNER_DRIVE + slab * 3 + comp
            first, second = turns(place.even, low_edge, high_edge)
            c_a[row : row + 1, :] = first
            c_b[row : row + 1, :] = second


def solve(gathered, low, high):
    depth = low.shape[-1]
    return pl.pallas_call(
        solve_kernel,
        in_specs=[VMEM] * 3,
        out_specs=[VMEM] * 3,
        out_shape=[f32(64, depth)] + [f32(CORNER_LATER, depth)] * 2,
        scratch_shapes=[pltpu.VMEM((64, LANES), jnp.float32)],
        compiler_params=PARAMS,
        name="solve",
    )(gathered, low, high)


def next_kernel(
    final, wide, core, low, high, y_a, y_b, c_a, c_b, drive_sums, drive, floor, rise, *refs
):
    if final:
        field_out, coarse_out, reluct_out, *scratch = refs
        edges = None
    else:
        field_out, coarse_out, x_lo, x_hi, yo_a, yo_b, *scratch = refs
        edges = (x_lo, x_hi, yo_a, yo_b)
    place = Place()
    field = scratch[0]
    put_field(field, core, low, high, y_a, y_b, c_a, c_b, place)
    mid = slice(TOP, TOP + EXT)
    cell = lax.broadcasted_iota(jnp.int32, (EXT, LANES), 0)
    for slab, (begin, end, shift, x) in enumerate(SLABS):
        for comp in range(3):
            for half in range(2):
                z = slice(half * LANES, (half + 1) * LANES)
                spot = CORNER_DRIVE + slab * 3 + comp
                back, front = place.sides(c_a[spot : spot + 1, z], c_b[spot : spot + 1, z])
                back = jnp.where(place.back, back, 0.0)
                front = jnp.where(place.front, front, 0.0)
                spot = x * 32 + comp * 3 + shift
                own = [wide[spot + 16 * y : spot + 16 * y + 1, z] for y in range(2)]
                tile = jnp.where(
                    cell < 12,
                    jnp.where(cell < 4, back, own[0]),
                    jnp.where(cell < 20, own[1], front),
                )
                for plane in range(begin, end):
                    field[comp, half, plane, mid] = field[comp, half, plane, mid] + tile
    coarse = fine_iteration(*scratch, drive_sums, drive, floor, rise)
    emit(field, coarse, field_out, edges, coarse_out, place)
    if final:
        reluct = scratch[2]
        for half in range(2):
            reluct_out[:, :, half * LANES : (half + 1) * LANES] = reluct[
                half, 4:20, CORE : CORE + BLOCK, :
            ]


def next_iteration(final, wide, core, messages, material, rows):
    outs = [f32(*core.shape), f32(rows, 4, LANES)]
    outs += [f32(*core.shape[1:])] if final else edge_shapes(core.shape[-1])
    return pl.pallas_call(
        functools.partial(next_kernel, final),
        in_specs=[VMEM] * 12,
        out_specs=[VMEM] * len(outs),
        out_shape=outs,
        scratch_shapes=SCRATCH,
        compiler_params=PARAMS,
        name="last_iteration" if final else "next_iteration",
    )(wide, core, *messages, *material)


def correct_kernel(gathered, core, field_out, target_out, picked):
    row = lax.axis_index("row")
    rows = gathered.shape[0]
    target, reluct = stripe_rows(gathered)
    correction, = coarse_solve([target], [reluct])
    wide = widen(correction, row, picked)
    cell = lax.broadcasted_iota(jnp.int32, (BLOCK, 2 * LANES), 0)
    for x in range(2):
        for comp in range(3):
            spot = x * 32 + comp * 3 + 1
            tile = jnp.where(
                cell < COARSEN, wide[spot : spot + 1], wide[spot + 16 : spot + 17]
            )
            for plane in range(x * COARSEN, (x + 1) * COARSEN):
                field_out[comp, plane] = core[comp, plane] + tile
    for comp in range(3):
        for x in range(2):
            for y in range(2):
                group = x * 2 + y
                moved = target[comp] if group == 0 else pltpu.roll(target[comp], LANES - 32 * group, 1)
                for r in range(rows):
                    target_out[comp, 2 * r + x, y : y + 1, :] = moved[r : r + 1, 0:32]


def correct(gathered, core):
    rows = gathered.shape[0]
    return pl.pallas_call(
        correct_kernel,
        in_specs=[VMEM] * 2,
        out_specs=[VMEM] * 2,
        out_shape=[f32(*core.shape), f32(3, 2 * rows, 2, 32)],
        scratch_shapes=[pltpu.VMEM((64, LANES), jnp.float32)],
        compiler_params=PARAMS,
        name="correct",
    )(gathered, core)


def rings(to_low, to_high):
    count = lax.axis_size("row")
    forward = [(i, (i + 1) % count) for i in range(count)]
    backward = [(target, source) for source, target in forward]
    return lax.ppermute(to_high, "row", forward), lax.ppermute(to_low, "row", backward)


def swaps(turn_a, turn_b):
    count = lax.axis_size("col")
    pairs = []
    for begin in (0, 1):
        partner = list(range(count))
        for i in range(begin, count - 1, 2):
            partner[i], partner[i + 1] = i + 1, i
        pairs.append(list(enumerate(partner)))
    return lax.ppermute(turn_a, "col", pairs[0]), lax.ppermute(turn_b, "col", pairs[1])


def shards(potential, source, labels, coil_mask, floor_table, rise_table):
    rows = lax.axis_size("row")
    x_lo, x_hi, y_a, y_b = pack_first(
        *(pltpu.with_memory_space_constraint(v, pltpu.HBM) for v in (potential, source, labels, coil_mask))
    )
    low, high = rings(x_lo, x_hi)
    y_a, y_b = swaps(y_a, y_b)
    c_a, c_b = swaps(*pack_corner(low, high))
    field, coarse, x_lo, x_hi, y_a, y_b, *material = first_iteration(
        potential, source, coil_mask, labels, (low, high, y_a, y_b, c_a, c_b),
        (floor_table, rise_table), rows,
    )
    for iteration in range(1, ITERS):
        final = iteration == ITERS - 1
        low, high = rings(x_lo, x_hi)
        y_a, y_b = swaps(y_a, y_b)
        gathered = lax.all_to_all(coarse, "row", 0, 0)
        wide, c_a, c_b = solve(gathered, low, high)
        c_a, c_b = swaps(c_a, c_b)
        outs = next_iteration(final, wide, field, (low, high, y_a, y_b, c_a, c_b), material, rows)
        if final:
            field, coarse, reluct = outs
        else:
            field, coarse, x_lo, x_hi, y_a, y_b = outs
    gathered = lax.all_to_all(coarse, "row", 0, 0)
    field, coarse_target = correct(gathered, field)
    return (field, reluct, coarse_target)


def solution(mesh):
    in_specs = (
        P(None, "row", "col", None),
        P(None, "row", "col", None),
        P("row", "col", None),
        P("row", "col", None),
        P(),
        P(),
    )
    out_specs = (P(None, "row", "col", None), P("row", "col", None), P(None, None, "col", None))
    return jax.shard_map(shards, mesh=mesh, in_specs=in_specs, out_specs=out_specs, check_vma=False)
```

```python
import functools
import jax
import jax.numpy as jnp
from jax import lax
from jax.experimental import pallas as pl
from jax.experimental.pallas import tpu as pltpu
from jax.sharding import PartitionSpec as P

ITERS = 3
SWEEPS = 2
COARSE_SWEEPS = 16
COARSEN = 8
RELAX = 0.8

HALO = 4
BLOCK = 16
EXT = BLOCK + 2 * HALO
LANES = 128
TOP = 8
CORE = TOP + HALO
ROWS = 40
HIGH = lax.Precision.HIGHEST
X_PAGES = 21
Y_PAGES = 91
DEEP = (1, BLOCK - 2)

VMEM = pl.BlockSpec(memory_space=pltpu.VMEM)
SMEM = pl.BlockSpec(memory_space=pltpu.SMEM)
PARAMS = pltpu.CompilerParams(vmem_limit_bytes=44 * 1024 * 1024)


def f32(*shape):
    return jax.ShapeDtypeStruct(shape, jnp.float32)


def turns(even, low_edge, high_edge):
    return jnp.where(even, high_edge, low_edge), jnp.where(even, low_edge, high_edge)


def corner_parts(reach):
    first = 0
    parts = []
    for distance in range(1, reach):
        parts.append((distance, first, reach - distance))
        first += reach - distance
    return parts, first


CORNER_FIELD, FIELD_ROWS = corner_parts(4)
CORNER_LABEL, LABEL_ROWS = corner_parts(3)
CORNER_DRIVE = 6 * FIELD_ROWS
CORNER_TABLE = CORNER_DRIVE + 6
CORNER_ALL = CORNER_TABLE + 2 * LABEL_ROWS
SLABS = ((0, 4, 0, 1), (4, 12, 1, 0), (12, 20, 1, 1), (20, 24, 2, 0))


def pack_first_kernel(
    potential, source, coil_mask, labels, x_lo, x_hi, y_a, y_b,
    pot_x, src_x, mask_x, lab_x, pot_y, src_y, mask_y, lab_y, sems,
):
    even = lax.axis_index("col") % 2 == 0
    copies = []

    def fetch(ref, scratch):
        copy = pltpu.make_async_copy(ref, scratch, sems.at[len(copies)])
        copy.start()
        copies.append(copy)

    for side, (cells, pair, rows) in enumerate((
        (slice(0, 4), slice(0, 2), slice(0, 8)),
        (slice(BLOCK - 4, BLOCK), slice(BLOCK - 2, BLOCK), slice(BLOCK - 8, BLOCK)),
    )):
        fetch(potential.at[:, cells], pot_x.at[side])
        fetch(source.at[:, pair], src_x.at[side])
        fetch(coil_mask.at[pair], mask_x.at[side])
        fetch(labels.at[cells], lab_x.at[side])
        fetch(potential.at[:, :, rows], pot_y.at[side])
        fetch(source.at[:, :, rows], src_y.at[side])
        fetch(coil_mask.at[:, rows], mask_y.at[side])
        fetch(labels.at[:, rows], lab_y.at[side])
    for copy in copies:
        copy.wait()
    for side, out in enumerate((x_lo, x_hi)):
        for comp in range(3):
            out[comp * 4 : comp * 4 + 4] = pot_x[side, comp]
            out[12 + comp * 2 : 14 + comp * 2] = (
                2.0 * src_x[side, comp] * mask_x[side].astype(jnp.float32)
            )
        out[18:21] = lab_x[side, side : side + 3].astype(jnp.float32)

    def send(page, low_edge, high_edge, rows=slice(0, 4)):
        first, second = turns(even, low_edge, high_edge)
        y_a[page, rows] = first
        y_b[page, rows] = second

    for x in range(BLOCK):
        mask_lo = 2.0 * mask_y[0, x, 0:2].astype(jnp.float32)
        mask_hi = 2.0 * mask_y[1, x, 6:8].astype(jnp.float32)
        for comp in range(3):
            send(comp * 16 + x, pot_y[0, comp, x, 0:4], pot_y[1, comp, x, 4:8])
            send(
                48 + comp * 8 + x // 2, src_y[0, comp, x, 0:2] * mask_lo,
                src_y[1, comp, x, 6:8] * mask_hi, slice((x % 2) * 2, (x % 2) * 2 + 2),
            )
        send(72 + x, lab_y[0, x, 0:4].astype(jnp.float32), lab_y[1, x, 4:8].astype(jnp.float32))
    for number, x in enumerate(DEEP):
        mask_lo = 2.0 * mask_y[0, x, 2:3].astype(jnp.float32)
        mask_hi = 2.0 * mask_y[1, x, 5:6].astype(jnp.float32)
        for comp in range(3):
            send(
                88 + comp, pot_y[0, comp, x, 4:5], pot_y[1, comp, x, 3:4],
                slice(number, number + 1),
            )
            send(
                88 + comp, src_y[0, comp, x, 2:3] * mask_lo, src_y[1, comp, x, 5:6] * mask_hi,
                slice(2 + number, 3 + number),
            )


def pack_first(potential, source, labels, coil_mask):
    depth = potential.shape[-1]
    scratch = [
        pltpu.VMEM((2, 3, 4, BLOCK, depth), jnp.float32),
        pltpu.VMEM((2, 3, 2, BLOCK, depth), jnp.float32),
        pltpu.VMEM((2, 2, BLOCK, depth), jnp.int32),
        pltpu.VMEM((2, 4, BLOCK, depth), jnp.int32),
        pltpu.VMEM((2, 3, BLOCK, 8, depth), jnp.float32),
        pltpu.VMEM((2, 3, BLOCK, 8, depth), jnp.float32),
        pltpu.VMEM((2, BLOCK, 8, depth), jnp.int32),
        pltpu.VMEM((2, BLOCK, 8, depth), jnp.int32),
        pltpu.SemaphoreType.DMA((16,)),
    ]
    return pl.pallas_call(
        pack_first_kernel,
        in_specs=[pl.BlockSpec(memory_space=pltpu.HBM)] * 4,
        out_specs=[VMEM] * 4,
        out_shape=[f32(X_PAGES, BLOCK, depth)] * 2 + [f32(Y_PAGES, HALO, depth)] * 2,
        scratch_shapes=scratch,
        compiler_params=PARAMS,
        name="pack_first",
    )(potential, source, coil_mask, labels)


def pack_corner_kernel(low, high, out_a, out_b):
    even = lax.axis_index("col") % 2 == 0

    def send(row, count, ref, page):
        rows = slice(row, row + count)
        first, second = turns(even, ref[page, 0:count], ref[page, BLOCK - count : BLOCK])
        out_a[rows, :] = first
        out_b[rows, :] = second

    for comp in range(3):
        for distance, first, count in CORNER_FIELD:
            row = comp * 2 * FIELD_ROWS + first
            send(row, count, low, comp * 4 + 4 - distance)
            send(row + FIELD_ROWS, count, high, comp * 4 + distance - 1)
    for comp in range(3):
        send(CORNER_DRIVE + comp * 2, 1, low, 12 + comp * 2 + 1)
        send(CORNER_DRIVE + comp * 2 + 1, 1, high, 12 + comp * 2)
    for distance, first, count in CORNER_LABEL:
        row = CORNER_TABLE + first
        send(row, count, low, 18 + 3 - distance)
        send(row + LABEL_ROWS, count, high, 18 + distance - 1)


def pack_corner(low, high):
    depth = low.shape[-1]
    return pl.pallas_call(
        pack_corner_kernel,
        in_specs=[VMEM] * 2,
        out_specs=[VMEM] * 2,
        out_shape=[f32(CORNER_ALL, depth)] * 2,
        compiler_params=PARAMS,
        name="pack_corner",
    )(low, high)


def coarse_solve(targets, relucts):
    shape = relucts[0].shape
    count = shape[0]
    lane = lax.broadcasted_iota(jnp.int32, shape, 1)
    row = lax.broadcasted_iota(jnp.int32, shape, 0)
    z = lane % 32
    first_y = (lane // 32) % 2 == 0
    first_x = lane // 64 == 0
    up_ok, down_ok = z < 31, z > 0
    far_ok = jnp.logical_not(
        jnp.logical_or(
            jnp.logical_and(first_x, row == 0),
            jnp.logical_and(jnp.logical_not(first_x), row == count - 1),
        )
    )

    def up(v):
        return pltpu.roll(v, LANES - 1, 1)

    def down(v):
        return pltpu.roll(v, 1, 1)

    def side(v):
        return jnp.where(first_y, pltpu.roll(v, LANES - 32, 1), pltpu.roll(v, 32, 1))

    def near(v):
        return pltpu.roll(v, 64, 1)

    def far(swapped, turned=False):
        below, above = pltpu.roll(swapped, 1, 0), pltpu.roll(swapped, count - 1, 0)
        return jnp.where(first_x, above, below) if turned else jnp.where(first_x, below, above)

    sets = []
    for r in relucts:
        swapped = near(r)
        c_up = r + jnp.where(up_ok, up(r), 0.0)
        c_down = r + jnp.where(down_ok, down(r), 0.0)
        c_side = r + side(r)
        c_near = r + swapped
        c_far = r + jnp.where(far_ok, far(swapped), 0.0)
        diag = ((c_up + c_down) + (c_side + r)) + (c_near + c_far)
        c_up = jnp.where(up_ok, c_up, 0.0)
        c_down = jnp.where(down_ok, c_down, 0.0)
        c_far = jnp.where(far_ok, c_far, 0.0)
        sets.append((c_up, c_down, c_side, c_near, c_far, diag, RELAX / diag))

    def neighbours(coeffs, v, swapped, turned=False):
        c_up, c_down, c_side, c_near, c_far = coeffs[:5]
        return (
            (c_up * up(v) + c_down * down(v)) + (c_side * side(v) + c_near * swapped)
        ) + c_far * far(swapped, turned)

    turned_sets = [[near(c) for c in coeffs] for coeffs in sets]
    doubled = [[2.0 * t for t in stripe] for stripe in targets]
    swapped_t = [[near(t) for t in stripe] for stripe in doubled]
    plain = [[coeffs[6] * t for t in stripe] for coeffs, stripe in zip(sets, doubled)]
    swapped = [[coeffs[6] * t for t in stripe] for coeffs, stripe in zip(turned_sets, swapped_t)]
    for step in range(COARSE_SWEEPS - 1):
        plain, swapped = [
            [
                (1.0 - RELAX) * v + coeffs[6] * (t + neighbours(coeffs, v, s))
                for v, s, t in zip(*stripe)
            ]
            for coeffs, stripe in zip(sets, zip(plain, swapped, doubled))
        ], [
            [
                (1.0 - RELAX) * s + coeffs[6] * (t + neighbours(coeffs, s, v, True))
                for v, s, t in zip(*stripe)
            ]
            for coeffs, stripe in zip(turned_sets, zip(plain, swapped, swapped_t))
        ]
    out = []
    for coeffs, *stripe in zip(sets, plain, swapped, doubled):
        total = jnp.sum(jnp.sum(coeffs[5], axis=1, keepdims=True), axis=0, keepdims=True)
        done = []
        for v, s, t in zip(*stripe):
            left = t - (coeffs[5] * v - neighbours(coeffs, v, s))
            left = jnp.sum(jnp.sum(left, axis=1, keepdims=True), axis=0, keepdims=True)
            done.append(v + left / total)
        out.append(done)
    return out


def pick_row(values, index):
    row = lax.broadcasted_iota(jnp.int32, values.shape, 0)
    return jnp.sum(jnp.where(row == index, values, 0.0), axis=0, keepdims=True)


def block_matrix(lanes_first):
    shape = (LANES, 2 * LANES) if lanes_first else (2 * LANES, LANES)
    lane = lax.broadcasted_iota(jnp.int32, shape, 0 if lanes_first else 1)
    cell = lax.broadcasted_iota(jnp.int32, shape, 1 if lanes_first else 0)
    return jnp.where(lane == cell // COARSEN, 1.0, 0.0)


def side_matrix():
    lane = lax.broadcasted_iota(jnp.int32, (2 * LANES, LANES), 1)
    cell = lax.broadcasted_iota(jnp.int32, (2 * LANES, LANES), 0)
    end = jnp.logical_and(cell % COARSEN == COARSEN - 1, lane < 32)
    block = cell // COARSEN
    return jnp.where(
        end, jnp.where(lane == block, 1.0, jnp.where(lane == block + 1, -1.0, 0.0)), 0.0
    )


def stripe_rows(rows, block):
    spot = lax.broadcasted_iota(jnp.int32, (rows, LANES), 0)
    out = []
    for comp in range(4):
        total = jnp.zeros((rows, LANES), jnp.float32)
        for row in range(rows):
            total = jnp.where(spot == row, block(row, slice(comp, comp + 1)), total)
        out.append(total)
    scale = 1.0 / float(COARSEN * COARSEN)
    return [out[comp] * scale for comp in range(3)], out[3]


def widen(corrections, slots, row, picked):
    lines = []
    for correction in corrections:
        picked[0:16, :] = jnp.zeros((16, LANES), jnp.float32)
        for comp in range(3):
            for shift in range(3):
                spot = comp * 3 + shift
                picked[spot : spot + 1, :] = pick_row(correction[comp], row + shift - 1)
        lines.append(picked[0:16, :])
    for number, (stripe, y) in enumerate(slots):
        for x in range(2):
            group = x * 2 + y
            spot = (2 * number + x) * 16
            picked[spot : spot + 16, :] = (
                lines[stripe] if group == 0 else pltpu.roll(lines[stripe], LANES - 32 * group, 1)
            )
    return jnp.dot(
        picked[...], block_matrix(True), precision=HIGH, preferred_element_type=jnp.float32
    )


class Place:
    def __init__(self):
        self.row, self.rows = lax.axis_index("row"), lax.axis_size("row")
        self.col, self.cols = lax.axis_index("col"), lax.axis_size("col")
        self.low, self.high = self.row > 0, self.row < self.rows - 1
        self.back, self.front = self.col > 0, self.col < self.cols - 1
        self.even = self.col % 2 == 0

    def sides(self, turn_a, turn_b):
        return jnp.where(self.even, turn_b, turn_a), jnp.where(self.even, turn_a, turn_b)


def put_corner(put, message, place, row, distance, count):
    for side, there in ((0, place.low), (1, place.high)):
        back, front = place.sides(message[0](row[side], count), message[1](row[side], count))
        plane = HALO - distance if side == 0 else HALO + BLOCK - 1 + distance
        put(plane, HALO - count, count, jnp.logical_and(there, place.back), back)
        put(plane, HALO + BLOCK, count, jnp.logical_and(there, place.front), front)


def put_field(field, core, low, high, y_a, y_b, deep, place, corners):
    for comp in range(3):
        for half in range(2):
            z = slice(half * LANES, half * LANES + LANES)
            own = slice(CORE, CORE + BLOCK)
            field[comp, half, 4:20, own, :] = core[comp, :, :, z]
            pages = slice(comp * 4, comp * 4 + 4)
            field[comp, half, 0:4, own, :] = jnp.where(place.low, low[pages, :, z], 0.0)
            field[comp, half, 20:24, own, :] = jnp.where(place.high, high[pages, :, z], 0.0)
            pages = slice(comp * 16, comp * 16 + 16)
            back, front = place.sides(y_a[pages, :, z], y_b[pages, :, z])
            field[comp, half, 4:20, TOP : TOP + HALO, :] = jnp.where(place.back, back, 0.0)
            field[comp, half, 4:20, CORE + BLOCK : CORE + BLOCK + HALO, :] = jnp.where(
                place.front, front, 0.0
            )

            def put(plane, row, count, there, value):
                field[comp, half, plane, TOP + row : TOP + row + count, :] = jnp.where(
                    there, value, 0.0
                )

            for number, x in enumerate(DEEP):
                rows = slice(number, number + 1)
                back, front = place.sides(y_a[deep + comp, rows, z], y_b[deep + comp, rows, z])
                put(HALO + x, -1, 1, place.back, back)
                put(HALO + x, EXT, 1, place.front, front)
            corners(put, comp, z)


def first_corners(c_a, c_b, place):
    def corners(put, comp, z):
        message = [lambda row, count, ref=ref: ref[row : row + count, z] for ref in (c_a, c_b)]
        for distance, first, count in CORNER_FIELD:
            row = comp * 2 * FIELD_ROWS + first
            put_corner(put, message, place, (row, row + FIELD_ROWS), distance, count)

    return corners


ROW_CORNERS = ((1, 1), (2, 1), (3, 1), (2, 2))
X_EDGE = 3 * HALO + 2
Y_EDGE = 3 * BLOCK + 6


def later_corners(low, high, y_a, y_b, place):
    def corners(put, comp, z):
        both = jnp.logical_and
        for ref, there, sign in ((low, place.low, -1), (high, place.high, 1)):
            for number, (along_x, along_y) in enumerate(ROW_CORNERS):
                plane = HALO - along_x if sign < 0 else HALO + BLOCK - 1 + along_x
                for end, side in enumerate((place.back, place.front)):
                    spot = comp * 8 + end * 4 + number
                    row = HALO - along_y if end == 0 else HALO + BLOCK - 1 + along_y
                    value = ref[12 + spot // 16, spot % 16 : spot % 16 + 1, z]
                    put(plane, row, 1, both(there, side), value)
        page = 3 * BLOCK + comp
        for number in range(4):
            along_y = 2 + number % 2
            plane, there = ((HALO - 1, place.low), (HALO + BLOCK, place.high))[number // 2]
            rows = slice(number, number + 1)
            back, front = place.sides(y_a[page, rows, z], y_b[page, rows, z])
            put(plane, HALO - along_y, 1, both(there, place.back), back)
            put(plane, HALO + BLOCK - 1 + along_y, 1, both(there, place.front), front)

    return corners


def put_material(
    drive, floor, rise, source, coil_mask, labels, low, high, y_a, y_b, c_a, c_b, floor_table,
    rise_table, place,
):
    for half in range(2):
        z = slice(half * LANES, half * LANES + LANES)
        own = slice(HALO, HALO + BLOCK)
        coil = 2.0 * coil_mask[:, :, z].astype(jnp.float32)
        message = [lambda row, count, ref=ref: ref[row : row + count, z] for ref in (c_a, c_b)]
        for comp in range(3):
            drive[comp, half, 4:20, own, :] = source[comp, :, :, z] * coil
            pages = slice(12 + comp * 2, 14 + comp * 2)
            drive[comp, half, 2:4, own, :] = low[pages, :, z]
            drive[comp, half, 20:22, own, :] = high[pages, :, z]
            for x in range(BLOCK):
                page, part = 48 + comp * 8 + x // 2, slice((x % 2) * 2, (x % 2) * 2 + 2)
                back, front = place.sides(y_a[page, part, z], y_b[page, part, z])
                drive[comp, half, 4 + x, 2:4, :] = back
                drive[comp, half, 4 + x, 20:22, :] = front

            def put_drive(plane, row, count, there, value):
                drive[comp, half, plane, row : row + count, :] = value

            row = CORNER_DRIVE + comp * 2
            put_corner(put_drive, message, place, (row, row + 1), 1, 1)
            for number, x in enumerate(DEEP):
                rows = slice(2 + number, 3 + number)
                back, front = place.sides(y_a[88 + comp, rows, z], y_b[88 + comp, rows, z])
                put_drive(HALO + x, 1, 1, None, back)
                put_drive(HALO + x, HALO + BLOCK + 2, 1, None, front)
        floor[half, 4:20, own, :] = labels[:, :, z].astype(jnp.float32)
        floor[half, 1:4, own, :] = jnp.where(place.low, low[18:21, :, z], -1.0)
        floor[half, 20:23, own, :] = jnp.where(place.high, high[18:21, :, z], -1.0)
        back, front = place.sides(y_a[72:88, :, z], y_b[72:88, :, z])
        floor[half, 4:20, 0:HALO, :] = jnp.where(place.back, back, -1.0)
        floor[half, 4:20, HALO + BLOCK : EXT, :] = jnp.where(place.front, front, -1.0)

        def put_label(plane, row, count, there, value):
            floor[half, plane, row : row + count, :] = jnp.where(there, value, -1.0)

        for distance, first, count in CORNER_LABEL:
            row = CORNER_TABLE + first
            put_corner(put_label, message, place, (row, row + LABEL_ROWS), distance, count)

    for x in range(1, EXT - 1):
        for half in range(2):
            label = floor[half, x]
            floor_cell = jnp.zeros_like(label)
            rise_cell = jnp.zeros_like(label)
            for number in range(floor_table.shape[0]):
                chosen = label == float(number)
                floor_cell = jnp.where(chosen, floor_table[number], floor_cell)
                rise_cell = jnp.where(chosen, rise_table[number], rise_cell)
            floor[half, x] = floor_cell
            rise[half, x] = rise_cell


def right_of(low, high, last):
    a, b = pltpu.roll(low, LANES - 1, 1), pltpu.roll(high, LANES - 1, 1)
    return jnp.where(last, b, a), b


def left_of(low, high, first):
    a, b = pltpu.roll(low, 1, 1), pltpu.roll(high, 1, 1)
    return a, jnp.where(first, a, b)


def each(begin, end, plane):
    for x in range(begin, end):
        for ref, value in plane(x):
            ref[...] = value


def fine_iteration(
    field, other, reluct, c_x, c_y, c_up, c_down, weight, sums, drive_sums, drive, floor, rise,
):
    mid = slice(TOP, TOP + EXT)
    plus = slice(TOP + 1, TOP + EXT + 1)
    minus = slice(TOP - 1, TOP + EXT - 1)
    lane = lax.broadcasted_iota(jnp.int32, (EXT, LANES), 1)
    first, last = lane == 0, lane == LANES - 1

    def reluct_plane(x):
        stores = []
        along_z = []
        for comp in range(2):
            low, high = field[comp, 0, x, mid], field[comp, 1, x, mid]
            r0, r1 = right_of(low, high, last)
            l0, l1 = left_of(low, high, first)
            along_z.append((r0 - jnp.where(first, 0.0, l0), jnp.where(last, 0.0, r1) - l1))
        for half in range(2):
            def along_y(comp):
                return field[comp, half, x, plus] - field[comp, half, x, minus]

            def along_x(comp):
                return field[comp, half, x + 1, mid] - field[comp, half, x - 1, mid]

            b0 = along_y(2) - along_z[1][half]
            b1 = along_z[0][half] - along_x(2)
            b2 = along_x(1) - along_y(0)
            square = 0.25 * (b0 * b0 + b1 * b1 + b2 * b2)
            stores.append((
                reluct.at[half, x, mid], floor[half, x] + rise[half, x] * (square / (1.0 + square))
            ))
        return stores

    each(1, EXT - 1, reluct_plane)

    def apply(src, x, rows, coeffs, first_lane, last_lane):
        rows_plus = slice(rows.start + 1, rows.stop + 1)
        rows_minus = slice(rows.start - 1, rows.stop - 1)
        out = []
        for comp in range(3):
            low, high = src[comp, 0, x, rows], src[comp, 1, x, rows]
            rights = right_of(low, high, last_lane)
            lefts = left_of(low, high, first_lane)
            for half in range(2):
                x_plus, x_minus, y_plus, y_minus, up, down = coeffs[half]
                total = (
                    (x_plus * src[comp, half, x + 1, rows] + x_minus * src[comp, half, x - 1, rows])
                    + (y_plus * src[comp, half, x, rows_plus] + y_minus * src[comp, half, x, rows_minus])
                    + (up * rights[half] + down * lefts[half])
                )
                out.append((comp, half, (low, high)[half], total))
        return out

    def load_coeffs(x, rows):
        rows_minus = slice(rows.start - 1, rows.stop - 1)
        return [
            (
                c_x[half, x, rows], c_x[half, x - 1, rows], c_y[half, x, rows],
                c_y[half, x, rows_minus], c_up[half, x, rows], c_down[half, x, rows],
            )
            for half in range(2)
        ]

    def first_plane(x):
        low, high = reluct[0, x, mid], reluct[1, x, mid]
        r0, r1 = right_of(low, high, last)
        l0, l1 = left_of(low, high, first)
        ups = (low + r0, high + jnp.where(last, 0.0, r1))
        downs = (low + jnp.where(first, 0.0, l0), high + l1)
        stores, coeffs, weights = [], [], []
        for half in range(2):
            here = (low, high)[half]
            x_plus = here + reluct[half, x + 1, mid]
            x_minus = here + reluct[half, x - 1, mid]
            y_plus = here + reluct[half, x, plus]
            y_minus = here + reluct[half, x, minus]
            total = ((x_plus + x_minus) + (y_plus + y_minus)) + (ups[half] + downs[half])
            up = ups[half] if half == 0 else jnp.where(last, 0.0, ups[half])
            down = jnp.where(first, 0.0, downs[half]) if half == 0 else downs[half]
            scale = jnp.where(floor[half, x] > 0.0, RELAX / total, 0.0)
            coeffs.append((x_plus, x_minus, y_plus, y_minus, up, down))
            weights.append(scale)
            for ref, value in (
                (c_x, x_plus), (c_y, y_plus), (c_up, up), (c_down, down), (weight, scale),
            ):
                stores.append((ref.at[half, x, mid], value))
        for comp, half, here, total in apply(field, x, mid, coeffs, first, last):
            stores.append((
                other.at[comp, half, x, mid],
                (1.0 - RELAX) * here + weights[half] * (drive[comp, half, x] + total),
            ))
        return stores

    each(2, EXT - 2, first_plane)

    def second_plane(x):
        stores = []
        weights = [weight[half, x, mid] for half in range(2)]
        for comp, half, here, total in apply(other, x, mid, load_coeffs(x, mid), first, last):
            stores.append((
                field.at[comp, half, x, mid],
                (1.0 - RELAX) * here + weights[half] * (drive[comp, half, x] + total),
            ))
        return stores

    each(3, EXT - 3, second_plane)

    own = slice(CORE, CORE + BLOCK)
    ends = pl.ds(CORE - 1, 3, stride=COARSEN)
    beyond = pl.ds(CORE, 3, stride=COARSEN)
    lane = lax.broadcasted_iota(jnp.int32, (BLOCK, LANES), 1)
    last_own = lane == LANES - 1
    lane = lax.broadcasted_iota(jnp.int32, (1, LANES), 1)
    rims = (lane == 0, lane == LANES - 1)
    zero = jnp.zeros((BLOCK, LANES), jnp.float32)
    thin = jnp.zeros((3, LANES), jnp.float32)

    def blocks(values):
        return [
            jnp.sum(values[part * COARSEN : (part + 1) * COARSEN], axis=0, keepdims=True)
            for part in range(2)
        ]

    def side(plane, comp, half):
        return blocks(
            c_x[half, plane, own]
            * (field[comp, half, plane + 1, own] - field[comp, half, plane, own])
        )

    sums[...] = jnp.zeros(sums.shape, jnp.float32)
    sides = [
        [[side(HALO - 1 + COARSEN * k, comp, half) for half in range(2)] for comp in range(3)]
        for k in range(3)
    ]
    for coarse in range(2):
        def plane(x, totals):
            across, rim, along, material = totals
            relucts = [reluct[half, x, own] for half in range(2)]
            ups = [c_up[half, x, own] for half in range(2)]
            ys = [c_y[half, x, ends, :] for half in range(2)]
            across_new, rim_new, along_new = [], [], []
            for comp in range(3):
                here = [field[comp, half, x, own] for half in range(2)]
                rights = right_of(here[0], here[1], last_own)
                for half in range(2):
                    number = comp * 2 + half
                    across_new.append(across[number] + ups[half] * (rights[half] - here[half]))
                    rim_new.append(rim[number] + relucts[half] * here[half])
                    along_new.append(
                        along[number]
                        + ys[half] * (field[comp, half, x, beyond, :] - field[comp, half, x, ends, :])
                    )
            return (
                tuple(across_new), tuple(rim_new), tuple(along_new),
                tuple(material[half] + relucts[half] for half in range(2)),
            )

        totals = ((zero,) * 6, (zero,) * 6, (thin,) * 6, (zero,) * 2)
        for step in range(COARSEN):
            totals = plane(HALO + coarse * COARSEN + step, totals)
        across, rim, along, material = totals
        for half in range(2):
            z = slice(half * LANES, (half + 1) * LANES)
            means = blocks(material[half])
            for comp in range(3):
                number = comp * 2 + half
                rims_sum, across_sum = blocks(rim[number]), blocks(across[number])
                for part in range(2):
                    row = (coarse * 2 + part) * 8
                    y_side = along[number][part + 1 : part + 2] - along[number][part : part + 1]
                    x_side = sides[coarse + 1][comp][half][part] - sides[coarse][comp][half][part]
                    spot = row + comp
                    sums[0, spot : spot + 1, z] = 0.5 * (
                        (drive_sums[spot : spot + 1, z] + (x_side + y_side))
                        - jnp.where(rims[half], rims_sum[part], 0.0)
                    )
                    sums[1, spot : spot + 1, z] = 0.5 * across_sum[part]
            for part in range(2):
                spot = (coarse * 2 + part) * 8 + 3
                sums[0, spot : spot + 1, z] = means[part] * (1.0 / float(COARSEN ** 3))
    totals = jnp.dot(
        sums[0], block_matrix(False), precision=HIGH, preferred_element_type=jnp.float32
    ) + jnp.dot(sums[1], side_matrix(), precision=HIGH, preferred_element_type=jnp.float32)
    result = totals[0:8]
    for group in range(1, 4):
        result = result + pltpu.roll(totals[group * 8 : group * 8 + 8], 32 * group, 1)
    return result[0:4]


def sum_drive(drive, drive_sums):
    own = slice(HALO, HALO + BLOCK)
    drive_sums[...] = jnp.zeros(drive_sums.shape, jnp.float32)
    for comp in range(3):
        for half in range(2):
            for coarse in range(2):
                total = drive[comp, half, HALO + coarse * COARSEN, own]
                for x in range(HALO + coarse * COARSEN + 1, HALO + (coarse + 1) * COARSEN):
                    total = total + drive[comp, half, x, own]
                for part in range(2):
                    spot = (coarse * 2 + part) * 8 + comp
                    drive_sums[spot : spot + 1, half * LANES : (half + 1) * LANES] = jnp.sum(
                        total[part * COARSEN : (part + 1) * COARSEN], axis=0, keepdims=True
                    )


SCRATCH = (
    [pltpu.VMEM((3, 2, EXT, ROWS, LANES), jnp.float32)] * 2
    + [pltpu.VMEM((2, EXT, ROWS, LANES), jnp.float32)] * 6
    + [pltpu.VMEM((2, 32, 2 * LANES), jnp.float32)]
)


def emit(field, coarse, field_out, edges, coarse_out, place):
    own = slice(CORE, CORE + BLOCK)
    for comp in range(3):
        for half in range(2):
            z = slice(half * LANES, half * LANES + LANES)
            field_out[comp, :, :, z] = field[comp, half, 4:20, own, :]
            if edges:
                x_lo, x_hi, y_a, y_b = edges
                x_lo[comp * 4 : comp * 4 + 4, :, z] = field[comp, half, 4:8, own, :]
                x_hi[comp * 4 : comp * 4 + 4, :, z] = field[comp, half, 16:20, own, :]
                first, second = turns(
                    place.even, field[comp, half, 4:20, CORE : CORE + 4, :],
                    field[comp, half, 4:20, CORE + BLOCK - 4 : CORE + BLOCK, :],
                )
                y_a[comp * 16 : comp * 16 + 16, :, z] = first
                y_b[comp * 16 : comp * 16 + 16, :, z] = second

                def cell(x, y):
                    return field[comp, half, HALO + x, CORE + y : CORE + y + 1, :]

                def send(page, row, x, low_y, high_y):
                    first, second = turns(place.even, cell(x, low_y), cell(x, high_y))
                    y_a[page, row : row + 1, z] = first
                    y_b[page, row : row + 1, z] = second

                for number, (along_x, along_y) in enumerate(ROW_CORNERS):
                    for end, y in enumerate((-along_y, BLOCK - 1 + along_y)):
                        spot = comp * 8 + end * 4 + number
                        rows = slice(spot % 16, spot % 16 + 1)
                        x_lo[12 + spot // 16, rows, z] = cell(along_x - 1, y)
                        x_hi[12 + spot // 16, rows, z] = cell(BLOCK - along_x, y)
                for number in range(4):
                    along_y = 2 + number % 2
                    send(
                        3 * BLOCK + comp, number, (-1, BLOCK)[number // 2], along_y - 1,
                        BLOCK - along_y,
                    )
                for number, x in enumerate(DEEP):
                    send(3 * BLOCK + 3 + comp, number, x, HALO, BLOCK - 1 - HALO)
    coarse_out[...] = jnp.broadcast_to(coarse[None], coarse_out.shape)


def edge_shapes(depth):
    return [f32(X_EDGE, BLOCK, depth)] * 2 + [f32(Y_EDGE, HALO, depth)] * 2


def first_kernel(
    potential, source, coil_mask, labels, low, high, y_a, y_b, c_a, c_b, floor_table, rise_table,
    field_out, coarse_out, x_lo, x_hi, yo_a, yo_b, drive_sums, drive, floor, rise, *scratch,
):
    place = Place()
    field = scratch[0]
    put_field(
        field, potential, low, high, y_a, y_b, 88, place, first_corners(c_a, c_b, place)
    )
    put_material(
        drive, floor, rise, source, coil_mask, labels, low, high, y_a, y_b, c_a, c_b, floor_table,
        rise_table, place,
    )
    sum_drive(drive, drive_sums)
    coarse = fine_iteration(*scratch, drive_sums, drive, floor, rise)
    emit(field, coarse, field_out, (x_lo, x_hi, yo_a, yo_b), coarse_out, place)


def first_iteration(potential, source, coil_mask, labels, messages, tables, devices):
    depth = potential.shape[-1]
    return pl.pallas_call(
        first_kernel,
        in_specs=[VMEM] * 10 + [SMEM] * 2,
        out_specs=[VMEM] * 10,
        out_shape=[f32(*potential.shape), f32(devices, 4, LANES)]
        + edge_shapes(depth)
        + [f32(32, 2 * LANES), f32(3, 2, EXT, EXT, LANES), f32(2, EXT, EXT, LANES), f32(2, EXT, EXT, LANES)],
        scratch_shapes=SCRATCH,
        compiler_params=PARAMS,
        name="first_iteration",
    )(potential, source, coil_mask, labels, *messages, *tables)


SLOTS = ((0, 1), (1, 0), (1, 1), (2, 0))


def solve_kernel(gathered, wide_out, picked):
    place = Place()
    targets, relucts = [], []
    for stripe in range(3):
        index = jnp.clip(place.col + stripe - 1, 0, place.cols - 1)
        target, reluct = stripe_rows(
            gathered.shape[0], lambda row, part, index=index: gathered[row, index, part, :]
        )
        targets.append(target)
        relucts.append(reluct)
    wide_out[...] = widen(coarse_solve(targets, relucts), SLOTS, place.row, picked)


def solve(gathered):
    return pl.pallas_call(
        solve_kernel,
        in_specs=[VMEM],
        out_specs=VMEM,
        out_shape=f32(128, 2 * LANES),
        scratch_shapes=[pltpu.VMEM((128, LANES), jnp.float32)],
        compiler_params=PARAMS,
        name="solve",
    )(gathered)


def next_kernel(
    final, wide, core, low, high, y_a, y_b, drive_sums, drive, floor, rise, *refs
):
    if final:
        field_out, coarse_out, reluct_out, *scratch = refs
        edges = None
    else:
        field_out, coarse_out, x_lo, x_hi, yo_a, yo_b, *scratch = refs
        edges = (x_lo, x_hi, yo_a, yo_b)
    place = Place()
    field = scratch[0]
    put_field(
        field, core, low, high, y_a, y_b, 3 * BLOCK + 3, place,
        later_corners(low, high, y_a, y_b, place),
    )
    mid = slice(TOP, TOP + EXT)
    cell = lax.broadcasted_iota(jnp.int32, (EXT, LANES), 0)
    for slab, (begin, end, shift, x) in enumerate(SLABS):
        for comp in range(3):
            for half in range(2):
                z = slice(half * LANES, (half + 1) * LANES)
                lines = [
                    wide[spot : spot + 1, z]
                    for spot in ((2 * slot + x) * 16 + comp * 3 + shift for slot in range(4))
                ]
                back = jnp.where(place.back, lines[0], 0.0)
                front = jnp.where(place.front, lines[3], 0.0)
                tile = jnp.where(
                    cell < 12,
                    jnp.where(cell < 4, back, lines[1]),
                    jnp.where(cell < 20, lines[2], front),
                )
                for plane in range(begin, end):
                    field[comp, half, plane, mid] = field[comp, half, plane, mid] + tile
                for plane in (HALO + x for x in DEEP):
                    if begin <= plane < end:
                        for row, line in ((TOP - 1, back), (TOP + EXT, front)):
                            field[comp, half, plane, row : row + 1, :] = (
                                field[comp, half, plane, row : row + 1, :] + line
                            )
    coarse = fine_iteration(*scratch, drive_sums, drive, floor, rise)
    emit(field, coarse, field_out, edges, coarse_out, place)
    if final:
        reluct = scratch[2]
        for half in range(2):
            reluct_out[:, :, half * LANES : (half + 1) * LANES] = reluct[
                half, 4:20, CORE : CORE + BLOCK, :
            ]


def next_iteration(final, wide, core, messages, material, devices):
    outs = [f32(*core.shape), f32(devices, 4, LANES)]
    outs += [f32(*core.shape[1:])] if final else edge_shapes(core.shape[-1])
    return pl.pallas_call(
        functools.partial(next_kernel, final),
        in_specs=[VMEM] * 10,
        out_specs=[VMEM] * len(outs),
        out_shape=outs,
        scratch_shapes=SCRATCH,
        compiler_params=PARAMS,
        name="last_iteration" if final else "next_iteration",
    )(wide, core, *messages, *material)


def correct_kernel(gathered, core, field_out, target_out, picked):
    row = lax.axis_index("row")
    rows = gathered.shape[0]
    target, reluct = stripe_rows(rows, lambda row, part: gathered[row, part, :])
    wide = widen(coarse_solve([target], [reluct]), ((0, 0), (0, 1)), row, picked)
    cell = lax.broadcasted_iota(jnp.int32, (BLOCK, 2 * LANES), 0)
    for x in range(2):
        for comp in range(3):
            spot = x * 16 + comp * 3 + 1
            tile = jnp.where(
                cell < COARSEN, wide[spot : spot + 1], wide[spot + 32 : spot + 33]
            )
            for plane in range(x * COARSEN, (x + 1) * COARSEN):
                field_out[comp, plane] = core[comp, plane] + tile
    for comp in range(3):
        for x in range(2):
            for y in range(2):
                group = x * 2 + y
                moved = target[comp] if group == 0 else pltpu.roll(target[comp], LANES - 32 * group, 1)
                for r in range(rows):
                    target_out[comp, 2 * r + x, y : y + 1, :] = moved[r : r + 1, 0:32]


def correct(gathered, core):
    rows = gathered.shape[0]
    return pl.pallas_call(
        correct_kernel,
        in_specs=[VMEM] * 2,
        out_specs=[VMEM] * 2,
        out_shape=[f32(*core.shape), f32(3, 2 * rows, 2, 32)],
        scratch_shapes=[pltpu.VMEM((64, LANES), jnp.float32)],
        compiler_params=PARAMS,
        name="correct",
    )(gathered, core)


def rings(to_low, to_high):
    count = lax.axis_size("row")
    forward = [(i, (i + 1) % count) for i in range(count)]
    backward = [(target, source) for source, target in forward]
    return lax.ppermute(to_high, "row", forward), lax.ppermute(to_low, "row", backward)


def swaps(turn_a, turn_b):
    count = lax.axis_size("col")
    pairs = []
    for begin in (0, 1):
        partner = list(range(count))
        for i in range(begin, count - 1, 2):
            partner[i], partner[i + 1] = i + 1, i
        pairs.append(list(enumerate(partner)))
    return lax.ppermute(turn_a, "col", pairs[0]), lax.ppermute(turn_b, "col", pairs[1])


def shards(potential, source, labels, coil_mask, floor_table, rise_table):
    rows, cols = lax.axis_size("row"), lax.axis_size("col")
    x_lo, x_hi, y_a, y_b = pack_first(
        *(pltpu.with_memory_space_constraint(v, pltpu.HBM) for v in (potential, source, labels, coil_mask))
    )
    low, high = rings(x_lo, x_hi)
    y_a, y_b = swaps(y_a, y_b)
    c_a, c_b = swaps(*pack_corner(low, high))
    field, coarse, x_lo, x_hi, y_a, y_b, *material = first_iteration(
        potential, source, coil_mask, labels, (low, high, y_a, y_b, c_a, c_b),
        (floor_table, rise_table), rows * cols,
    )
    for iteration in range(1, ITERS):
        final = iteration == ITERS - 1
        low, high = rings(x_lo, x_hi)
        y_a, y_b = swaps(y_a, y_b)
        gathered = lax.all_to_all(coarse, ("row", "col"), 0, 0)
        wide = solve(gathered.reshape(rows, cols, 4, LANES))
        outs = next_iteration(
            final, wide, field, (low, high, y_a, y_b), material, rows if final else rows * cols
        )
        if final:
            field, coarse, reluct = outs
        else:
            field, coarse, x_lo, x_hi, y_a, y_b = outs
    gathered = lax.all_to_all(coarse, "row", 0, 0)
    field, coarse_target = correct(gathered, field)
    return (field, reluct, coarse_target)


def solution(mesh):
    in_specs = (
        P(None, "row", "col", None),
        P(None, "row", "col", None),
        P("row", "col", None),
        P("row", "col", None),
        P(),
        P(),
    )
    out_specs = (P(None, "row", "col", None), P("row", "col", None), P(None, None, "col", None))
    return jax.shard_map(shards, mesh=mesh, in_specs=in_specs, out_specs=out_specs, check_vma=False)
```

```python
import functools
import jax
import jax.numpy as jnp
from jax import lax
from jax.experimental import pallas as pl
from jax.experimental.pallas import tpu as pltpu
from jax.sharding import PartitionSpec as P

ITERS = 3
SWEEPS = 2
COARSE_SWEEPS = 16
COARSEN = 8
RELAX = 0.8

HALO = 4
BLOCK = 16
EXT = BLOCK + 2 * HALO
LANES = 128
TOP = 8
CORE = TOP + HALO
ROWS = 40
HIGH = lax.Precision.HIGHEST
X_PAGES = 21
Y_PAGES = 91
DEEP = (1, BLOCK - 2)

VMEM = pl.BlockSpec(memory_space=pltpu.VMEM)
SMEM = pl.BlockSpec(memory_space=pltpu.SMEM)
PARAMS = pltpu.CompilerParams(vmem_limit_bytes=44 * 1024 * 1024)


def f32(*shape):
    return jax.ShapeDtypeStruct(shape, jnp.float32)


def turns(even, low_edge, high_edge):
    return jnp.where(even, high_edge, low_edge), jnp.where(even, low_edge, high_edge)


def corner_parts(reach):
    first = 0
    parts = []
    for distance in range(1, reach):
        parts.append((distance, first, reach - distance))
        first += reach - distance
    return parts, first


CORNER_FIELD, FIELD_ROWS = corner_parts(4)
CORNER_LABEL, LABEL_ROWS = corner_parts(3)
CORNER_DRIVE = 6 * FIELD_ROWS
CORNER_TABLE = CORNER_DRIVE + 6
CORNER_ALL = CORNER_TABLE + 2 * LABEL_ROWS
SLABS = ((0, 4, 0, 1), (4, 12, 1, 0), (12, 20, 1, 1), (20, 24, 2, 0))


def fetch_all(sems, pairs):
    copies = [
        pltpu.make_async_copy(ref, scratch, sems.at[number])
        for number, (ref, scratch) in enumerate(pairs)
    ]
    for copy in copies:
        copy.start()
    for copy in copies:
        copy.wait()


def pack_x_kernel(potential, source, coil_mask, labels, x_lo, x_hi, pot, src, mask, lab, sems):
    pairs = []
    for side, (cells, pair) in enumerate((
        (slice(0, 4), slice(0, 2)), (slice(BLOCK - 4, BLOCK), slice(BLOCK - 2, BLOCK)),
    )):
        pairs += [
            (potential.at[:, cells], pot.at[side]), (source.at[:, pair], src.at[side]),
            (coil_mask.at[pair], mask.at[side]), (labels.at[cells], lab.at[side]),
        ]
    fetch_all(sems, pairs)
    for side, out in enumerate((x_lo, x_hi)):
        for comp in range(3):
            out[comp * 4 : comp * 4 + 4] = pot[side, comp]
            out[12 + comp * 2 : 14 + comp * 2] = 2.0 * src[side, comp] * mask[side].astype(jnp.float32)
        out[18:21] = lab[side, side : side + 3].astype(jnp.float32)


def pack_y_kernel(potential, source, coil_mask, labels, y_a, y_b, pot, src, mask, lab, sems):
    even = lax.axis_index("col") % 2 == 0
    pairs = []
    for side, rows in enumerate((slice(0, 8), slice(BLOCK - 8, BLOCK))):
        pairs += [
            (potential.at[:, :, rows], pot.at[side]), (source.at[:, :, rows], src.at[side]),
            (coil_mask.at[:, rows], mask.at[side]), (labels.at[:, rows], lab.at[side]),
        ]
    fetch_all(sems, pairs)

    def send(page, low_edge, high_edge, rows=slice(0, 4)):
        first, second = turns(even, low_edge, high_edge)
        y_a[page, rows] = first
        y_b[page, rows] = second

    for x in range(BLOCK):
        mask_lo = 2.0 * mask[0, x, 0:2].astype(jnp.float32)
        mask_hi = 2.0 * mask[1, x, 6:8].astype(jnp.float32)
        for comp in range(3):
            send(comp * 16 + x, pot[0, comp, x, 0:4], pot[1, comp, x, 4:8])
            send(
                48 + comp * 8 + x // 2, src[0, comp, x, 0:2] * mask_lo,
                src[1, comp, x, 6:8] * mask_hi, slice((x % 2) * 2, (x % 2) * 2 + 2),
            )
        send(72 + x, lab[0, x, 0:4].astype(jnp.float32), lab[1, x, 4:8].astype(jnp.float32))
    for number, x in enumerate(DEEP):
        mask_lo = 2.0 * mask[0, x, 2:3].astype(jnp.float32)
        mask_hi = 2.0 * mask[1, x, 5:6].astype(jnp.float32)
        for comp in range(3):
            send(88 + comp, pot[0, comp, x, 4:5], pot[1, comp, x, 3:4], slice(number, number + 1))
            send(
                88 + comp, src[0, comp, x, 2:3] * mask_lo, src[1, comp, x, 5:6] * mask_hi,
                slice(2 + number, 3 + number),
            )


def pack_edges(kernel, name, shapes, out, arrays):
    types = (jnp.float32, jnp.float32, jnp.int32, jnp.int32)
    return pl.pallas_call(
        kernel,
        in_specs=[pl.BlockSpec(memory_space=pltpu.HBM)] * 4,
        out_specs=[VMEM] * 2,
        out_shape=[out] * 2,
        scratch_shapes=[pltpu.VMEM((2,) + shape, kind) for shape, kind in zip(shapes, types)]
        + [pltpu.SemaphoreType.DMA((8,))],
        compiler_params=PARAMS,
        name=name,
    )(*(pltpu.with_memory_space_constraint(v, pltpu.HBM) for v in arrays))


def pack_x(arrays):
    depth = arrays[0].shape[-1]
    shapes = ((3, 4, BLOCK, depth), (3, 2, BLOCK, depth), (2, BLOCK, depth), (4, BLOCK, depth))
    return pack_edges(pack_x_kernel, "pack_x", shapes, f32(X_PAGES, BLOCK, depth), arrays)


def pack_y(arrays):
    depth = arrays[0].shape[-1]
    shapes = ((3, BLOCK, 8, depth),) * 2 + ((BLOCK, 8, depth),) * 2
    return pack_edges(pack_y_kernel, "pack_y", shapes, f32(Y_PAGES, HALO, depth), arrays)


def pack_corner_kernel(low, high, out_a, out_b):
    even = lax.axis_index("col") % 2 == 0

    def send(row, count, ref, page):
        rows = slice(row, row + count)
        first, second = turns(even, ref[page, 0:count], ref[page, BLOCK - count : BLOCK])
        out_a[rows, :] = first
        out_b[rows, :] = second

    for comp in range(3):
        for distance, first, count in CORNER_FIELD:
            row = comp * 2 * FIELD_ROWS + first
            send(row, count, low, comp * 4 + 4 - distance)
            send(row + FIELD_ROWS, count, high, comp * 4 + distance - 1)
    for comp in range(3):
        send(CORNER_DRIVE + comp * 2, 1, low, 12 + comp * 2 + 1)
        send(CORNER_DRIVE + comp * 2 + 1, 1, high, 12 + comp * 2)
    for distance, first, count in CORNER_LABEL:
        row = CORNER_TABLE + first
        send(row, count, low, 18 + 3 - distance)
        send(row + LABEL_ROWS, count, high, 18 + distance - 1)


def pack_corner(low, high):
    depth = low.shape[-1]
    return pl.pallas_call(
        pack_corner_kernel,
        in_specs=[VMEM] * 2,
        out_specs=[VMEM] * 2,
        out_shape=[f32(CORNER_ALL, depth)] * 2,
        compiler_params=PARAMS,
        name="pack_corner",
    )(low, high)


def coarse_solve(targets, relucts):
    shape = relucts[0].shape
    count = shape[0]
    lane = lax.broadcasted_iota(jnp.int32, shape, 1)
    row = lax.broadcasted_iota(jnp.int32, shape, 0)
    z = lane % 32
    first_y = (lane // 32) % 2 == 0
    first_x = lane // 64 == 0
    up_ok, down_ok = z < 31, z > 0
    far_ok = jnp.logical_not(
        jnp.logical_or(
            jnp.logical_and(first_x, row == 0),
            jnp.logical_and(jnp.logical_not(first_x), row == count - 1),
        )
    )

    def up(v):
        return pltpu.roll(v, LANES - 1, 1)

    def down(v):
        return pltpu.roll(v, 1, 1)

    def side(v):
        return jnp.where(first_y, pltpu.roll(v, LANES - 32, 1), pltpu.roll(v, 32, 1))

    def near(v):
        return pltpu.roll(v, 64, 1)

    def far(swapped, turned=False):
        below, above = pltpu.roll(swapped, 1, 0), pltpu.roll(swapped, count - 1, 0)
        return jnp.where(first_x, above, below) if turned else jnp.where(first_x, below, above)

    sets = []
    for r in relucts:
        swapped = near(r)
        c_up = r + jnp.where(up_ok, up(r), 0.0)
        c_down = r + jnp.where(down_ok, down(r), 0.0)
        c_side = r + side(r)
        c_near = r + swapped
        c_far = r + jnp.where(far_ok, far(swapped), 0.0)
        diag = ((c_up + c_down) + (c_side + r)) + (c_near + c_far)
        c_up = jnp.where(up_ok, c_up, 0.0)
        c_down = jnp.where(down_ok, c_down, 0.0)
        c_far = jnp.where(far_ok, c_far, 0.0)
        sets.append((c_up, c_down, c_side, c_near, c_far, diag, RELAX / diag))

    def neighbours(coeffs, v, swapped, turned=False):
        c_up, c_down, c_side, c_near, c_far = coeffs[:5]
        return (
            (c_up * up(v) + c_down * down(v)) + (c_side * side(v) + c_near * swapped)
        ) + c_far * far(swapped, turned)

    turned_sets = [[near(c) for c in coeffs] for coeffs in sets]
    doubled = [[2.0 * t for t in stripe] for stripe in targets]
    swapped_t = [[near(t) for t in stripe] for stripe in doubled]
    plain = [[coeffs[6] * t for t in stripe] for coeffs, stripe in zip(sets, doubled)]
    swapped = [[coeffs[6] * t for t in stripe] for coeffs, stripe in zip(turned_sets, swapped_t)]
    for step in range(COARSE_SWEEPS - 1):
        plain, swapped = [
            [
                (1.0 - RELAX) * v + coeffs[6] * (t + neighbours(coeffs, v, s))
                for v, s, t in zip(*stripe)
            ]
            for coeffs, stripe in zip(sets, zip(plain, swapped, doubled))
        ], [
            [
                (1.0 - RELAX) * s + coeffs[6] * (t + neighbours(coeffs, s, v, True))
                for v, s, t in zip(*stripe)
            ]
            for coeffs, stripe in zip(turned_sets, zip(plain, swapped, swapped_t))
        ]
    out = []
    for coeffs, *stripe in zip(sets, plain, swapped, doubled):
        total = jnp.sum(jnp.sum(coeffs[5], axis=1, keepdims=True), axis=0, keepdims=True)
        done = []
        for v, s, t in zip(*stripe):
            left = t - (coeffs[5] * v - neighbours(coeffs, v, s))
            left = jnp.sum(jnp.sum(left, axis=1, keepdims=True), axis=0, keepdims=True)
            done.append(v + left / total)
        out.append(done)
    return out


def pick_row(values, index):
    row = lax.broadcasted_iota(jnp.int32, values.shape, 0)
    return jnp.sum(jnp.where(row == index, values, 0.0), axis=0, keepdims=True)


def block_matrix(lanes_first):
    shape = (LANES, 2 * LANES) if lanes_first else (2 * LANES, LANES)
    lane = lax.broadcasted_iota(jnp.int32, shape, 0 if lanes_first else 1)
    cell = lax.broadcasted_iota(jnp.int32, shape, 1 if lanes_first else 0)
    return jnp.where(lane == cell // COARSEN, 1.0, 0.0)


def side_matrix():
    lane = lax.broadcasted_iota(jnp.int32, (2 * LANES, LANES), 1)
    cell = lax.broadcasted_iota(jnp.int32, (2 * LANES, LANES), 0)
    end = jnp.logical_and(cell % COARSEN == COARSEN - 1, lane < 32)
    block = cell // COARSEN
    return jnp.where(
        end, jnp.where(lane == block, 1.0, jnp.where(lane == block + 1, -1.0, 0.0)), 0.0
    )


def stripe_rows(rows, block):
    spot = lax.broadcasted_iota(jnp.int32, (rows, LANES), 0)
    out = []
    for comp in range(4):
        total = jnp.zeros((rows, LANES), jnp.float32)
        for row in range(rows):
            total = jnp.where(spot == row, block(row, slice(comp, comp + 1)), total)
        out.append(total)
    scale = 1.0 / float(COARSEN * COARSEN)
    return [out[comp] * scale for comp in range(3)], out[3]


def widen(corrections, slots, row, picked):
    lines = []
    for correction in corrections:
        picked[0:16, :] = jnp.zeros((16, LANES), jnp.float32)
        for comp in range(3):
            for shift in range(3):
                spot = comp * 3 + shift
                picked[spot : spot + 1, :] = pick_row(correction[comp], row + shift - 1)
        lines.append(picked[0:16, :])
    for number, (stripe, y) in enumerate(slots):
        for x in range(2):
            group = x * 2 + y
            spot = (2 * number + x) * 16
            picked[spot : spot + 16, :] = (
                lines[stripe] if group == 0 else pltpu.roll(lines[stripe], LANES - 32 * group, 1)
            )
    return jnp.dot(
        picked[...], block_matrix(True), precision=HIGH, preferred_element_type=jnp.float32
    )


class Place:
    def __init__(self):
        self.row, self.rows = lax.axis_index("row"), lax.axis_size("row")
        self.col, self.cols = lax.axis_index("col"), lax.axis_size("col")
        self.low, self.high = self.row > 0, self.row < self.rows - 1
        self.back, self.front = self.col > 0, self.col < self.cols - 1
        self.even = self.col % 2 == 0

    def sides(self, turn_a, turn_b):
        return jnp.where(self.even, turn_b, turn_a), jnp.where(self.even, turn_a, turn_b)


def put_corner(put, message, place, row, distance, count):
    for side, there in ((0, place.low), (1, place.high)):
        back, front = place.sides(message[0](row[side], count), message[1](row[side], count))
        plane = HALO - distance if side == 0 else HALO + BLOCK - 1 + distance
        put(plane, HALO - count, count, jnp.logical_and(there, place.back), back)
        put(plane, HALO + BLOCK, count, jnp.logical_and(there, place.front), front)


def put_field(field, core, low, high, y_a, y_b, deep, place, corners):
    for comp in range(3):
        for half in range(2):
            z = slice(half * LANES, half * LANES + LANES)
            own = slice(CORE, CORE + BLOCK)
            field[comp, half, 4:20, own, :] = core[comp, :, :, z]
            pages = slice(comp * 4, comp * 4 + 4)
            field[comp, half, 0:4, own, :] = jnp.where(place.low, low[pages, :, z], 0.0)
            field[comp, half, 20:24, own, :] = jnp.where(place.high, high[pages, :, z], 0.0)
            pages = slice(comp * 16, comp * 16 + 16)
            back, front = place.sides(y_a[pages, :, z], y_b[pages, :, z])
            field[comp, half, 4:20, TOP : TOP + HALO, :] = jnp.where(place.back, back, 0.0)
            field[comp, half, 4:20, CORE + BLOCK : CORE + BLOCK + HALO, :] = jnp.where(
                place.front, front, 0.0
            )

            def put(plane, row, count, there, value):
                field[comp, half, plane, TOP + row : TOP + row + count, :] = jnp.where(
                    there, value, 0.0
                )

            for number, x in enumerate(DEEP):
                rows = slice(number, number + 1)
                back, front = place.sides(y_a[deep + comp, rows, z], y_b[deep + comp, rows, z])
                put(HALO + x, -1, 1, place.back, back)
                put(HALO + x, EXT, 1, place.front, front)
            corners(put, comp, z)


def first_corners(c_a, c_b, place):
    def corners(put, comp, z):
        message = [lambda row, count, ref=ref: ref[row : row + count, z] for ref in (c_a, c_b)]
        for distance, first, count in CORNER_FIELD:
            row = comp * 2 * FIELD_ROWS + first
            put_corner(put, message, place, (row, row + FIELD_ROWS), distance, count)

    return corners


ROW_CORNERS = ((1, 1), (2, 1), (3, 1), (2, 2))
X_EDGE = 3 * HALO + 2
Y_EDGE = 3 * BLOCK + 6


def later_corners(low, high, y_a, y_b, place):
    def corners(put, comp, z):
        both = jnp.logical_and
        for ref, there, sign in ((low, place.low, -1), (high, place.high, 1)):
            for number, (along_x, along_y) in enumerate(ROW_CORNERS):
                plane = HALO - along_x if sign < 0 else HALO + BLOCK - 1 + along_x
                for end, side in enumerate((place.back, place.front)):
                    spot = comp * 8 + end * 4 + number
                    row = HALO - along_y if end == 0 else HALO + BLOCK - 1 + along_y
                    value = ref[12 + spot // 16, spot % 16 : spot % 16 + 1, z]
                    put(plane, row, 1, both(there, side), value)
        page = 3 * BLOCK + comp
        for number in range(4):
            along_y = 2 + number % 2
            plane, there = ((HALO - 1, place.low), (HALO + BLOCK, place.high))[number // 2]
            rows = slice(number, number + 1)
            back, front = place.sides(y_a[page, rows, z], y_b[page, rows, z])
            put(plane, HALO - along_y, 1, both(there, place.back), back)
            put(plane, HALO + BLOCK - 1 + along_y, 1, both(there, place.front), front)

    return corners


def put_material(
    drive, floor, rise, source, coil_mask, labels, low, high, y_a, y_b, c_a, c_b, floor_table,
    rise_table, place,
):
    for half in range(2):
        z = slice(half * LANES, half * LANES + LANES)
        own = slice(HALO, HALO + BLOCK)
        coil = 2.0 * coil_mask[:, :, z].astype(jnp.float32)
        message = [lambda row, count, ref=ref: ref[row : row + count, z] for ref in (c_a, c_b)]
        for comp in range(3):
            drive[comp, half, 4:20, own, :] = source[comp, :, :, z] * coil
            pages = slice(12 + comp * 2, 14 + comp * 2)
            drive[comp, half, 2:4, own, :] = low[pages, :, z]
            drive[comp, half, 20:22, own, :] = high[pages, :, z]
            for x in range(BLOCK):
                page, part = 48 + comp * 8 + x // 2, slice((x % 2) * 2, (x % 2) * 2 + 2)
                back, front = place.sides(y_a[page, part, z], y_b[page, part, z])
                drive[comp, half, 4 + x, 2:4, :] = back
                drive[comp, half, 4 + x, 20:22, :] = front

            def put_drive(plane, row, count, there, value):
                drive[comp, half, plane, row : row + count, :] = value

            row = CORNER_DRIVE + comp * 2
            put_corner(put_drive, message, place, (row, row + 1), 1, 1)
            for number, x in enumerate(DEEP):
                rows = slice(2 + number, 3 + number)
                back, front = place.sides(y_a[88 + comp, rows, z], y_b[88 + comp, rows, z])
                put_drive(HALO + x, 1, 1, None, back)
                put_drive(HALO + x, HALO + BLOCK + 2, 1, None, front)
        floor[half, 4:20, own, :] = labels[:, :, z].astype(jnp.float32)
        floor[half, 1:4, own, :] = jnp.where(place.low, low[18:21, :, z], -1.0)
        floor[half, 20:23, own, :] = jnp.where(place.high, high[18:21, :, z], -1.0)
        back, front = place.sides(y_a[72:88, :, z], y_b[72:88, :, z])
        floor[half, 4:20, 0:HALO, :] = jnp.where(place.back, back, -1.0)
        floor[half, 4:20, HALO + BLOCK : EXT, :] = jnp.where(place.front, front, -1.0)

        def put_label(plane, row, count, there, value):
            floor[half, plane, row : row + count, :] = jnp.where(there, value, -1.0)

        for distance, first, count in CORNER_LABEL:
            row = CORNER_TABLE + first
            put_corner(put_label, message, place, (row, row + LABEL_ROWS), distance, count)

    for x in range(1, EXT - 1):
        for half in range(2):
            label = floor[half, x]
            floor_cell = jnp.zeros_like(label)
            rise_cell = jnp.zeros_like(label)
            for number in range(floor_table.shape[0]):
                chosen = label == float(number)
                floor_cell = jnp.where(chosen, floor_table[number], floor_cell)
                rise_cell = jnp.where(chosen, rise_table[number], rise_cell)
            floor[half, x] = floor_cell
            rise[half, x] = rise_cell


def right_of(low, high, last):
    a, b = pltpu.roll(low, LANES - 1, 1), pltpu.roll(high, LANES - 1, 1)
    return jnp.where(last, b, a), b


def left_of(low, high, first):
    a, b = pltpu.roll(low, 1, 1), pltpu.roll(high, 1, 1)
    return a, jnp.where(first, a, b)


def each(begin, end, plane):
    for x in range(begin, end):
        for ref, value in plane(x):
            ref[...] = value


def fine_iteration(
    field, other, reluct, c_x, c_y, c_up, c_down, weight, sums, drive_sums, drive, floor, rise,
):
    mid = slice(TOP, TOP + EXT)
    plus = slice(TOP + 1, TOP + EXT + 1)
    minus = slice(TOP - 1, TOP + EXT - 1)
    lane = lax.broadcasted_iota(jnp.int32, (EXT, LANES), 1)
    first, last = lane == 0, lane == LANES - 1

    def reluct_plane(x):
        stores = []
        along_z = []
        for comp in range(2):
            low, high = field[comp, 0, x, mid], field[comp, 1, x, mid]
            r0, r1 = right_of(low, high, last)
            l0, l1 = left_of(low, high, first)
            along_z.append((r0 - jnp.where(first, 0.0, l0), jnp.where(last, 0.0, r1) - l1))
        for half in range(2):
            def along_y(comp):
                return field[comp, half, x, plus] - field[comp, half, x, minus]

            def along_x(comp):
                return field[comp, half, x + 1, mid] - field[comp, half, x - 1, mid]

            b0 = along_y(2) - along_z[1][half]
            b1 = along_z[0][half] - along_x(2)
            b2 = along_x(1) - along_y(0)
            square = 0.25 * (b0 * b0 + b1 * b1 + b2 * b2)
            stores.append((
                reluct.at[half, x, mid], floor[half, x] + rise[half, x] * (square / (1.0 + square))
            ))
        return stores

    each(1, EXT - 1, reluct_plane)

    def apply(src, x, rows, coeffs, first_lane, last_lane):
        rows_plus = slice(rows.start + 1, rows.stop + 1)
        rows_minus = slice(rows.start - 1, rows.stop - 1)
        out = []
        for comp in range(3):
            low, high = src[comp, 0, x, rows], src[comp, 1, x, rows]
            rights = right_of(low, high, last_lane)
            lefts = left_of(low, high, first_lane)
            for half in range(2):
                x_plus, x_minus, y_plus, y_minus, up, down = coeffs[half]
                total = (
                    (x_plus * src[comp, half, x + 1, rows] + x_minus * src[comp, half, x - 1, rows])
                    + (y_plus * src[comp, half, x, rows_plus] + y_minus * src[comp, half, x, rows_minus])
                    + (up * rights[half] + down * lefts[half])
                )
                out.append((comp, half, (low, high)[half], total))
        return out

    def load_coeffs(x, rows):
        rows_minus = slice(rows.start - 1, rows.stop - 1)
        return [
            (
                c_x[half, x, rows], c_x[half, x - 1, rows], c_y[half, x, rows],
                c_y[half, x, rows_minus], c_up[half, x, rows], c_down[half, x, rows],
            )
            for half in range(2)
        ]

    def first_plane(x):
        low, high = reluct[0, x, mid], reluct[1, x, mid]
        r0, r1 = right_of(low, high, last)
        l0, l1 = left_of(low, high, first)
        ups = (low + r0, high + jnp.where(last, 0.0, r1))
        downs = (low + jnp.where(first, 0.0, l0), high + l1)
        stores, coeffs, weights = [], [], []
        for half in range(2):
            here = (low, high)[half]
            x_plus = here + reluct[half, x + 1, mid]
            x_minus = here + reluct[half, x - 1, mid]
            y_plus = here + reluct[half, x, plus]
            y_minus = here + reluct[half, x, minus]
            total = ((x_plus + x_minus) + (y_plus + y_minus)) + (ups[half] + downs[half])
            up = ups[half] if half == 0 else jnp.where(last, 0.0, ups[half])
            down = jnp.where(first, 0.0, downs[half]) if half == 0 else downs[half]
            scale = jnp.where(floor[half, x] > 0.0, RELAX / total, 0.0)
            coeffs.append((x_plus, x_minus, y_plus, y_minus, up, down))
            weights.append(scale)
            for ref, value in (
                (c_x, x_plus), (c_y, y_plus), (c_up, up), (c_down, down), (weight, scale),
            ):
                stores.append((ref.at[half, x, mid], value))
        for comp, half, here, total in apply(field, x, mid, coeffs, first, last):
            stores.append((
                other.at[comp, half, x, mid],
                (1.0 - RELAX) * here + weights[half] * (drive[comp, half, x] + total),
            ))
        return stores

    each(2, EXT - 2, first_plane)

    def second_plane(x):
        stores = []
        weights = [weight[half, x, mid] for half in range(2)]
        for comp, half, here, total in apply(other, x, mid, load_coeffs(x, mid), first, last):
            stores.append((
                field.at[comp, half, x, mid],
                (1.0 - RELAX) * here + weights[half] * (drive[comp, half, x] + total),
            ))
        return stores

    each(3, EXT - 3, second_plane)

    own = slice(CORE, CORE + BLOCK)
    ends = pl.ds(CORE - 1, 3, stride=COARSEN)
    beyond = pl.ds(CORE, 3, stride=COARSEN)
    lane = lax.broadcasted_iota(jnp.int32, (BLOCK, LANES), 1)
    last_own = lane == LANES - 1
    lane = lax.broadcasted_iota(jnp.int32, (1, LANES), 1)
    rims = (lane == 0, lane == LANES - 1)
    zero = jnp.zeros((BLOCK, LANES), jnp.float32)
    thin = jnp.zeros((3, LANES), jnp.float32)

    def blocks(values):
        return [
            jnp.sum(values[part * COARSEN : (part + 1) * COARSEN], axis=0, keepdims=True)
            for part in range(2)
        ]

    def side(plane, comp, half):
        return blocks(
            c_x[half, plane, own]
            * (field[comp, half, plane + 1, own] - field[comp, half, plane, own])
        )

    sums[...] = jnp.zeros(sums.shape, jnp.float32)
    sides = [
        [[side(HALO - 1 + COARSEN * k, comp, half) for half in range(2)] for comp in range(3)]
        for k in range(3)
    ]
    for coarse in range(2):
        def plane(x, totals):
            across, rim, along, material = totals
            relucts = [reluct[half, x, own] for half in range(2)]
            ups = [c_up[half, x, own] for half in range(2)]
            ys = [c_y[half, x, ends, :] for half in range(2)]
            across_new, rim_new, along_new = [], [], []
            for comp in range(3):
                here = [field[comp, half, x, own] for half in range(2)]
                rights = right_of(here[0], here[1], last_own)
                for half in range(2):
                    number = comp * 2 + half
                    across_new.append(across[number] + ups[half] * (rights[half] - here[half]))
                    rim_new.append(rim[number] + relucts[half] * here[half])
                    along_new.append(
                        along[number]
                        + ys[half] * (field[comp, half, x, beyond, :] - field[comp, half, x, ends, :])
                    )
            return (
                tuple(across_new), tuple(rim_new), tuple(along_new),
                tuple(material[half] + relucts[half] for half in range(2)),
            )

        totals = ((zero,) * 6, (zero,) * 6, (thin,) * 6, (zero,) * 2)
        for step in range(COARSEN):
            totals = plane(HALO + coarse * COARSEN + step, totals)
        across, rim, along, material = totals
        for half in range(2):
            z = slice(half * LANES, (half + 1) * LANES)
            means = blocks(material[half])
            for comp in range(3):
                number = comp * 2 + half
                rims_sum, across_sum = blocks(rim[number]), blocks(across[number])
                for part in range(2):
                    row = (coarse * 2 + part) * 8
                    y_side = along[number][part + 1 : part + 2] - along[number][part : part + 1]
                    x_side = sides[coarse + 1][comp][half][part] - sides[coarse][comp][half][part]
                    spot = row + comp
                    sums[0, spot : spot + 1, z] = 0.5 * (
                        (drive_sums[spot : spot + 1, z] + (x_side + y_side))
                        - jnp.where(rims[half], rims_sum[part], 0.0)
                    )
                    sums[1, spot : spot + 1, z] = 0.5 * across_sum[part]
            for part in range(2):
                spot = (coarse * 2 + part) * 8 + 3
                sums[0, spot : spot + 1, z] = means[part] * (1.0 / float(COARSEN ** 3))
    totals = jnp.dot(
        sums[0], block_matrix(False), precision=HIGH, preferred_element_type=jnp.float32
    ) + jnp.dot(sums[1], side_matrix(), precision=HIGH, preferred_element_type=jnp.float32)
    result = totals[0:8]
    for group in range(1, 4):
        result = result + pltpu.roll(totals[group * 8 : group * 8 + 8], 32 * group, 1)
    return result[0:4]


def sum_drive(drive, drive_sums):
    own = slice(HALO, HALO + BLOCK)
    drive_sums[...] = jnp.zeros(drive_sums.shape, jnp.float32)
    for comp in range(3):
        for half in range(2):
            for coarse in range(2):
                total = drive[comp, half, HALO + coarse * COARSEN, own]
                for x in range(HALO + coarse * COARSEN + 1, HALO + (coarse + 1) * COARSEN):
                    total = total + drive[comp, half, x, own]
                for part in range(2):
                    spot = (coarse * 2 + part) * 8 + comp
                    drive_sums[spot : spot + 1, half * LANES : (half + 1) * LANES] = jnp.sum(
                        total[part * COARSEN : (part + 1) * COARSEN], axis=0, keepdims=True
                    )


SCRATCH = (
    [pltpu.VMEM((3, 2, EXT, ROWS, LANES), jnp.float32)] * 2
    + [pltpu.VMEM((2, EXT, ROWS, LANES), jnp.float32)] * 6
    + [pltpu.VMEM((2, 32, 2 * LANES), jnp.float32)]
)


def emit(field, coarse, field_out, edges, coarse_out, place):
    own = slice(CORE, CORE + BLOCK)
    for comp in range(3):
        for half in range(2):
            z = slice(half * LANES, half * LANES + LANES)
            field_out[comp, :, :, z] = field[comp, half, 4:20, own, :]
            if edges:
                x_lo, x_hi, y_a, y_b = edges
                x_lo[comp * 4 : comp * 4 + 4, :, z] = field[comp, half, 4:8, own, :]
                x_hi[comp * 4 : comp * 4 + 4, :, z] = field[comp, half, 16:20, own, :]
                first, second = turns(
                    place.even, field[comp, half, 4:20, CORE : CORE + 4, :],
                    field[comp, half, 4:20, CORE + BLOCK - 4 : CORE + BLOCK, :],
                )
                y_a[comp * 16 : comp * 16 + 16, :, z] = first
                y_b[comp * 16 : comp * 16 + 16, :, z] = second

                def cell(x, y):
                    return field[comp, half, HALO + x, CORE + y : CORE + y + 1, :]

                def send(page, row, x, low_y, high_y):
                    first, second = turns(place.even, cell(x, low_y), cell(x, high_y))
                    y_a[page, row : row + 1, z] = first
                    y_b[page, row : row + 1, z] = second

                for number, (along_x, along_y) in enumerate(ROW_CORNERS):
                    for end, y in enumerate((-along_y, BLOCK - 1 + along_y)):
                        spot = comp * 8 + end * 4 + number
                        rows = slice(spot % 16, spot % 16 + 1)
                        x_lo[12 + spot // 16, rows, z] = cell(along_x - 1, y)
                        x_hi[12 + spot // 16, rows, z] = cell(BLOCK - along_x, y)
                for number in range(4):
                    along_y = 2 + number % 2
                    send(
                        3 * BLOCK + comp, number, (-1, BLOCK)[number // 2], along_y - 1,
                        BLOCK - along_y,
                    )
                for number, x in enumerate(DEEP):
                    send(3 * BLOCK + 3 + comp, number, x, HALO, BLOCK - 1 - HALO)
    coarse_out[...] = jnp.broadcast_to(coarse[None], coarse_out.shape)


def edge_shapes(depth):
    return [f32(X_EDGE, BLOCK, depth)] * 2 + [f32(Y_EDGE, HALO, depth)] * 2


def first_kernel(
    potential, source, coil_mask, labels, low, high, y_a, y_b, c_a, c_b, floor_table, rise_table,
    field_out, coarse_out, x_lo, x_hi, yo_a, yo_b, drive_sums, drive, floor, rise, *scratch,
):
    place = Place()
    field = scratch[0]
    put_field(
        field, potential, low, high, y_a, y_b, 88, place, first_corners(c_a, c_b, place)
    )
    put_material(
        drive, floor, rise, source, coil_mask, labels, low, high, y_a, y_b, c_a, c_b, floor_table,
        rise_table, place,
    )
    sum_drive(drive, drive_sums)
    coarse = fine_iteration(*scratch, drive_sums, drive, floor, rise)
    emit(field, coarse, field_out, (x_lo, x_hi, yo_a, yo_b), coarse_out, place)


def first_iteration(potential, source, coil_mask, labels, messages, tables, devices):
    depth = potential.shape[-1]
    return pl.pallas_call(
        first_kernel,
        in_specs=[VMEM] * 10 + [SMEM] * 2,
        out_specs=[VMEM] * 10,
        out_shape=[f32(*potential.shape), f32(devices, 4, LANES)]
        + edge_shapes(depth)
        + [f32(32, 2 * LANES), f32(3, 2, EXT, EXT, LANES), f32(2, EXT, EXT, LANES), f32(2, EXT, EXT, LANES)],
        scratch_shapes=SCRATCH,
        compiler_params=PARAMS,
        name="first_iteration",
    )(potential, source, coil_mask, labels, *messages, *tables)


SLOTS = ((0, 1), (1, 0), (1, 1), (2, 0))


def solve_kernel(gathered, wide_out, picked):
    place = Place()
    targets, relucts = [], []
    for stripe in range(3):
        index = jnp.clip(place.col + stripe - 1, 0, place.cols - 1)
        target, reluct = stripe_rows(
            gathered.shape[0], lambda row, part, index=index: gathered[row, index, part, :]
        )
        targets.append(target)
        relucts.append(reluct)
    wide_out[...] = widen(coarse_solve(targets, relucts), SLOTS, place.row, picked)


def solve(gathered):
    return pl.pallas_call(
        solve_kernel,
        in_specs=[VMEM],
        out_specs=VMEM,
        out_shape=f32(128, 2 * LANES),
        scratch_shapes=[pltpu.VMEM((128, LANES), jnp.float32)],
        compiler_params=PARAMS,
        name="solve",
    )(gathered)


def next_kernel(
    final, wide, core, low, high, y_a, y_b, drive_sums, drive, floor, rise, *refs
):
    if final:
        field_out, coarse_out, reluct_out, *scratch = refs
        edges = None
    else:
        field_out, coarse_out, x_lo, x_hi, yo_a, yo_b, *scratch = refs
        edges = (x_lo, x_hi, yo_a, yo_b)
    place = Place()
    field = scratch[0]
    put_field(
        field, core, low, high, y_a, y_b, 3 * BLOCK + 3, place,
        later_corners(low, high, y_a, y_b, place),
    )
    mid = slice(TOP, TOP + EXT)
    cell = lax.broadcasted_iota(jnp.int32, (EXT, LANES), 0)
    for slab, (begin, end, shift, x) in enumerate(SLABS):
        for comp in range(3):
            for half in range(2):
                z = slice(half * LANES, (half + 1) * LANES)
                lines = [
                    wide[spot : spot + 1, z]
                    for spot in ((2 * slot + x) * 16 + comp * 3 + shift for slot in range(4))
                ]
                back = jnp.where(place.back, lines[0], 0.0)
                front = jnp.where(place.front, lines[3], 0.0)
                tile = jnp.where(
                    cell < 12,
                    jnp.where(cell < 4, back, lines[1]),
                    jnp.where(cell < 20, lines[2], front),
                )
                for plane in range(begin, end):
                    field[comp, half, plane, mid] = field[comp, half, plane, mid] + tile
                for plane in (HALO + x for x in DEEP):
                    if begin <= plane < end:
                        for row, line in ((TOP - 1, back), (TOP + EXT, front)):
                            field[comp, half, plane, row : row + 1, :] = (
                                field[comp, half, plane, row : row + 1, :] + line
                            )
    coarse = fine_iteration(*scratch, drive_sums, drive, floor, rise)
    emit(field, coarse, field_out, edges, coarse_out, place)
    if final:
        reluct = scratch[2]
        for half in range(2):
            reluct_out[:, :, half * LANES : (half + 1) * LANES] = reluct[
                half, 4:20, CORE : CORE + BLOCK, :
            ]


def next_iteration(final, wide, core, messages, material, devices):
    outs = [f32(*core.shape), f32(devices, 4, LANES)]
    outs += [f32(*core.shape[1:])] if final else edge_shapes(core.shape[-1])
    return pl.pallas_call(
        functools.partial(next_kernel, final),
        in_specs=[VMEM] * 10,
        out_specs=[VMEM] * len(outs),
        out_shape=outs,
        scratch_shapes=SCRATCH,
        compiler_params=PARAMS,
        name="last_iteration" if final else "next_iteration",
    )(wide, core, *messages, *material)


def correct_kernel(gathered, core, field_out, target_out, picked):
    row = lax.axis_index("row")
    rows = gathered.shape[0]
    target, reluct = stripe_rows(rows, lambda row, part: gathered[row, part, :])
    wide = widen(coarse_solve([target], [reluct]), ((0, 0), (0, 1)), row, picked)
    cell = lax.broadcasted_iota(jnp.int32, (BLOCK, 2 * LANES), 0)
    for x in range(2):
        for comp in range(3):
            spot = x * 16 + comp * 3 + 1
            tile = jnp.where(
                cell < COARSEN, wide[spot : spot + 1], wide[spot + 32 : spot + 33]
            )
            for plane in range(x * COARSEN, (x + 1) * COARSEN):
                field_out[comp, plane] = core[comp, plane] + tile
    for comp in range(3):
        for x in range(2):
            for y in range(2):
                group = x * 2 + y
                moved = target[comp] if group == 0 else pltpu.roll(target[comp], LANES - 32 * group, 1)
                for r in range(rows):
                    target_out[comp, 2 * r + x, y : y + 1, :] = moved[r : r + 1, 0:32]


def correct(gathered, core):
    rows = gathered.shape[0]
    return pl.pallas_call(
        correct_kernel,
        in_specs=[VMEM] * 2,
        out_specs=[VMEM] * 2,
        out_shape=[f32(*core.shape), f32(3, 2 * rows, 2, 32)],
        scratch_shapes=[pltpu.VMEM((64, LANES), jnp.float32)],
        compiler_params=PARAMS,
        name="correct",
    )(gathered, core)


def rings(to_low, to_high):
    count = lax.axis_size("row")
    forward = [(i, (i + 1) % count) for i in range(count)]
    backward = [(target, source) for source, target in forward]
    return lax.ppermute(to_high, "row", forward), lax.ppermute(to_low, "row", backward)


def swaps(turn_a, turn_b):
    count = lax.axis_size("col")
    pairs = []
    for begin in (0, 1):
        partner = list(range(count))
        for i in range(begin, count - 1, 2):
            partner[i], partner[i + 1] = i + 1, i
        pairs.append(list(enumerate(partner)))
    return lax.ppermute(turn_a, "col", pairs[0]), lax.ppermute(turn_b, "col", pairs[1])


def shards(potential, source, labels, coil_mask, floor_table, rise_table):
    rows, cols = lax.axis_size("row"), lax.axis_size("col")
    arrays = (potential, source, coil_mask, labels)
    x_lo, x_hi = pack_x(arrays)
    low, high = rings(x_lo, x_hi)
    y_a, y_b, *arrays = lax.optimization_barrier((*pack_y(arrays), *arrays))
    y_a, y_b = swaps(y_a, y_b)
    c_a, c_b = swaps(*pack_corner(low, high))
    field, coarse, x_lo, x_hi, y_a, y_b, *material = first_iteration(
        *arrays, (low, high, y_a, y_b, c_a, c_b),
        (floor_table, rise_table), rows * cols,
    )
    for iteration in range(1, ITERS):
        final = iteration == ITERS - 1
        low, high = rings(x_lo, x_hi)
        y_a, y_b = swaps(y_a, y_b)
        gathered = lax.all_to_all(coarse, ("row", "col"), 0, 0)
        wide = solve(gathered.reshape(rows, cols, 4, LANES))
        outs = next_iteration(
            final, wide, field, (low, high, y_a, y_b), material, rows if final else rows * cols
        )
        if final:
            field, coarse, reluct = outs
        else:
            field, coarse, x_lo, x_hi, y_a, y_b = outs
    gathered = lax.all_to_all(coarse, "row", 0, 0)
    field, coarse_target = correct(gathered, field)
    return (field, reluct, coarse_target)


def solution(mesh):
    in_specs = (
        P(None, "row", "col", None),
        P(None, "row", "col", None),
        P("row", "col", None),
        P("row", "col", None),
        P(),
        P(),
    )
    out_specs = (P(None, "row", "col", None), P("row", "col", None), P(None, None, "col", None))
    return jax.shard_map(shards, mesh=mesh, in_specs=in_specs, out_specs=out_specs, check_vma=False)
```

```python
import functools
import jax
import jax.numpy as jnp
from jax import lax
from jax.experimental import pallas as pl
from jax.experimental.pallas import tpu as pltpu
from jax.sharding import PartitionSpec as P

ITERS = 3
SWEEPS = 2
COARSE_SWEEPS = 16
COARSEN = 8
RELAX = 0.8

HALO = 4
BLOCK = 16
EXT = BLOCK + 2 * HALO
LANES = 128
TOP = 8
CORE = TOP + HALO
ROWS = 40
HIGH = lax.Precision.HIGHEST
X_PAGES = 21
Y_PAGES = 91
DEEP = (1, BLOCK - 2)

VMEM = pl.BlockSpec(memory_space=pltpu.VMEM)
SMEM = pl.BlockSpec(memory_space=pltpu.SMEM)
PARAMS = pltpu.CompilerParams(vmem_limit_bytes=44 * 1024 * 1024)


def f32(*shape):
    return jax.ShapeDtypeStruct(shape, jnp.float32)


def turns(even, low_edge, high_edge):
    return jnp.where(even, high_edge, low_edge), jnp.where(even, low_edge, high_edge)


def corner_parts(reach):
    first = 0
    parts = []
    for distance in range(1, reach):
        parts.append((distance, first, reach - distance))
        first += reach - distance
    return parts, first


CORNER_FIELD, FIELD_ROWS = corner_parts(4)
CORNER_LABEL, LABEL_ROWS = corner_parts(3)
CORNER_DRIVE = 6 * FIELD_ROWS
CORNER_TABLE = CORNER_DRIVE + 6
CORNER_ALL = CORNER_TABLE + 2 * LABEL_ROWS
SLABS = ((0, 4, 0, 1), (4, 12, 1, 0), (12, 20, 1, 1), (20, 24, 2, 0))


def fetch_all(sems, pairs):
    copies = [
        pltpu.make_async_copy(ref, scratch, sems.at[number])
        for number, (ref, scratch) in enumerate(pairs)
    ]
    for copy in copies:
        copy.start()
    for copy in copies:
        copy.wait()


def pack_x_kernel(potential, source, coil_mask, labels, x_lo, x_hi, pot, src, mask, lab, sems):
    pairs = []
    for side, (cells, pair) in enumerate((
        (slice(0, 4), slice(0, 2)), (slice(BLOCK - 4, BLOCK), slice(BLOCK - 2, BLOCK)),
    )):
        pairs += [
            (potential.at[:, cells], pot.at[side]), (source.at[:, pair], src.at[side]),
            (coil_mask.at[pair], mask.at[side]), (labels.at[cells], lab.at[side]),
        ]
    fetch_all(sems, pairs)
    for side, out in enumerate((x_lo, x_hi)):
        for comp in range(3):
            out[comp * 4 : comp * 4 + 4] = pot[side, comp]
            out[12 + comp * 2 : 14 + comp * 2] = 2.0 * src[side, comp] * mask[side].astype(jnp.float32)
        out[18:21] = lab[side, side : side + 3].astype(jnp.float32)


def pack_y_kernel(potential, source, coil_mask, labels, y_a, y_b, pot, src, mask, lab, sems):
    even = lax.axis_index("col") % 2 == 0
    pairs = []
    for side, rows in enumerate((slice(0, 8), slice(BLOCK - 8, BLOCK))):
        pairs += [
            (potential.at[:, :, rows], pot.at[side]), (source.at[:, :, rows], src.at[side]),
            (coil_mask.at[:, rows], mask.at[side]), (labels.at[:, rows], lab.at[side]),
        ]
    fetch_all(sems, pairs)

    def send(page, low_edge, high_edge, rows=slice(0, 4)):
        first, second = turns(even, low_edge, high_edge)
        y_a[page, rows] = first
        y_b[page, rows] = second

    for x in range(BLOCK):
        mask_lo = 2.0 * mask[0, x, 0:2].astype(jnp.float32)
        mask_hi = 2.0 * mask[1, x, 6:8].astype(jnp.float32)
        for comp in range(3):
            send(comp * 16 + x, pot[0, comp, x, 0:4], pot[1, comp, x, 4:8])
            send(
                48 + comp * 8 + x // 2, src[0, comp, x, 0:2] * mask_lo,
                src[1, comp, x, 6:8] * mask_hi, slice((x % 2) * 2, (x % 2) * 2 + 2),
            )
        send(72 + x, lab[0, x, 0:4].astype(jnp.float32), lab[1, x, 4:8].astype(jnp.float32))
    for number, x in enumerate(DEEP):
        mask_lo = 2.0 * mask[0, x, 2:3].astype(jnp.float32)
        mask_hi = 2.0 * mask[1, x, 5:6].astype(jnp.float32)
        for comp in range(3):
            send(88 + comp, pot[0, comp, x, 4:5], pot[1, comp, x, 3:4], slice(number, number + 1))
            send(
                88 + comp, src[0, comp, x, 2:3] * mask_lo, src[1, comp, x, 5:6] * mask_hi,
                slice(2 + number, 3 + number),
            )


def pack_edges(kernel, name, shapes, out, arrays):
    types = (jnp.float32, jnp.float32, jnp.int32, jnp.int32)
    return pl.pallas_call(
        kernel,
        in_specs=[pl.BlockSpec(memory_space=pltpu.HBM)] * 4,
        out_specs=[VMEM] * 2,
        out_shape=[out] * 2,
        scratch_shapes=[pltpu.VMEM((2,) + shape, kind) for shape, kind in zip(shapes, types)]
        + [pltpu.SemaphoreType.DMA((8,))],
        compiler_params=PARAMS,
        name=name,
    )(*(pltpu.with_memory_space_constraint(v, pltpu.HBM) for v in arrays))


def pack_x(arrays):
    depth = arrays[0].shape[-1]
    shapes = ((3, 4, BLOCK, depth), (3, 2, BLOCK, depth), (2, BLOCK, depth), (4, BLOCK, depth))
    return pack_edges(pack_x_kernel, "pack_x", shapes, f32(X_PAGES, BLOCK, depth), arrays)


def pack_y(arrays):
    depth = arrays[0].shape[-1]
    shapes = ((3, BLOCK, 8, depth),) * 2 + ((BLOCK, 8, depth),) * 2
    return pack_edges(pack_y_kernel, "pack_y", shapes, f32(Y_PAGES, HALO, depth), arrays)


def pack_corner_kernel(low, high, out_a, out_b):
    even = lax.axis_index("col") % 2 == 0

    def send(row, count, ref, page):
        rows = slice(row, row + count)
        first, second = turns(even, ref[page, 0:count], ref[page, BLOCK - count : BLOCK])
        out_a[rows, :] = first
        out_b[rows, :] = second

    for comp in range(3):
        for distance, first, count in CORNER_FIELD:
            row = comp * 2 * FIELD_ROWS + first
            send(row, count, low, comp * 4 + 4 - distance)
            send(row + FIELD_ROWS, count, high, comp * 4 + distance - 1)
    for comp in range(3):
        send(CORNER_DRIVE + comp * 2, 1, low, 12 + comp * 2 + 1)
        send(CORNER_DRIVE + comp * 2 + 1, 1, high, 12 + comp * 2)
    for distance, first, count in CORNER_LABEL:
        row = CORNER_TABLE + first
        send(row, count, low, 18 + 3 - distance)
        send(row + LABEL_ROWS, count, high, 18 + distance - 1)


def pack_corner(low, high):
    depth = low.shape[-1]
    return pl.pallas_call(
        pack_corner_kernel,
        in_specs=[VMEM] * 2,
        out_specs=[VMEM] * 2,
        out_shape=[f32(CORNER_ALL, depth)] * 2,
        compiler_params=PARAMS,
        name="pack_corner",
    )(low, high)


def coarse_solve(targets, relucts):
    shape = relucts[0].shape
    count = shape[0]
    lane = lax.broadcasted_iota(jnp.int32, shape, 1)
    row = lax.broadcasted_iota(jnp.int32, shape, 0)
    z = lane % 32
    first_y = (lane // 32) % 2 == 0
    first_x = lane // 64 == 0
    up_ok, down_ok = z < 31, z > 0
    far_ok = jnp.logical_not(
        jnp.logical_or(
            jnp.logical_and(first_x, row == 0),
            jnp.logical_and(jnp.logical_not(first_x), row == count - 1),
        )
    )

    def up(v):
        return pltpu.roll(v, LANES - 1, 1)

    def down(v):
        return pltpu.roll(v, 1, 1)

    def side(v):
        return jnp.where(first_y, pltpu.roll(v, LANES - 32, 1), pltpu.roll(v, 32, 1))

    def near(v):
        return pltpu.roll(v, 64, 1)

    def far(swapped, turned=False):
        below, above = pltpu.roll(swapped, 1, 0), pltpu.roll(swapped, count - 1, 0)
        return jnp.where(first_x, above, below) if turned else jnp.where(first_x, below, above)

    sets = []
    for r in relucts:
        swapped = near(r)
        c_up = r + jnp.where(up_ok, up(r), 0.0)
        c_down = r + jnp.where(down_ok, down(r), 0.0)
        c_side = r + side(r)
        c_near = r + swapped
        c_far = r + jnp.where(far_ok, far(swapped), 0.0)
        diag = ((c_up + c_down) + (c_side + r)) + (c_near + c_far)
        c_up = jnp.where(up_ok, c_up, 0.0)
        c_down = jnp.where(down_ok, c_down, 0.0)
        c_far = jnp.where(far_ok, c_far, 0.0)
        sets.append((c_up, c_down, c_side, c_near, c_far, diag, RELAX / diag))

    def neighbours(coeffs, v, swapped, turned=False):
        c_up, c_down, c_side, c_near, c_far = coeffs[:5]
        return (
            (c_up * up(v) + c_down * down(v)) + (c_side * side(v) + c_near * swapped)
        ) + c_far * far(swapped, turned)

    turned_sets = [[near(c) for c in coeffs] for coeffs in sets]
    doubled = [[2.0 * t for t in stripe] for stripe in targets]
    swapped_t = [[near(t) for t in stripe] for stripe in doubled]
    plain = [[coeffs[6] * t for t in stripe] for coeffs, stripe in zip(sets, doubled)]
    swapped = [[coeffs[6] * t for t in stripe] for coeffs, stripe in zip(turned_sets, swapped_t)]
    for step in range(COARSE_SWEEPS - 1):
        plain, swapped = [
            [
                (1.0 - RELAX) * v + coeffs[6] * (t + neighbours(coeffs, v, s))
                for v, s, t in zip(*stripe)
            ]
            for coeffs, stripe in zip(sets, zip(plain, swapped, doubled))
        ], [
            [
                (1.0 - RELAX) * s + coeffs[6] * (t + neighbours(coeffs, s, v, True))
                for v, s, t in zip(*stripe)
            ]
            for coeffs, stripe in zip(turned_sets, zip(plain, swapped, swapped_t))
        ]
    out = []
    for coeffs, *stripe in zip(sets, plain, swapped, doubled):
        total = jnp.sum(jnp.sum(coeffs[5], axis=1, keepdims=True), axis=0, keepdims=True)
        done = []
        for v, s, t in zip(*stripe):
            left = t - (coeffs[5] * v - neighbours(coeffs, v, s))
            left = jnp.sum(jnp.sum(left, axis=1, keepdims=True), axis=0, keepdims=True)
            done.append(v + left / total)
        out.append(done)
    return out


def pick_row(values, index):
    row = lax.broadcasted_iota(jnp.int32, values.shape, 0)
    return jnp.sum(jnp.where(row == index, values, 0.0), axis=0, keepdims=True)


def block_matrix(lanes_first):
    shape = (LANES, 2 * LANES) if lanes_first else (2 * LANES, LANES)
    lane = lax.broadcasted_iota(jnp.int32, shape, 0 if lanes_first else 1)
    cell = lax.broadcasted_iota(jnp.int32, shape, 1 if lanes_first else 0)
    return jnp.where(lane == cell // COARSEN, 1.0, 0.0)


def side_matrix():
    lane = lax.broadcasted_iota(jnp.int32, (2 * LANES, LANES), 1)
    cell = lax.broadcasted_iota(jnp.int32, (2 * LANES, LANES), 0)
    end = jnp.logical_and(cell % COARSEN == COARSEN - 1, lane < 32)
    block = cell // COARSEN
    return jnp.where(
        end, jnp.where(lane == block, 1.0, jnp.where(lane == block + 1, -1.0, 0.0)), 0.0
    )


def stripe_rows(rows, block):
    spot = lax.broadcasted_iota(jnp.int32, (rows, LANES), 0)
    out = []
    for comp in range(4):
        total = jnp.zeros((rows, LANES), jnp.float32)
        for row in range(rows):
            total = jnp.where(spot == row, block(row, slice(comp, comp + 1)), total)
        out.append(total)
    scale = 1.0 / float(COARSEN * COARSEN)
    return [out[comp] * scale for comp in range(3)], out[3]


def widen(corrections, slots, row, picked):
    lines = []
    for correction in corrections:
        picked[0:16, :] = jnp.zeros((16, LANES), jnp.float32)
        for comp in range(3):
            for shift in range(3):
                spot = comp * 3 + shift
                picked[spot : spot + 1, :] = pick_row(correction[comp], row + shift - 1)
        lines.append(picked[0:16, :])
    for number, (stripe, y) in enumerate(slots):
        for x in range(2):
            group = x * 2 + y
            spot = (2 * number + x) * 16
            picked[spot : spot + 16, :] = (
                lines[stripe] if group == 0 else pltpu.roll(lines[stripe], LANES - 32 * group, 1)
            )
    return jnp.dot(
        picked[...], block_matrix(True), precision=HIGH, preferred_element_type=jnp.float32
    )


class Place:
    def __init__(self):
        self.row, self.rows = lax.axis_index("row"), lax.axis_size("row")
        self.col, self.cols = lax.axis_index("col"), lax.axis_size("col")
        self.low, self.high = self.row > 0, self.row < self.rows - 1
        self.back, self.front = self.col > 0, self.col < self.cols - 1
        self.even = self.col % 2 == 0

    def sides(self, turn_a, turn_b):
        return jnp.where(self.even, turn_b, turn_a), jnp.where(self.even, turn_a, turn_b)


def put_corner(put, message, place, row, distance, count):
    for side, there in ((0, place.low), (1, place.high)):
        back, front = place.sides(message[0](row[side], count), message[1](row[side], count))
        plane = HALO - distance if side == 0 else HALO + BLOCK - 1 + distance
        put(plane, HALO - count, count, jnp.logical_and(there, place.back), back)
        put(plane, HALO + BLOCK, count, jnp.logical_and(there, place.front), front)


def put_field(field, core, low, high, y_a, y_b, deep, place, corners):
    for comp in range(3):
        for half in range(2):
            z = slice(half * LANES, half * LANES + LANES)
            own = slice(CORE, CORE + BLOCK)
            field[comp, half, 4:20, own, :] = core[comp, :, :, z]
            pages = slice(comp * 4, comp * 4 + 4)
            field[comp, half, 0:4, own, :] = jnp.where(place.low, low[pages, :, z], 0.0)
            field[comp, half, 20:24, own, :] = jnp.where(place.high, high[pages, :, z], 0.0)
            pages = slice(comp * 16, comp * 16 + 16)
            back, front = place.sides(y_a[pages, :, z], y_b[pages, :, z])
            field[comp, half, 4:20, TOP : TOP + HALO, :] = jnp.where(place.back, back, 0.0)
            field[comp, half, 4:20, CORE + BLOCK : CORE + BLOCK + HALO, :] = jnp.where(
                place.front, front, 0.0
            )

            def put(plane, row, count, there, value):
                field[comp, half, plane, TOP + row : TOP + row + count, :] = jnp.where(
                    there, value, 0.0
                )

            for number, x in enumerate(DEEP):
                rows = slice(number, number + 1)
                back, front = place.sides(y_a[deep + comp, rows, z], y_b[deep + comp, rows, z])
                put(HALO + x, -1, 1, place.back, back)
                put(HALO + x, EXT, 1, place.front, front)
            corners(put, comp, z)


def first_corners(c_a, c_b, place):
    def corners(put, comp, z):
        message = [lambda row, count, ref=ref: ref[row : row + count, z] for ref in (c_a, c_b)]
        for distance, first, count in CORNER_FIELD:
            row = comp * 2 * FIELD_ROWS + first
            put_corner(put, message, place, (row, row + FIELD_ROWS), distance, count)

    return corners


ROW_CORNERS = ((1, 1), (2, 1), (3, 1), (2, 2))
X_EDGE = 3 * HALO + 2
Y_EDGE = 3 * BLOCK + 6


def later_corners(low, high, y_a, y_b, place):
    def corners(put, comp, z):
        both = jnp.logical_and
        for ref, there, sign in ((low, place.low, -1), (high, place.high, 1)):
            for number, (along_x, along_y) in enumerate(ROW_CORNERS):
                plane = HALO - along_x if sign < 0 else HALO + BLOCK - 1 + along_x
                for end, side in enumerate((place.back, place.front)):
                    spot = comp * 8 + end * 4 + number
                    row = HALO - along_y if end == 0 else HALO + BLOCK - 1 + along_y
                    value = ref[12 + spot // 16, spot % 16 : spot % 16 + 1, z]
                    put(plane, row, 1, both(there, side), value)
        page = 3 * BLOCK + comp
        for number in range(4):
            along_y = 2 + number % 2
            plane, there = ((HALO - 1, place.low), (HALO + BLOCK, place.high))[number // 2]
            rows = slice(number, number + 1)
            back, front = place.sides(y_a[page, rows, z], y_b[page, rows, z])
            put(plane, HALO - along_y, 1, both(there, place.back), back)
            put(plane, HALO + BLOCK - 1 + along_y, 1, both(there, place.front), front)

    return corners


def look_up(label, floor_table, rise_table):
    floor_cell = jnp.zeros(label.shape, jnp.float32)
    rise_cell = jnp.zeros(label.shape, jnp.float32)
    for number in range(floor_table.shape[0]):
        chosen = label == float(number)
        floor_cell = jnp.where(chosen, floor_table[number], floor_cell)
        rise_cell = jnp.where(chosen, rise_table[number], rise_cell)
    return floor_cell, rise_cell


def prepare_kernel(
    source, coil_mask, labels, floor_table, rise_table, drive_sums, drive, floor, rise
):
    own = slice(HALO, HALO + BLOCK)
    for half in range(2):
        z = slice(half * LANES, half * LANES + LANES)
        for x in range(BLOCK):
            coil = 2.0 * coil_mask[x, :, z].astype(jnp.float32)
            for comp in range(3):
                drive[comp, half, HALO + x, own, :] = source[comp, x, :, z] * coil
            floor[half, HALO + x, own, :], rise[half, HALO + x, own, :] = look_up(
                labels[x, :, z].astype(jnp.float32), floor_table, rise_table
            )
    sum_drive(drive, drive_sums)


def prepare(source, coil_mask, labels, tables):
    return pl.pallas_call(
        prepare_kernel,
        in_specs=[VMEM] * 3 + [SMEM] * 2,
        out_specs=[VMEM] * 4,
        out_shape=[
            f32(32, 2 * LANES), f32(3, 2, EXT, EXT, LANES), f32(2, EXT, EXT, LANES),
            f32(2, EXT, EXT, LANES),
        ],
        compiler_params=PARAMS,
        name="prepare",
    )(source, coil_mask, labels, *tables)


def put_material(drive, floor, rise, low, high, y_a, y_b, c_a, c_b, floor_table, rise_table, place):
    for half in range(2):
        z = slice(half * LANES, half * LANES + LANES)
        own = slice(HALO, HALO + BLOCK)
        message = [lambda row, count, ref=ref: ref[row : row + count, z] for ref in (c_a, c_b)]
        for comp in range(3):
            pages = slice(12 + comp * 2, 14 + comp * 2)
            drive[comp, half, 2:4, own, :] = low[pages, :, z]
            drive[comp, half, 20:22, own, :] = high[pages, :, z]
            for x in range(BLOCK):
                page, part = 48 + comp * 8 + x // 2, slice((x % 2) * 2, (x % 2) * 2 + 2)
                back, front = place.sides(y_a[page, part, z], y_b[page, part, z])
                drive[comp, half, 4 + x, 2:4, :] = back
                drive[comp, half, 4 + x, 20:22, :] = front

            def put_drive(plane, row, count, there, value):
                drive[comp, half, plane, row : row + count, :] = value

            row = CORNER_DRIVE + comp * 2
            put_corner(put_drive, message, place, (row, row + 1), 1, 1)
            for number, x in enumerate(DEEP):
                rows = slice(2 + number, 3 + number)
                back, front = place.sides(y_a[88 + comp, rows, z], y_b[88 + comp, rows, z])
                put_drive(HALO + x, 1, 1, None, back)
                put_drive(HALO + x, HALO + BLOCK + 2, 1, None, front)
        floor[half, 1:4, own, :] = jnp.where(place.low, low[18:21, :, z], -1.0)
        floor[half, 20:23, own, :] = jnp.where(place.high, high[18:21, :, z], -1.0)

        def put_label(plane, row, count, there, value):
            floor[half, plane, row : row + count, :] = jnp.where(there, value, -1.0)

        for distance, first, count in CORNER_LABEL:
            row = CORNER_TABLE + first
            put_corner(put_label, message, place, (row, row + LABEL_ROWS), distance, count)
        for x in (1, 2, 3, 20, 21, 22):
            floor[half, x], rise[half, x] = look_up(floor[half, x], floor_table, rise_table)
        for x in range(BLOCK):
            back, front = place.sides(y_a[72 + x, :, z], y_b[72 + x, :, z])
            label = jnp.concatenate(
                [jnp.where(place.back, back, -1.0), jnp.where(place.front, front, -1.0)], axis=0
            )
            for ref, value in zip((floor, rise), look_up(label, floor_table, rise_table)):
                ref[half, HALO + x, 0:HALO, :] = value[:HALO]
                ref[half, HALO + x, HALO + BLOCK :, :] = value[HALO:]


def right_of(low, high, last):
    a, b = pltpu.roll(low, LANES - 1, 1), pltpu.roll(high, LANES - 1, 1)
    return jnp.where(last, b, a), b


def left_of(low, high, first):
    a, b = pltpu.roll(low, 1, 1), pltpu.roll(high, 1, 1)
    return a, jnp.where(first, a, b)


def each(begin, end, plane):
    for x in range(begin, end):
        for ref, value in plane(x):
            ref[...] = value


def fine_iteration(
    field, other, reluct, c_x, c_y, c_up, c_down, weight, sums, drive_sums, drive, floor, rise,
):
    mid = slice(TOP, TOP + EXT)
    plus = slice(TOP + 1, TOP + EXT + 1)
    minus = slice(TOP - 1, TOP + EXT - 1)
    lane = lax.broadcasted_iota(jnp.int32, (EXT, LANES), 1)
    first, last = lane == 0, lane == LANES - 1

    def reluct_plane(x):
        stores = []
        along_z = []
        for comp in range(2):
            low, high = field[comp, 0, x, mid], field[comp, 1, x, mid]
            r0, r1 = right_of(low, high, last)
            l0, l1 = left_of(low, high, first)
            along_z.append((r0 - jnp.where(first, 0.0, l0), jnp.where(last, 0.0, r1) - l1))
        for half in range(2):
            def along_y(comp):
                return field[comp, half, x, plus] - field[comp, half, x, minus]

            def along_x(comp):
                return field[comp, half, x + 1, mid] - field[comp, half, x - 1, mid]

            b0 = along_y(2) - along_z[1][half]
            b1 = along_z[0][half] - along_x(2)
            b2 = along_x(1) - along_y(0)
            square = 0.25 * (b0 * b0 + b1 * b1 + b2 * b2)
            stores.append((
                reluct.at[half, x, mid], floor[half, x] + rise[half, x] * (square / (1.0 + square))
            ))
        return stores

    each(1, EXT - 1, reluct_plane)

    def apply(src, x, rows, coeffs, first_lane, last_lane):
        rows_plus = slice(rows.start + 1, rows.stop + 1)
        rows_minus = slice(rows.start - 1, rows.stop - 1)
        out = []
        for comp in range(3):
            low, high = src[comp, 0, x, rows], src[comp, 1, x, rows]
            rights = right_of(low, high, last_lane)
            lefts = left_of(low, high, first_lane)
            for half in range(2):
                x_plus, x_minus, y_plus, y_minus, up, down = coeffs[half]
                total = (
                    (x_plus * src[comp, half, x + 1, rows] + x_minus * src[comp, half, x - 1, rows])
                    + (y_plus * src[comp, half, x, rows_plus] + y_minus * src[comp, half, x, rows_minus])
                    + (up * rights[half] + down * lefts[half])
                )
                out.append((comp, half, (low, high)[half], total))
        return out

    def load_coeffs(x, rows):
        rows_minus = slice(rows.start - 1, rows.stop - 1)
        return [
            (
                c_x[half, x, rows], c_x[half, x - 1, rows], c_y[half, x, rows],
                c_y[half, x, rows_minus], c_up[half, x, rows], c_down[half, x, rows],
            )
            for half in range(2)
        ]

    def first_plane(x):
        low, high = reluct[0, x, mid], reluct[1, x, mid]
        r0, r1 = right_of(low, high, last)
        l0, l1 = left_of(low, high, first)
        ups = (low + r0, high + jnp.where(last, 0.0, r1))
        downs = (low + jnp.where(first, 0.0, l0), high + l1)
        stores, coeffs, weights = [], [], []
        for half in range(2):
            here = (low, high)[half]
            x_plus = here + reluct[half, x + 1, mid]
            x_minus = here + reluct[half, x - 1, mid]
            y_plus = here + reluct[half, x, plus]
            y_minus = here + reluct[half, x, minus]
            total = ((x_plus + x_minus) + (y_plus + y_minus)) + (ups[half] + downs[half])
            up = ups[half] if half == 0 else jnp.where(last, 0.0, ups[half])
            down = jnp.where(first, 0.0, downs[half]) if half == 0 else downs[half]
            scale = jnp.where(floor[half, x] > 0.0, RELAX / total, 0.0)
            coeffs.append((x_plus, x_minus, y_plus, y_minus, up, down))
            weights.append(scale)
            for ref, value in (
                (c_x, x_plus), (c_y, y_plus), (c_up, up), (c_down, down), (weight, scale),
            ):
                stores.append((ref.at[half, x, mid], value))
        for comp, half, here, total in apply(field, x, mid, coeffs, first, last):
            stores.append((
                other.at[comp, half, x, mid],
                (1.0 - RELAX) * here + weights[half] * (drive[comp, half, x] + total),
            ))
        return stores

    each(2, EXT - 2, first_plane)

    def second_plane(x):
        stores = []
        weights = [weight[half, x, mid] for half in range(2)]
        for comp, half, here, total in apply(other, x, mid, load_coeffs(x, mid), first, last):
            stores.append((
                field.at[comp, half, x, mid],
                (1.0 - RELAX) * here + weights[half] * (drive[comp, half, x] + total),
            ))
        return stores

    each(3, EXT - 3, second_plane)

    own = slice(CORE, CORE + BLOCK)
    ends = pl.ds(CORE - 1, 3, stride=COARSEN)
    beyond = pl.ds(CORE, 3, stride=COARSEN)
    lane = lax.broadcasted_iota(jnp.int32, (BLOCK, LANES), 1)
    last_own = lane == LANES - 1
    lane = lax.broadcasted_iota(jnp.int32, (1, LANES), 1)
    rims = (lane == 0, lane == LANES - 1)
    zero = jnp.zeros((BLOCK, LANES), jnp.float32)
    thin = jnp.zeros((3, LANES), jnp.float32)

    def blocks(values):
        return [
            jnp.sum(values[part * COARSEN : (part + 1) * COARSEN], axis=0, keepdims=True)
            for part in range(2)
        ]

    def side(plane, comp, half):
        return blocks(
            c_x[half, plane, own]
            * (field[comp, half, plane + 1, own] - field[comp, half, plane, own])
        )

    sums[...] = jnp.zeros(sums.shape, jnp.float32)
    sides = [
        [[side(HALO - 1 + COARSEN * k, comp, half) for half in range(2)] for comp in range(3)]
        for k in range(3)
    ]
    for coarse in range(2):
        def plane(x, totals):
            across, rim, along, material = totals
            relucts = [reluct[half, x, own] for half in range(2)]
            ups = [c_up[half, x, own] for half in range(2)]
            ys = [c_y[half, x, ends, :] for half in range(2)]
            across_new, rim_new, along_new = [], [], []
            for comp in range(3):
                here = [field[comp, half, x, own] for half in range(2)]
                rights = right_of(here[0], here[1], last_own)
                for half in range(2):
                    number = comp * 2 + half
                    across_new.append(across[number] + ups[half] * (rights[half] - here[half]))
                    rim_new.append(rim[number] + relucts[half] * here[half])
                    along_new.append(
                        along[number]
                        + ys[half] * (field[comp, half, x, beyond, :] - field[comp, half, x, ends, :])
                    )
            return (
                tuple(across_new), tuple(rim_new), tuple(along_new),
                tuple(material[half] + relucts[half] for half in range(2)),
            )

        totals = ((zero,) * 6, (zero,) * 6, (thin,) * 6, (zero,) * 2)
        for step in range(COARSEN):
            totals = plane(HALO + coarse * COARSEN + step, totals)
        across, rim, along, material = totals
        for half in range(2):
            z = slice(half * LANES, (half + 1) * LANES)
            means = blocks(material[half])
            for comp in range(3):
                number = comp * 2 + half
                rims_sum, across_sum = blocks(rim[number]), blocks(across[number])
                for part in range(2):
                    row = (coarse * 2 + part) * 8
                    y_side = along[number][part + 1 : part + 2] - along[number][part : part + 1]
                    x_side = sides[coarse + 1][comp][half][part] - sides[coarse][comp][half][part]
                    spot = row + comp
                    sums[0, spot : spot + 1, z] = 0.5 * (
                        (drive_sums[spot : spot + 1, z] + (x_side + y_side))
                        - jnp.where(rims[half], rims_sum[part], 0.0)
                    )
                    sums[1, spot : spot + 1, z] = 0.5 * across_sum[part]
            for part in range(2):
                spot = (coarse * 2 + part) * 8 + 3
                sums[0, spot : spot + 1, z] = means[part] * (1.0 / float(COARSEN ** 3))
    totals = jnp.dot(
        sums[0], block_matrix(False), precision=HIGH, preferred_element_type=jnp.float32
    ) + jnp.dot(sums[1], side_matrix(), precision=HIGH, preferred_element_type=jnp.float32)
    result = totals[0:8]
    for group in range(1, 4):
        result = result + pltpu.roll(totals[group * 8 : group * 8 + 8], 32 * group, 1)
    return result[0:4]


def sum_drive(drive, drive_sums):
    own = slice(HALO, HALO + BLOCK)
    drive_sums[...] = jnp.zeros(drive_sums.shape, jnp.float32)
    for comp in range(3):
        for half in range(2):
            for coarse in range(2):
                total = drive[comp, half, HALO + coarse * COARSEN, own]
                for x in range(HALO + coarse * COARSEN + 1, HALO + (coarse + 1) * COARSEN):
                    total = total + drive[comp, half, x, own]
                for part in range(2):
                    spot = (coarse * 2 + part) * 8 + comp
                    drive_sums[spot : spot + 1, half * LANES : (half + 1) * LANES] = jnp.sum(
                        total[part * COARSEN : (part + 1) * COARSEN], axis=0, keepdims=True
                    )


SCRATCH = (
    [pltpu.VMEM((3, 2, EXT, ROWS, LANES), jnp.float32)] * 2
    + [pltpu.VMEM((2, EXT, ROWS, LANES), jnp.float32)] * 6
    + [pltpu.VMEM((2, 32, 2 * LANES), jnp.float32)]
)


def emit(field, coarse, field_out, edges, coarse_out, place):
    own = slice(CORE, CORE + BLOCK)
    for comp in range(3):
        for half in range(2):
            z = slice(half * LANES, half * LANES + LANES)
            field_out[comp, :, :, z] = field[comp, half, 4:20, own, :]
            if edges:
                x_lo, x_hi, y_a, y_b = edges
                x_lo[comp * 4 : comp * 4 + 4, :, z] = field[comp, half, 4:8, own, :]
                x_hi[comp * 4 : comp * 4 + 4, :, z] = field[comp, half, 16:20, own, :]
                first, second = turns(
                    place.even, field[comp, half, 4:20, CORE : CORE + 4, :],
                    field[comp, half, 4:20, CORE + BLOCK - 4 : CORE + BLOCK, :],
                )
                y_a[comp * 16 : comp * 16 + 16, :, z] = first
                y_b[comp * 16 : comp * 16 + 16, :, z] = second

                def cell(x, y):
                    return field[comp, half, HALO + x, CORE + y : CORE + y + 1, :]

                def send(page, row, x, low_y, high_y):
                    first, second = turns(place.even, cell(x, low_y), cell(x, high_y))
                    y_a[page, row : row + 1, z] = first
                    y_b[page, row : row + 1, z] = second

                for number, (along_x, along_y) in enumerate(ROW_CORNERS):
                    for end, y in enumerate((-along_y, BLOCK - 1 + along_y)):
                        spot = comp * 8 + end * 4 + number
                        rows = slice(spot % 16, spot % 16 + 1)
                        x_lo[12 + spot // 16, rows, z] = cell(along_x - 1, y)
                        x_hi[12 + spot // 16, rows, z] = cell(BLOCK - along_x, y)
                for number in range(4):
                    along_y = 2 + number % 2
                    send(
                        3 * BLOCK + comp, number, (-1, BLOCK)[number // 2], along_y - 1,
                        BLOCK - along_y,
                    )
                for number, x in enumerate(DEEP):
                    send(3 * BLOCK + 3 + comp, number, x, HALO, BLOCK - 1 - HALO)
    coarse_out[...] = jnp.broadcast_to(coarse[None], coarse_out.shape)


def edge_shapes(depth):
    return [f32(X_EDGE, BLOCK, depth)] * 2 + [f32(Y_EDGE, HALO, depth)] * 2


def first_kernel(
    potential, low, high, y_a, y_b, c_a, c_b, floor_table, rise_table, drive_sums, drive_in, floor_in,
    rise_in, field_out, coarse_out, x_lo, x_hi, yo_a, yo_b, drive, floor, rise, *scratch,
):
    place = Place()
    field = scratch[0]
    put_field(
        field, potential, low, high, y_a, y_b, 88, place, first_corners(c_a, c_b, place)
    )
    put_material(drive, floor, rise, low, high, y_a, y_b, c_a, c_b, floor_table, rise_table, place)
    coarse = fine_iteration(*scratch, drive_sums, drive, floor, rise)
    emit(field, coarse, field_out, (x_lo, x_hi, yo_a, yo_b), coarse_out, place)


def first_iteration(potential, messages, tables, material, devices):
    depth = potential.shape[-1]
    return pl.pallas_call(
        first_kernel,
        in_specs=[VMEM] * 7 + [SMEM] * 2 + [VMEM] * 4,
        out_specs=[VMEM] * 9,
        out_shape=[f32(*potential.shape), f32(devices, 4, LANES)]
        + edge_shapes(depth)
        + [f32(*part.shape) for part in material[1:]],
        scratch_shapes=SCRATCH,
        input_output_aliases={10: 6, 11: 7, 12: 8},
        compiler_params=PARAMS,
        name="first_iteration",
    )(potential, *messages, *tables, *material)


SLOTS = ((0, 1), (1, 0), (1, 1), (2, 0))


def solve_kernel(gathered, wide_out, picked):
    place = Place()
    targets, relucts = [], []
    for stripe in range(3):
        index = jnp.clip(place.col + stripe - 1, 0, place.cols - 1)
        target, reluct = stripe_rows(
            gathered.shape[0], lambda row, part, index=index: gathered[row, index, part, :]
        )
        targets.append(target)
        relucts.append(reluct)
    wide_out[...] = widen(coarse_solve(targets, relucts), SLOTS, place.row, picked)


def solve(gathered):
    return pl.pallas_call(
        solve_kernel,
        in_specs=[VMEM],
        out_specs=VMEM,
        out_shape=f32(128, 2 * LANES),
        scratch_shapes=[pltpu.VMEM((128, LANES), jnp.float32)],
        compiler_params=PARAMS,
        name="solve",
    )(gathered)


def next_kernel(
    final, wide, core, low, high, y_a, y_b, drive_sums, drive, floor, rise, *refs
):
    if final:
        field_out, coarse_out, reluct_out, *scratch = refs
        edges = None
    else:
        field_out, coarse_out, x_lo, x_hi, yo_a, yo_b, *scratch = refs
        edges = (x_lo, x_hi, yo_a, yo_b)
    place = Place()
    field = scratch[0]
    put_field(
        field, core, low, high, y_a, y_b, 3 * BLOCK + 3, place,
        later_corners(low, high, y_a, y_b, place),
    )
    mid = slice(TOP, TOP + EXT)
    cell = lax.broadcasted_iota(jnp.int32, (EXT, LANES), 0)
    for slab, (begin, end, shift, x) in enumerate(SLABS):
        for comp in range(3):
            for half in range(2):
                z = slice(half * LANES, (half + 1) * LANES)
                lines = [
                    wide[spot : spot + 1, z]
                    for spot in ((2 * slot + x) * 16 + comp * 3 + shift for slot in range(4))
                ]
                back = jnp.where(place.back, lines[0], 0.0)
                front = jnp.where(place.front, lines[3], 0.0)
                tile = jnp.where(
                    cell < 12,
                    jnp.where(cell < 4, back, lines[1]),
                    jnp.where(cell < 20, lines[2], front),
                )
                for plane in range(begin, end):
                    field[comp, half, plane, mid] = field[comp, half, plane, mid] + tile
                for plane in (HALO + x for x in DEEP):
                    if begin <= plane < end:
                        for row, line in ((TOP - 1, back), (TOP + EXT, front)):
                            field[comp, half, plane, row : row + 1, :] = (
                                field[comp, half, plane, row : row + 1, :] + line
                            )
    coarse = fine_iteration(*scratch, drive_sums, drive, floor, rise)
    emit(field, coarse, field_out, edges, coarse_out, place)
    if final:
        reluct = scratch[2]
        for half in range(2):
            reluct_out[:, :, half * LANES : (half + 1) * LANES] = reluct[
                half, 4:20, CORE : CORE + BLOCK, :
            ]


def next_iteration(final, wide, core, messages, material, devices):
    outs = [f32(*core.shape), f32(devices, 4, LANES)]
    outs += [f32(*core.shape[1:])] if final else edge_shapes(core.shape[-1])
    return pl.pallas_call(
        functools.partial(next_kernel, final),
        in_specs=[VMEM] * 10,
        out_specs=[VMEM] * len(outs),
        out_shape=outs,
        scratch_shapes=SCRATCH,
        compiler_params=PARAMS,
        name="last_iteration" if final else "next_iteration",
    )(wide, core, *messages, *material)


def correct_kernel(gathered, core, field_out, target_out, picked):
    row = lax.axis_index("row")
    rows = gathered.shape[0]
    target, reluct = stripe_rows(rows, lambda row, part: gathered[row, part, :])
    wide = widen(coarse_solve([target], [reluct]), ((0, 0), (0, 1)), row, picked)
    cell = lax.broadcasted_iota(jnp.int32, (BLOCK, 2 * LANES), 0)
    for x in range(2):
        for comp in range(3):
            spot = x * 16 + comp * 3 + 1
            tile = jnp.where(
                cell < COARSEN, wide[spot : spot + 1], wide[spot + 32 : spot + 33]
            )
            for plane in range(x * COARSEN, (x + 1) * COARSEN):
                field_out[comp, plane] = core[comp, plane] + tile
    for comp in range(3):
        for x in range(2):
            for y in range(2):
                group = x * 2 + y
                moved = target[comp] if group == 0 else pltpu.roll(target[comp], LANES - 32 * group, 1)
                for r in range(rows):
                    target_out[comp, 2 * r + x, y : y + 1, :] = moved[r : r + 1, 0:32]


def correct(gathered, core):
    rows = gathered.shape[0]
    return pl.pallas_call(
        correct_kernel,
        in_specs=[VMEM] * 2,
        out_specs=[VMEM] * 2,
        out_shape=[f32(*core.shape), f32(3, 2 * rows, 2, 32)],
        scratch_shapes=[pltpu.VMEM((64, LANES), jnp.float32)],
        compiler_params=PARAMS,
        name="correct",
    )(gathered, core)


def rings(to_low, to_high):
    count = lax.axis_size("row")
    forward = [(i, (i + 1) % count) for i in range(count)]
    backward = [(target, source) for source, target in forward]
    return lax.ppermute(to_high, "row", forward), lax.ppermute(to_low, "row", backward)


def swaps(turn_a, turn_b):
    count = lax.axis_size("col")
    pairs = []
    for begin in (0, 1):
        partner = list(range(count))
        for i in range(begin, count - 1, 2):
            partner[i], partner[i + 1] = i + 1, i
        pairs.append(list(enumerate(partner)))
    return lax.ppermute(turn_a, "col", pairs[0]), lax.ppermute(turn_b, "col", pairs[1])


def shards(potential, source, labels, coil_mask, floor_table, rise_table):
    rows, cols = lax.axis_size("row"), lax.axis_size("col")
    arrays = (potential, source, coil_mask, labels)
    x_lo, x_hi = pack_x(arrays)
    low, high = rings(x_lo, x_hi)
    y_a, y_b, *arrays = lax.optimization_barrier((*pack_y(arrays), *arrays))
    y_a, y_b = swaps(y_a, y_b)
    tables = (floor_table, rise_table)
    potential, *rest = arrays
    drive_sums, *material = prepare(*rest, tables)
    low, high, drive_sums = lax.optimization_barrier((low, high, drive_sums))
    c_a, c_b = swaps(*pack_corner(low, high))
    field, coarse, x_lo, x_hi, y_a, y_b, *material = first_iteration(
        potential, (low, high, y_a, y_b, c_a, c_b), tables, (drive_sums, *material), rows * cols,
    )
    material = (drive_sums, *material)
    for iteration in range(1, ITERS):
        final = iteration == ITERS - 1
        low, high = rings(x_lo, x_hi)
        y_a, y_b = swaps(y_a, y_b)
        gathered = lax.all_to_all(coarse, ("row", "col"), 0, 0)
        wide = solve(gathered.reshape(rows, cols, 4, LANES))
        outs = next_iteration(
            final, wide, field, (low, high, y_a, y_b), material, rows if final else rows * cols
        )
        if final:
            field, coarse, reluct = outs
        else:
            field, coarse, x_lo, x_hi, y_a, y_b = outs
    gathered = lax.all_to_all(coarse, "row", 0, 0)
    field, coarse_target = correct(gathered, field)
    return (field, reluct, coarse_target)


def solution(mesh):
    in_specs = (
        P(None, "row", "col", None),
        P(None, "row", "col", None),
        P("row", "col", None),
        P("row", "col", None),
        P(),
        P(),
    )
    out_specs = (P(None, "row", "col", None), P("row", "col", None), P(None, None, "col", None))
    return jax.shard_map(shards, mesh=mesh, in_specs=in_specs, out_specs=out_specs, check_vma=False)
```

```python
import functools
import jax
import jax.numpy as jnp
from jax import lax
from jax.experimental import pallas as pl
from jax.experimental.pallas import tpu as pltpu
from jax.sharding import PartitionSpec as P

ITERS = 3
SWEEPS = 2
COARSE_SWEEPS = 16
COARSEN = 8
RELAX = 0.8

HALO = 4
BLOCK = 16
EXT = BLOCK + 2 * HALO
LANES = 128
TOP = 8
CORE = TOP + HALO
ROWS = 40
X_PAGES = 21
Y_PAGES = 91
DEEP = (1, BLOCK - 2)

VMEM = pl.BlockSpec(memory_space=pltpu.VMEM)
SMEM = pl.BlockSpec(memory_space=pltpu.SMEM)
PARAMS = pltpu.CompilerParams(vmem_limit_bytes=44 * 1024 * 1024)


def f32(*shape):
    return jax.ShapeDtypeStruct(shape, jnp.float32)


def turns(even, low_edge, high_edge):
    return jnp.where(even, high_edge, low_edge), jnp.where(even, low_edge, high_edge)


def corner_parts(reach):
    first = 0
    parts = []
    for distance in range(1, reach):
        parts.append((distance, first, reach - distance))
        first += reach - distance
    return parts, first


CORNER_FIELD, FIELD_ROWS = corner_parts(4)
CORNER_LABEL, LABEL_ROWS = corner_parts(3)
CORNER_DRIVE = 6 * FIELD_ROWS
CORNER_TABLE = CORNER_DRIVE + 6
CORNER_ALL = CORNER_TABLE + 2 * LABEL_ROWS
SLABS = ((0, 4, 0, 1), (4, 12, 1, 0), (12, 20, 1, 1), (20, 24, 2, 0))


def fetch_all(sems, pairs):
    copies = [
        pltpu.make_async_copy(ref, scratch, sems.at[number])
        for number, (ref, scratch) in enumerate(pairs)
    ]
    for copy in copies:
        copy.start()
    for copy in copies:
        copy.wait()


def pack_x_kernel(potential, source, coil_mask, labels, x_lo, x_hi, pot, src, mask, lab, sems):
    pairs = []
    for side, (cells, pair) in enumerate((
        (slice(0, 4), slice(0, 2)), (slice(BLOCK - 4, BLOCK), slice(BLOCK - 2, BLOCK)),
    )):
        pairs += [
            (potential.at[:, cells], pot.at[side]), (source.at[:, pair], src.at[side]),
            (coil_mask.at[pair], mask.at[side]), (labels.at[cells], lab.at[side]),
        ]
    fetch_all(sems, pairs)
    for side, out in enumerate((x_lo, x_hi)):
        for comp in range(3):
            out[comp * 4 : comp * 4 + 4] = pot[side, comp]
            out[12 + comp * 2 : 14 + comp * 2] = 2.0 * src[side, comp] * mask[side].astype(jnp.float32)
        out[18:21] = lab[side, side : side + 3].astype(jnp.float32)


def pack_y_kernel(potential, source, coil_mask, labels, y_a, y_b, pot, src, mask, lab, sems):
    even = lax.axis_index("col") % 2 == 0
    pairs = []
    for side, rows in enumerate((slice(0, 8), slice(BLOCK - 8, BLOCK))):
        pairs += [
            (potential.at[:, :, rows], pot.at[side]), (source.at[:, :, rows], src.at[side]),
            (coil_mask.at[:, rows], mask.at[side]), (labels.at[:, rows], lab.at[side]),
        ]
    fetch_all(sems, pairs)

    def send(page, low_edge, high_edge, rows=slice(0, 4)):
        first, second = turns(even, low_edge, high_edge)
        y_a[page, rows] = first
        y_b[page, rows] = second

    for x in range(BLOCK):
        mask_lo = 2.0 * mask[0, x, 0:2].astype(jnp.float32)
        mask_hi = 2.0 * mask[1, x, 6:8].astype(jnp.float32)
        for comp in range(3):
            send(comp * 16 + x, pot[0, comp, x, 0:4], pot[1, comp, x, 4:8])
            send(
                48 + comp * 8 + x // 2, src[0, comp, x, 0:2] * mask_lo,
                src[1, comp, x, 6:8] * mask_hi, slice((x % 2) * 2, (x % 2) * 2 + 2),
            )
        send(72 + x, lab[0, x, 0:4].astype(jnp.float32), lab[1, x, 4:8].astype(jnp.float32))
    for number, x in enumerate(DEEP):
        mask_lo = 2.0 * mask[0, x, 2:3].astype(jnp.float32)
        mask_hi = 2.0 * mask[1, x, 5:6].astype(jnp.float32)
        for comp in range(3):
            send(88 + comp, pot[0, comp, x, 4:5], pot[1, comp, x, 3:4], slice(number, number + 1))
            send(
                88 + comp, src[0, comp, x, 2:3] * mask_lo, src[1, comp, x, 5:6] * mask_hi,
                slice(2 + number, 3 + number),
            )


def pack_edges(kernel, name, shapes, out, arrays):
    types = (jnp.float32, jnp.float32, jnp.int32, jnp.int32)
    return pl.pallas_call(
        kernel,
        in_specs=[pl.BlockSpec(memory_space=pltpu.HBM)] * 4,
        out_specs=[VMEM] * 2,
        out_shape=[out] * 2,
        scratch_shapes=[pltpu.VMEM((2,) + shape, kind) for shape, kind in zip(shapes, types)]
        + [pltpu.SemaphoreType.DMA((8,))],
        compiler_params=PARAMS,
        name=name,
    )(*(pltpu.with_memory_space_constraint(v, pltpu.HBM) for v in arrays))


def pack_x(arrays):
    depth = arrays[0].shape[-1]
    shapes = ((3, 4, BLOCK, depth), (3, 2, BLOCK, depth), (2, BLOCK, depth), (4, BLOCK, depth))
    return pack_edges(pack_x_kernel, "pack_x", shapes, f32(X_PAGES, BLOCK, depth), arrays)


def pack_y(arrays):
    depth = arrays[0].shape[-1]
    shapes = ((3, BLOCK, 8, depth),) * 2 + ((BLOCK, 8, depth),) * 2
    return pack_edges(pack_y_kernel, "pack_y", shapes, f32(Y_PAGES, HALO, depth), arrays)


def pack_corner_kernel(low, high, out_a, out_b):
    even = lax.axis_index("col") % 2 == 0

    def send(row, count, ref, page):
        rows = slice(row, row + count)
        first, second = turns(even, ref[page, 0:count], ref[page, BLOCK - count : BLOCK])
        out_a[rows, :] = first
        out_b[rows, :] = second

    for comp in range(3):
        for distance, first, count in CORNER_FIELD:
            row = comp * 2 * FIELD_ROWS + first
            send(row, count, low, comp * 4 + 4 - distance)
            send(row + FIELD_ROWS, count, high, comp * 4 + distance - 1)
    for comp in range(3):
        send(CORNER_DRIVE + comp * 2, 1, low, 12 + comp * 2 + 1)
        send(CORNER_DRIVE + comp * 2 + 1, 1, high, 12 + comp * 2)
    for distance, first, count in CORNER_LABEL:
        row = CORNER_TABLE + first
        send(row, count, low, 18 + 3 - distance)
        send(row + LABEL_ROWS, count, high, 18 + distance - 1)


def pack_corner(low, high):
    depth = low.shape[-1]
    return pl.pallas_call(
        pack_corner_kernel,
        in_specs=[VMEM] * 2,
        out_specs=[VMEM] * 2,
        out_shape=[f32(CORNER_ALL, depth)] * 2,
        compiler_params=PARAMS,
        name="pack_corner",
    )(low, high)


def coarse_solve(targets, relucts):
    shape = relucts[0].shape
    count = shape[0]
    lane = lax.broadcasted_iota(jnp.int32, shape, 1)
    row = lax.broadcasted_iota(jnp.int32, shape, 0)
    z = lane % 32
    first_y = (lane // 32) % 2 == 0
    first_x = lane // 64 == 0
    up_ok, down_ok = z < 31, z > 0
    far_ok = jnp.logical_not(
        jnp.logical_or(
            jnp.logical_and(first_x, row == 0),
            jnp.logical_and(jnp.logical_not(first_x), row == count - 1),
        )
    )

    def up(v):
        return pltpu.roll(v, LANES - 1, 1)

    def down(v):
        return pltpu.roll(v, 1, 1)

    def side(v):
        return jnp.where(first_y, pltpu.roll(v, LANES - 32, 1), pltpu.roll(v, 32, 1))

    def near(v):
        return pltpu.roll(v, 64, 1)

    def far(swapped, turned=False):
        below, above = pltpu.roll(swapped, 1, 0), pltpu.roll(swapped, count - 1, 0)
        return jnp.where(first_x, above, below) if turned else jnp.where(first_x, below, above)

    sets = []
    for r in relucts:
        swapped = near(r)
        c_up = r + jnp.where(up_ok, up(r), 0.0)
        c_down = r + jnp.where(down_ok, down(r), 0.0)
        c_side = r + side(r)
        c_near = r + swapped
        c_far = r + jnp.where(far_ok, far(swapped), 0.0)
        diag = ((c_up + c_down) + (c_side + r)) + (c_near + c_far)
        c_up = jnp.where(up_ok, c_up, 0.0)
        c_down = jnp.where(down_ok, c_down, 0.0)
        c_far = jnp.where(far_ok, c_far, 0.0)
        sets.append((c_up, c_down, c_side, c_near, c_far, diag, RELAX / diag))

    def neighbours(coeffs, v, swapped, turned=False):
        c_up, c_down, c_side, c_near, c_far = coeffs[:5]
        return (
            (c_up * up(v) + c_down * down(v)) + (c_side * side(v) + c_near * swapped)
        ) + c_far * far(swapped, turned)

    turned_sets = [[near(c) for c in coeffs] for coeffs in sets]
    doubled = [[2.0 * t for t in stripe] for stripe in targets]
    swapped_t = [[near(t) for t in stripe] for stripe in doubled]
    plain = [[coeffs[6] * t for t in stripe] for coeffs, stripe in zip(sets, doubled)]
    swapped = [[coeffs[6] * t for t in stripe] for coeffs, stripe in zip(turned_sets, swapped_t)]
    for step in range(COARSE_SWEEPS - 1):
        plain, swapped = [
            [
                (1.0 - RELAX) * v + coeffs[6] * (t + neighbours(coeffs, v, s))
                for v, s, t in zip(*stripe)
            ]
            for coeffs, stripe in zip(sets, zip(plain, swapped, doubled))
        ], [
            [
                (1.0 - RELAX) * s + coeffs[6] * (t + neighbours(coeffs, s, v, True))
                for v, s, t in zip(*stripe)
            ]
            for coeffs, stripe in zip(turned_sets, zip(plain, swapped, swapped_t))
        ]
    out = []
    for coeffs, *stripe in zip(sets, plain, swapped, doubled):
        total = jnp.sum(jnp.sum(coeffs[5], axis=1, keepdims=True), axis=0, keepdims=True)
        done = []
        for v, s, t in zip(*stripe):
            left = t - (coeffs[5] * v - neighbours(coeffs, v, s))
            left = jnp.sum(jnp.sum(left, axis=1, keepdims=True), axis=0, keepdims=True)
            done.append(v + left / total)
        out.append(done)
    return out


def exact_dot(values, matrix):
    high = values.astype(jnp.bfloat16)
    rest = values - high.astype(jnp.float32)
    middle = rest.astype(jnp.bfloat16)
    low = (rest - middle.astype(jnp.float32)).astype(jnp.bfloat16)
    count = values.shape[0]
    parts = jnp.dot(
        jnp.concatenate([high, middle, low], axis=0), matrix.astype(jnp.bfloat16),
        preferred_element_type=jnp.float32,
    )
    return (parts[2 * count :] + parts[count : 2 * count]) + parts[:count]


def pick_row(values, index):
    row = lax.broadcasted_iota(jnp.int32, values.shape, 0)
    return jnp.sum(jnp.where(row == index, values, 0.0), axis=0, keepdims=True)


def block_matrix(lanes_first):
    shape = (LANES, 2 * LANES) if lanes_first else (2 * LANES, LANES)
    lane = lax.broadcasted_iota(jnp.int32, shape, 0 if lanes_first else 1)
    cell = lax.broadcasted_iota(jnp.int32, shape, 1 if lanes_first else 0)
    return jnp.where(lane == cell // COARSEN, 1.0, 0.0)


def side_matrix():
    lane = lax.broadcasted_iota(jnp.int32, (2 * LANES, LANES), 1)
    cell = lax.broadcasted_iota(jnp.int32, (2 * LANES, LANES), 0)
    end = jnp.logical_and(cell % COARSEN == COARSEN - 1, lane < 32)
    block = cell // COARSEN
    return jnp.where(
        end, jnp.where(lane == block, 1.0, jnp.where(lane == block + 1, -1.0, 0.0)), 0.0
    )


def stripe_rows(rows, block):
    spot = lax.broadcasted_iota(jnp.int32, (rows, LANES), 0)
    out = []
    for comp in range(4):
        total = jnp.zeros((rows, LANES), jnp.float32)
        for row in range(rows):
            total = jnp.where(spot == row, block(row, slice(comp, comp + 1)), total)
        out.append(total)
    scale = 1.0 / float(COARSEN * COARSEN)
    return [out[comp] * scale for comp in range(3)], out[3]


def widen(corrections, slots, row, picked):
    lines = []
    for correction in corrections:
        picked[0:16, :] = jnp.zeros((16, LANES), jnp.float32)
        for comp in range(3):
            for shift in range(3):
                spot = comp * 3 + shift
                picked[spot : spot + 1, :] = pick_row(correction[comp], row + shift - 1)
        lines.append(picked[0:16, :])
    for number, (stripe, y) in enumerate(slots):
        for x in range(2):
            group = x * 2 + y
            spot = (2 * number + x) * 16
            picked[spot : spot + 16, :] = (
                lines[stripe] if group == 0 else pltpu.roll(lines[stripe], LANES - 32 * group, 1)
            )
    return exact_dot(picked[...], block_matrix(True))


class Place:
    def __init__(self):
        self.row, self.rows = lax.axis_index("row"), lax.axis_size("row")
        self.col, self.cols = lax.axis_index("col"), lax.axis_size("col")
        self.low, self.high = self.row > 0, self.row < self.rows - 1
        self.back, self.front = self.col > 0, self.col < self.cols - 1
        self.even = self.col % 2 == 0

    def sides(self, turn_a, turn_b):
        return jnp.where(self.even, turn_b, turn_a), jnp.where(self.even, turn_a, turn_b)


def put_corner(put, message, place, row, distance, count):
    for side, there in ((0, place.low), (1, place.high)):
        back, front = place.sides(message[0](row[side], count), message[1](row[side], count))
        plane = HALO - distance if side == 0 else HALO + BLOCK - 1 + distance
        put(plane, HALO - count, count, jnp.logical_and(there, place.back), back)
        put(plane, HALO + BLOCK, count, jnp.logical_and(there, place.front), front)


def put_field(field, core, low, high, y_a, y_b, deep, place, corners):
    for comp in range(3):
        for half in range(2):
            z = slice(half * LANES, half * LANES + LANES)
            own = slice(CORE, CORE + BLOCK)
            field[comp, half, 4:20, own, :] = core[comp, :, :, z]
            pages = slice(comp * 4, comp * 4 + 4)
            field[comp, half, 0:4, own, :] = jnp.where(place.low, low[pages, :, z], 0.0)
            field[comp, half, 20:24, own, :] = jnp.where(place.high, high[pages, :, z], 0.0)
            pages = slice(comp * 16, comp * 16 + 16)
            back, front = place.sides(y_a[pages, :, z], y_b[pages, :, z])
            field[comp, half, 4:20, TOP : TOP + HALO, :] = jnp.where(place.back, back, 0.0)
            field[comp, half, 4:20, CORE + BLOCK : CORE + BLOCK + HALO, :] = jnp.where(
                place.front, front, 0.0
            )

            def put(plane, row, count, there, value):
                field[comp, half, plane, TOP + row : TOP + row + count, :] = jnp.where(
                    there, value, 0.0
                )

            for number, x in enumerate(DEEP):
                rows = slice(number, number + 1)
                back, front = place.sides(y_a[deep + comp, rows, z], y_b[deep + comp, rows, z])
                put(HALO + x, -1, 1, place.back, back)
                put(HALO + x, EXT, 1, place.front, front)
            corners(put, comp, z)


def first_corners(c_a, c_b, place):
    def corners(put, comp, z):
        message = [lambda row, count, ref=ref: ref[row : row + count, z] for ref in (c_a, c_b)]
        for distance, first, count in CORNER_FIELD:
            row = comp * 2 * FIELD_ROWS + first
            put_corner(put, message, place, (row, row + FIELD_ROWS), distance, count)

    return corners


ROW_CORNERS = ((1, 1), (2, 1), (3, 1), (2, 2))
X_EDGE = 3 * HALO + 2
Y_EDGE = 3 * BLOCK + 6


def later_corners(low, high, y_a, y_b, place):
    def corners(put, comp, z):
        both = jnp.logical_and
        for ref, there, sign in ((low, place.low, -1), (high, place.high, 1)):
            for number, (along_x, along_y) in enumerate(ROW_CORNERS):
                plane = HALO - along_x if sign < 0 else HALO + BLOCK - 1 + along_x
                for end, side in enumerate((place.back, place.front)):
                    spot = comp * 8 + end * 4 + number
                    row = HALO - along_y if end == 0 else HALO + BLOCK - 1 + along_y
                    value = ref[12 + spot // 16, spot % 16 : spot % 16 + 1, z]
                    put(plane, row, 1, both(there, side), value)
        page = 3 * BLOCK + comp
        for number in range(4):
            along_y = 2 + number % 2
            plane, there = ((HALO - 1, place.low), (HALO + BLOCK, place.high))[number // 2]
            rows = slice(number, number + 1)
            back, front = place.sides(y_a[page, rows, z], y_b[page, rows, z])
            put(plane, HALO - along_y, 1, both(there, place.back), back)
            put(plane, HALO + BLOCK - 1 + along_y, 1, both(there, place.front), front)

    return corners


def look_up(label, floor_table, rise_table):
    floor_cell = jnp.zeros(label.shape, jnp.float32)
    rise_cell = jnp.zeros(label.shape, jnp.float32)
    for number in range(floor_table.shape[0]):
        chosen = label == float(number)
        floor_cell = jnp.where(chosen, floor_table[number], floor_cell)
        rise_cell = jnp.where(chosen, rise_table[number], rise_cell)
    return floor_cell, rise_cell


def prepare_kernel(
    source, coil_mask, labels, floor_table, rise_table, drive_sums, drive, floor, rise
):
    own = slice(HALO, HALO + BLOCK)
    for half in range(2):
        z = slice(half * LANES, half * LANES + LANES)
        for x in range(BLOCK):
            coil = 2.0 * coil_mask[x, :, z].astype(jnp.float32)
            for comp in range(3):
                drive[comp, half, HALO + x, own, :] = source[comp, x, :, z] * coil
            floor[half, HALO + x, own, :], rise[half, HALO + x, own, :] = look_up(
                labels[x, :, z].astype(jnp.float32), floor_table, rise_table
            )
    sum_drive(drive, drive_sums)


def prepare(source, coil_mask, labels, tables):
    return pl.pallas_call(
        prepare_kernel,
        in_specs=[VMEM] * 3 + [SMEM] * 2,
        out_specs=[VMEM] * 4,
        out_shape=[
            f32(32, 2 * LANES), f32(3, 2, EXT, EXT, LANES), f32(2, EXT, EXT, LANES),
            f32(2, EXT, EXT, LANES),
        ],
        compiler_params=PARAMS,
        name="prepare",
    )(source, coil_mask, labels, *tables)


def put_material(drive, floor, rise, low, high, y_a, y_b, c_a, c_b, floor_table, rise_table, place):
    for half in range(2):
        z = slice(half * LANES, half * LANES + LANES)
        own = slice(HALO, HALO + BLOCK)
        message = [lambda row, count, ref=ref: ref[row : row + count, z] for ref in (c_a, c_b)]
        for comp in range(3):
            pages = slice(12 + comp * 2, 14 + comp * 2)
            drive[comp, half, 2:4, own, :] = low[pages, :, z]
            drive[comp, half, 20:22, own, :] = high[pages, :, z]
            for x in range(BLOCK):
                page, part = 48 + comp * 8 + x // 2, slice((x % 2) * 2, (x % 2) * 2 + 2)
                back, front = place.sides(y_a[page, part, z], y_b[page, part, z])
                drive[comp, half, 4 + x, 2:4, :] = back
                drive[comp, half, 4 + x, 20:22, :] = front

            def put_drive(plane, row, count, there, value):
                drive[comp, half, plane, row : row + count, :] = value

            row = CORNER_DRIVE + comp * 2
            put_corner(put_drive, message, place, (row, row + 1), 1, 1)
            for number, x in enumerate(DEEP):
                rows = slice(2 + number, 3 + number)
                back, front = place.sides(y_a[88 + comp, rows, z], y_b[88 + comp, rows, z])
                put_drive(HALO + x, 1, 1, None, back)
                put_drive(HALO + x, HALO + BLOCK + 2, 1, None, front)
        floor[half, 1:4, own, :] = jnp.where(place.low, low[18:21, :, z], -1.0)
        floor[half, 20:23, own, :] = jnp.where(place.high, high[18:21, :, z], -1.0)

        def put_label(plane, row, count, there, value):
            floor[half, plane, row : row + count, :] = jnp.where(there, value, -1.0)

        for distance, first, count in CORNER_LABEL:
            row = CORNER_TABLE + first
            put_corner(put_label, message, place, (row, row + LABEL_ROWS), distance, count)
        for x in (1, 2, 3, 20, 21, 22):
            floor[half, x], rise[half, x] = look_up(floor[half, x], floor_table, rise_table)
        for x in range(BLOCK):
            back, front = place.sides(y_a[72 + x, :, z], y_b[72 + x, :, z])
            label = jnp.concatenate(
                [jnp.where(place.back, back, -1.0), jnp.where(place.front, front, -1.0)], axis=0
            )
            for ref, value in zip((floor, rise), look_up(label, floor_table, rise_table)):
                ref[half, HALO + x, 0:HALO, :] = value[:HALO]
                ref[half, HALO + x, HALO + BLOCK :, :] = value[HALO:]


def right_of(low, high, last):
    a, b = pltpu.roll(low, LANES - 1, 1), pltpu.roll(high, LANES - 1, 1)
    return jnp.where(last, b, a), b


def left_of(low, high, first):
    a, b = pltpu.roll(low, 1, 1), pltpu.roll(high, 1, 1)
    return a, jnp.where(first, a, b)


def each(begin, end, plane):
    for x in range(begin, end):
        for ref, value in plane(x):
            ref[...] = value


def fine_iteration(
    field, other, reluct, c_x, c_y, c_up, c_down, weight, sums, drive_sums, drive, floor, rise,
):
    mid = slice(TOP, TOP + EXT)
    plus = slice(TOP + 1, TOP + EXT + 1)
    minus = slice(TOP - 1, TOP + EXT - 1)
    lane = lax.broadcasted_iota(jnp.int32, (EXT, LANES), 1)
    first, last = lane == 0, lane == LANES - 1

    def reluct_plane(x):
        stores = []
        along_z = []
        for comp in range(2):
            low, high = field[comp, 0, x, mid], field[comp, 1, x, mid]
            r0, r1 = right_of(low, high, last)
            l0, l1 = left_of(low, high, first)
            along_z.append((r0 - jnp.where(first, 0.0, l0), jnp.where(last, 0.0, r1) - l1))
        for half in range(2):
            def along_y(comp):
                return field[comp, half, x, plus] - field[comp, half, x, minus]

            def along_x(comp):
                return field[comp, half, x + 1, mid] - field[comp, half, x - 1, mid]

            b0 = along_y(2) - along_z[1][half]
            b1 = along_z[0][half] - along_x(2)
            b2 = along_x(1) - along_y(0)
            square = 0.25 * (b0 * b0 + b1 * b1 + b2 * b2)
            stores.append((
                reluct.at[half, x, mid], floor[half, x] + rise[half, x] * (square / (1.0 + square))
            ))
        return stores

    each(1, EXT - 1, reluct_plane)

    def apply(src, x, rows, coeffs, first_lane, last_lane):
        rows_plus = slice(rows.start + 1, rows.stop + 1)
        rows_minus = slice(rows.start - 1, rows.stop - 1)
        out = []
        for comp in range(3):
            low, high = src[comp, 0, x, rows], src[comp, 1, x, rows]
            rights = right_of(low, high, last_lane)
            lefts = left_of(low, high, first_lane)
            for half in range(2):
                x_plus, x_minus, y_plus, y_minus, up, down = coeffs[half]
                total = (
                    (x_plus * src[comp, half, x + 1, rows] + x_minus * src[comp, half, x - 1, rows])
                    + (y_plus * src[comp, half, x, rows_plus] + y_minus * src[comp, half, x, rows_minus])
                    + (up * rights[half] + down * lefts[half])
                )
                out.append((comp, half, (low, high)[half], total))
        return out

    def load_coeffs(x, rows):
        rows_minus = slice(rows.start - 1, rows.stop - 1)
        return [
            (
                c_x[half, x, rows], c_x[half, x - 1, rows], c_y[half, x, rows],
                c_y[half, x, rows_minus], c_up[half, x, rows], c_down[half, x, rows],
            )
            for half in range(2)
        ]

    def first_plane(x):
        low, high = reluct[0, x, mid], reluct[1, x, mid]
        r0, r1 = right_of(low, high, last)
        l0, l1 = left_of(low, high, first)
        ups = (low + r0, high + jnp.where(last, 0.0, r1))
        downs = (low + jnp.where(first, 0.0, l0), high + l1)
        stores, coeffs, weights = [], [], []
        for half in range(2):
            here = (low, high)[half]
            x_plus = here + reluct[half, x + 1, mid]
            x_minus = here + reluct[half, x - 1, mid]
            y_plus = here + reluct[half, x, plus]
            y_minus = here + reluct[half, x, minus]
            total = ((x_plus + x_minus) + (y_plus + y_minus)) + (ups[half] + downs[half])
            up = ups[half] if half == 0 else jnp.where(last, 0.0, ups[half])
            down = jnp.where(first, 0.0, downs[half]) if half == 0 else downs[half]
            scale = jnp.where(floor[half, x] > 0.0, RELAX / total, 0.0)
            coeffs.append((x_plus, x_minus, y_plus, y_minus, up, down))
            weights.append(scale)
            for ref, value in (
                (c_x, x_plus), (c_y, y_plus), (c_up, up), (c_down, down), (weight, scale),
            ):
                stores.append((ref.at[half, x, mid], value))
        for comp, half, here, total in apply(field, x, mid, coeffs, first, last):
            stores.append((
                other.at[comp, half, x, mid],
                (1.0 - RELAX) * here + weights[half] * (drive[comp, half, x] + total),
            ))
        return stores

    each(2, EXT - 2, first_plane)

    def second_plane(x):
        stores = []
        weights = [weight[half, x, mid] for half in range(2)]
        for comp, half, here, total in apply(other, x, mid, load_coeffs(x, mid), first, last):
            stores.append((
                field.at[comp, half, x, mid],
                (1.0 - RELAX) * here + weights[half] * (drive[comp, half, x] + total),
            ))
        return stores

    each(3, EXT - 3, second_plane)

    own = slice(CORE, CORE + BLOCK)
    ends = pl.ds(CORE - 1, 3, stride=COARSEN)
    beyond = pl.ds(CORE, 3, stride=COARSEN)
    lane = lax.broadcasted_iota(jnp.int32, (BLOCK, LANES), 1)
    last_own = lane == LANES - 1
    lane = lax.broadcasted_iota(jnp.int32, (1, LANES), 1)
    rims = (lane == 0, lane == LANES - 1)
    zero = jnp.zeros((BLOCK, LANES), jnp.float32)
    thin = jnp.zeros((3, LANES), jnp.float32)

    def blocks(values):
        return [
            jnp.sum(values[part * COARSEN : (part + 1) * COARSEN], axis=0, keepdims=True)
            for part in range(2)
        ]

    def side(plane, comp, half):
        return blocks(
            c_x[half, plane, own]
            * (field[comp, half, plane + 1, own] - field[comp, half, plane, own])
        )

    sums[...] = jnp.zeros(sums.shape, jnp.float32)
    sides = [
        [[side(HALO - 1 + COARSEN * k, comp, half) for half in range(2)] for comp in range(3)]
        for k in range(3)
    ]
    for coarse in range(2):
        def plane(x, totals):
            across, rim, along, material = totals
            relucts = [reluct[half, x, own] for half in range(2)]
            ups = [c_up[half, x, own] for half in range(2)]
            ys = [c_y[half, x, ends, :] for half in range(2)]
            across_new, rim_new, along_new = [], [], []
            for comp in range(3):
                here = [field[comp, half, x, own] for half in range(2)]
                rights = right_of(here[0], here[1], last_own)
                for half in range(2):
                    number = comp * 2 + half
                    across_new.append(across[number] + ups[half] * (rights[half] - here[half]))
                    rim_new.append(rim[number] + relucts[half] * here[half])
                    along_new.append(
                        along[number]
                        + ys[half] * (field[comp, half, x, beyond, :] - field[comp, half, x, ends, :])
                    )
            return (
                tuple(across_new), tuple(rim_new), tuple(along_new),
                tuple(material[half] + relucts[half] for half in range(2)),
            )

        totals = ((zero,) * 6, (zero,) * 6, (thin,) * 6, (zero,) * 2)
        for step in range(COARSEN):
            totals = plane(HALO + coarse * COARSEN + step, totals)
        across, rim, along, material = totals
        for half in range(2):
            z = slice(half * LANES, (half + 1) * LANES)
            means = blocks(material[half])
            for comp in range(3):
                number = comp * 2 + half
                rims_sum, across_sum = blocks(rim[number]), blocks(across[number])
                for part in range(2):
                    row = (coarse * 2 + part) * 8
                    y_side = along[number][part + 1 : part + 2] - along[number][part : part + 1]
                    x_side = sides[coarse + 1][comp][half][part] - sides[coarse][comp][half][part]
                    spot = row + comp
                    sums[0, spot : spot + 1, z] = 0.5 * (
                        (drive_sums[spot : spot + 1, z] + (x_side + y_side))
                        - jnp.where(rims[half], rims_sum[part], 0.0)
                    )
                    sums[1, spot : spot + 1, z] = 0.5 * across_sum[part]
            for part in range(2):
                spot = (coarse * 2 + part) * 8 + 3
                sums[0, spot : spot + 1, z] = means[part] * (1.0 / float(COARSEN ** 3))
    totals = exact_dot(sums[0], block_matrix(False)) + exact_dot(sums[1], side_matrix())
    result = totals[0:8]
    for group in range(1, 4):
        result = result + pltpu.roll(totals[group * 8 : group * 8 + 8], 32 * group, 1)
    return result[0:4]


def sum_drive(drive, drive_sums):
    own = slice(HALO, HALO + BLOCK)
    drive_sums[...] = jnp.zeros(drive_sums.shape, jnp.float32)
    for comp in range(3):
        for half in range(2):
            for coarse in range(2):
                total = drive[comp, half, HALO + coarse * COARSEN, own]
                for x in range(HALO + coarse * COARSEN + 1, HALO + (coarse + 1) * COARSEN):
                    total = total + drive[comp, half, x, own]
                for part in range(2):
                    spot = (coarse * 2 + part) * 8 + comp
                    drive_sums[spot : spot + 1, half * LANES : (half + 1) * LANES] = jnp.sum(
                        total[part * COARSEN : (part + 1) * COARSEN], axis=0, keepdims=True
                    )


SCRATCH = (
    [pltpu.VMEM((3, 2, EXT, ROWS, LANES), jnp.float32)] * 2
    + [pltpu.VMEM((2, EXT, ROWS, LANES), jnp.float32)] * 6
    + [pltpu.VMEM((2, 32, 2 * LANES), jnp.float32)]
)


def emit(field, coarse, field_out, edges, coarse_out, place):
    own = slice(CORE, CORE + BLOCK)
    for comp in range(3):
        for half in range(2):
            z = slice(half * LANES, half * LANES + LANES)
            field_out[comp, :, :, z] = field[comp, half, 4:20, own, :]
            if edges:
                x_lo, x_hi, y_a, y_b = edges
                x_lo[comp * 4 : comp * 4 + 4, :, z] = field[comp, half, 4:8, own, :]
                x_hi[comp * 4 : comp * 4 + 4, :, z] = field[comp, half, 16:20, own, :]
                first, second = turns(
                    place.even, field[comp, half, 4:20, CORE : CORE + 4, :],
                    field[comp, half, 4:20, CORE + BLOCK - 4 : CORE + BLOCK, :],
                )
                y_a[comp * 16 : comp * 16 + 16, :, z] = first
                y_b[comp * 16 : comp * 16 + 16, :, z] = second

                def cell(x, y):
                    return field[comp, half, HALO + x, CORE + y : CORE + y + 1, :]

                def send(page, row, x, low_y, high_y):
                    first, second = turns(place.even, cell(x, low_y), cell(x, high_y))
                    y_a[page, row : row + 1, z] = first
                    y_b[page, row : row + 1, z] = second

                for number, (along_x, along_y) in enumerate(ROW_CORNERS):
                    for end, y in enumerate((-along_y, BLOCK - 1 + along_y)):
                        spot = comp * 8 + end * 4 + number
                        rows = slice(spot % 16, spot % 16 + 1)
                        x_lo[12 + spot // 16, rows, z] = cell(along_x - 1, y)
                        x_hi[12 + spot // 16, rows, z] = cell(BLOCK - along_x, y)
                for number in range(4):
                    along_y = 2 + number % 2
                    send(
                        3 * BLOCK + comp, number, (-1, BLOCK)[number // 2], along_y - 1,
                        BLOCK - along_y,
                    )
                for number, x in enumerate(DEEP):
                    send(3 * BLOCK + 3 + comp, number, x, HALO, BLOCK - 1 - HALO)
    coarse_out[...] = jnp.broadcast_to(coarse[None], coarse_out.shape)


def edge_shapes(depth):
    return [f32(X_EDGE, BLOCK, depth)] * 2 + [f32(Y_EDGE, HALO, depth)] * 2


def first_kernel(
    potential, low, high, y_a, y_b, c_a, c_b, floor_table, rise_table, drive_sums, drive_in, floor_in,
    rise_in, field_out, coarse_out, x_lo, x_hi, yo_a, yo_b, drive, floor, rise, *scratch,
):
    place = Place()
    field = scratch[0]
    put_field(
        field, potential, low, high, y_a, y_b, 88, place, first_corners(c_a, c_b, place)
    )
    put_material(drive, floor, rise, low, high, y_a, y_b, c_a, c_b, floor_table, rise_table, place)
    coarse = fine_iteration(*scratch, drive_sums, drive, floor, rise)
    emit(field, coarse, field_out, (x_lo, x_hi, yo_a, yo_b), coarse_out, place)


def first_iteration(potential, messages, tables, material, devices):
    depth = potential.shape[-1]
    return pl.pallas_call(
        first_kernel,
        in_specs=[VMEM] * 7 + [SMEM] * 2 + [VMEM] * 4,
        out_specs=[VMEM] * 9,
        out_shape=[f32(*potential.shape), f32(devices, 4, LANES)]
        + edge_shapes(depth)
        + [f32(*part.shape) for part in material[1:]],
        scratch_shapes=SCRATCH,
        input_output_aliases={10: 6, 11: 7, 12: 8},
        compiler_params=PARAMS,
        name="first_iteration",
    )(potential, *messages, *tables, *material)


SLOTS = ((0, 1), (1, 0), (1, 1), (2, 0))


def solve_kernel(gathered, wide_out, picked):
    place = Place()
    targets, relucts = [], []
    for stripe in range(3):
        index = jnp.clip(place.col + stripe - 1, 0, place.cols - 1)
        target, reluct = stripe_rows(
            gathered.shape[0], lambda row, part, index=index: gathered[row, index, part, :]
        )
        targets.append(target)
        relucts.append(reluct)
    wide_out[...] = widen(coarse_solve(targets, relucts), SLOTS, place.row, picked)


def solve(gathered):
    return pl.pallas_call(
        solve_kernel,
        in_specs=[VMEM],
        out_specs=VMEM,
        out_shape=f32(128, 2 * LANES),
        scratch_shapes=[pltpu.VMEM((128, LANES), jnp.float32)],
        compiler_params=PARAMS,
        name="solve",
    )(gathered)


def next_kernel(
    final, wide, core, low, high, y_a, y_b, drive_sums, drive, floor, rise, *refs
):
    if final:
        field_out, coarse_out, reluct_out, *scratch = refs
        edges = None
    else:
        field_out, coarse_out, x_lo, x_hi, yo_a, yo_b, *scratch = refs
        edges = (x_lo, x_hi, yo_a, yo_b)
    place = Place()
    field = scratch[0]
    put_field(
        field, core, low, high, y_a, y_b, 3 * BLOCK + 3, place,
        later_corners(low, high, y_a, y_b, place),
    )
    mid = slice(TOP, TOP + EXT)
    cell = lax.broadcasted_iota(jnp.int32, (EXT, LANES), 0)
    for slab, (begin, end, shift, x) in enumerate(SLABS):
        for comp in range(3):
            for half in range(2):
                z = slice(half * LANES, (half + 1) * LANES)
                lines = [
                    wide[spot : spot + 1, z]
                    for spot in ((2 * slot + x) * 16 + comp * 3 + shift for slot in range(4))
                ]
                back = jnp.where(place.back, lines[0], 0.0)
                front = jnp.where(place.front, lines[3], 0.0)
                tile = jnp.where(
                    cell < 12,
                    jnp.where(cell < 4, back, lines[1]),
                    jnp.where(cell < 20, lines[2], front),
                )
                for plane in range(begin, end):
                    field[comp, half, plane, mid] = field[comp, half, plane, mid] + tile
                for plane in (HALO + x for x in DEEP):
                    if begin <= plane < end:
                        for row, line in ((TOP - 1, back), (TOP + EXT, front)):
                            field[comp, half, plane, row : row + 1, :] = (
                                field[comp, half, plane, row : row + 1, :] + line
                            )
    coarse = fine_iteration(*scratch, drive_sums, drive, floor, rise)
    emit(field, coarse, field_out, edges, coarse_out, place)
    if final:
        reluct = scratch[2]
        for half in range(2):
            reluct_out[:, :, half * LANES : (half + 1) * LANES] = reluct[
                half, 4:20, CORE : CORE + BLOCK, :
            ]


def next_iteration(final, wide, core, messages, material, devices):
    outs = [f32(*core.shape), f32(devices, 4, LANES)]
    outs += [f32(*core.shape[1:])] if final else edge_shapes(core.shape[-1])
    return pl.pallas_call(
        functools.partial(next_kernel, final),
        in_specs=[VMEM] * 10,
        out_specs=[VMEM] * len(outs),
        out_shape=outs,
        scratch_shapes=SCRATCH,
        compiler_params=PARAMS,
        name="last_iteration" if final else "next_iteration",
    )(wide, core, *messages, *material)


def correct_kernel(gathered, core, field_out, target_out, picked):
    row = lax.axis_index("row")
    rows = gathered.shape[0]
    target, reluct = stripe_rows(rows, lambda row, part: gathered[row, part, :])
    wide = widen(coarse_solve([target], [reluct]), ((0, 0), (0, 1)), row, picked)
    cell = lax.broadcasted_iota(jnp.int32, (BLOCK, 2 * LANES), 0)
    for x in range(2):
        for comp in range(3):
            spot = x * 16 + comp * 3 + 1
            tile = jnp.where(
                cell < COARSEN, wide[spot : spot + 1], wide[spot + 32 : spot + 33]
            )
            for plane in range(x * COARSEN, (x + 1) * COARSEN):
                field_out[comp, plane] = core[comp, plane] + tile
    for comp in range(3):
        for x in range(2):
            for y in range(2):
                group = x * 2 + y
                moved = target[comp] if group == 0 else pltpu.roll(target[comp], LANES - 32 * group, 1)
                for r in range(rows):
                    target_out[comp, 2 * r + x, y : y + 1, :] = moved[r : r + 1, 0:32]


def correct(gathered, core):
    rows = gathered.shape[0]
    return pl.pallas_call(
        correct_kernel,
        in_specs=[VMEM] * 2,
        out_specs=[VMEM] * 2,
        out_shape=[f32(*core.shape), f32(3, 2 * rows, 2, 32)],
        scratch_shapes=[pltpu.VMEM((64, LANES), jnp.float32)],
        compiler_params=PARAMS,
        name="correct",
    )(gathered, core)


def rings(to_low, to_high):
    count = lax.axis_size("row")
    forward = [(i, (i + 1) % count) for i in range(count)]
    backward = [(target, source) for source, target in forward]
    return lax.ppermute(to_high, "row", forward), lax.ppermute(to_low, "row", backward)


def swaps(turn_a, turn_b):
    count = lax.axis_size("col")
    pairs = []
    for begin in (0, 1):
        partner = list(range(count))
        for i in range(begin, count - 1, 2):
            partner[i], partner[i + 1] = i + 1, i
        pairs.append(list(enumerate(partner)))
    return lax.ppermute(turn_a, "col", pairs[0]), lax.ppermute(turn_b, "col", pairs[1])


def shards(potential, source, labels, coil_mask, floor_table, rise_table):
    rows, cols = lax.axis_size("row"), lax.axis_size("col")
    arrays = (potential, source, coil_mask, labels)
    x_lo, x_hi = pack_x(arrays)
    low, high = rings(x_lo, x_hi)
    y_a, y_b, *arrays = lax.optimization_barrier((*pack_y(arrays), *arrays))
    y_a, y_b = swaps(y_a, y_b)
    tables = (floor_table, rise_table)
    potential, *rest = arrays
    drive_sums, *material = prepare(*rest, tables)
    low, high, drive_sums = lax.optimization_barrier((low, high, drive_sums))
    c_a, c_b = swaps(*pack_corner(low, high))
    field, coarse, x_lo, x_hi, y_a, y_b, *material = first_iteration(
        potential, (low, high, y_a, y_b, c_a, c_b), tables, (drive_sums, *material), rows * cols,
    )
    material = (drive_sums, *material)
    for iteration in range(1, ITERS):
        final = iteration == ITERS - 1
        low, high = rings(x_lo, x_hi)
        y_a, y_b = swaps(y_a, y_b)
        gathered = lax.all_to_all(coarse, ("row", "col"), 0, 0)
        wide = solve(gathered.reshape(rows, cols, 4, LANES))
        outs = next_iteration(
            final, wide, field, (low, high, y_a, y_b), material, rows if final else rows * cols
        )
        if final:
            field, coarse, reluct = outs
        else:
            field, coarse, x_lo, x_hi, y_a, y_b = outs
    gathered = lax.all_to_all(coarse, "row", 0, 0)
    field, coarse_target = correct(gathered, field)
    return (field, reluct, coarse_target)


def solution(mesh):
    in_specs = (
        P(None, "row", "col", None),
        P(None, "row", "col", None),
        P("row", "col", None),
        P("row", "col", None),
        P(),
        P(),
    )
    out_specs = (P(None, "row", "col", None), P("row", "col", None), P(None, None, "col", None))
    return jax.shard_map(shards, mesh=mesh, in_specs=in_specs, out_specs=out_specs, check_vma=False)
```
